32 devices in a mesh: dp: 2 (over y), fsdp: 16 (over z, x, core).
Axes of the slice: x: 2, y: 2, z: 4, core: 2. Of those that a mesh axis runs over, the one named last changes fastest.
Arguments:
- tokens: bfloat16 [32768, 768], P(('dp', 'fsdp')), may hold values from -6 to 6
- segment_ids: int32 [32, 1024], P(('dp', 'fsdp')), may hold values from 0 to 7, never falling along the last dimension, each value on 1 to 512 neighbouring positions
- padding: int32 [32, 1024], P(('dp', 'fsdp')), may hold values 0 or 1
- qkv_weight: bfloat16 [768, 2304], P(None, 'fsdp'), may hold values from -0.21875 to 0.21875
- query_bias: bfloat16 [768], P('fsdp'), may hold values from -1.25 to 1.25
- value_bias: bfloat16 [768], P('fsdp'), may hold values from -1.25 to 1.25
- out_weight: bfloat16 [768, 768], P('fsdp'), may hold values from -0.875 to 0.875
- out_bias: bfloat16 [768], P('fsdp'), may hold values from -1.25 to 1.25
- first_gain: bfloat16 [768], P('fsdp'), may hold values from 0.5 to 1.5
- first_shift: bfloat16 [768], P('fsdp'), may hold values from -1.25 to 1.25
- second_gain: bfloat16 [768], P('fsdp'), may hold values from 0.5 to 1.5
- second_shift: bfloat16 [768], P('fsdp'), may hold values from -1.25 to 1.25
- up_weight: bfloat16 [768, 3072], P(None, 'fsdp'), may hold values from -0.21875 to 0.21875
- up_bias: bfloat16 [3072], P('fsdp'), may hold values from -1.25 to 1.25
- down_weight: bfloat16 [3072, 768], P('fsdp'), may hold values from -0.109375 to 0.109375
- down_bias: bfloat16 [768], P('fsdp'), may hold values from -1.25 to 1.25
- align_weight: bfloat16 [768, 1024], P(None, 'fsdp'), may hold values from -0.21875 to 0.21875
- align_bias: bfloat16 [1024], P('fsdp'), may hold values from -1.25 to 1.25
- grad_output: bfloat16 [32768, 768], P(('dp', 'fsdp')), may hold values from -12 to 12
- grad_aligned: bfloat16 [32768, 1024], P(('dp', 'fsdp')), may hold values from -6 to 6
Outputs:
- block_out: bfloat16 [32768, 768], P(('dp', 'fsdp'))
- aligned: bfloat16 [32768, 1024], P(('dp', 'fsdp'))
- grad_tokens: bfloat16 [32768, 768], P(('dp', 'fsdp'))
- grad_qkv_weight: float32 [768, 2304], P(None, 'fsdp')
- grad_query_bias: float32 [768], P('fsdp')
- grad_value_bias: float32 [768], P('fsdp')
- grad_out_weight: float32 [768, 768], P('fsdp')
- grad_out_bias: float32 [768], P('fsdp')
- grad_first_gain: float32 [768], P('fsdp')
- grad_first_shift: float32 [768], P('fsdp')
- grad_second_gain: float32 [768], P('fsdp')
- grad_second_shift: float32 [768], P('fsdp')
- grad_up_weight: float32 [768, 3072], P(None, 'fsdp')
- grad_up_bias: float32 [3072], P('fsdp')
- grad_down_weight: float32 [3072, 768], P('fsdp')
- grad_down_bias: float32 [768], P('fsdp')
- grad_align_weight: float32 [768, 1024], P(None, 'fsdp')
- grad_align_bias: float32 [1024], P('fsdp')
The draws below stay inside these ranges and needn't reach their ends.
Inputs may be any that keep to these rules, and one draw needn't show every extreme that they name: `segment_ids`: segment numbers never fall along a packed sequence; each clip holds at most 512 tokens.
All inputs are finite; a program needn't handle non-finite values. No bound on the sum of `padding` on one device may be relied on, other than what follows from the above.
Results may differ from the reference program's by a relative error of at most 0.014.
Values may be sent and summed in bfloat16 or wider, within the bound.
A program may use at most 256 MiB of HBM per device.

```python
import math
import jax
import jax.numpy as jnp
import numpy as np
from jax import lax

D = 768
HEADS = 12
FF = 3072
AL = 1024
LEN = 1024
SEQS = 32
TOKENS = 32768


def plant(drawn, own_key, least, largest):
    shape = drawn.shape
    index_at = [jax.random.randint(jax.random.fold_in(own_key, axis), (), 0, shape[axis]) for axis in range(len(shape))]
    drawn = drawn.at[tuple(index_at)].set(least)
    longest = shape.index(max(shape))
    index_at[longest] = (index_at[longest] + 1) % shape[longest]
    return drawn.at[tuple(index_at)].set(largest)


def strengthened(result, own_key, source, target, parts, factor):
    owner, partner = [(jnp.arange(result.shape[position]) // (result.shape[position] // parts)).reshape([-1 if axis == position else 1 for axis in range(result.ndim)]) for position in (source, target)]
    chosen = jax.random.permutation(own_key, parts)[partner]
    strong = (owner == chosen) | (owner == (partner + parts // 2) % parts)
    return jnp.where(strong, factor * result, result)


def block_scale(stream_key, shape, shards, low, top_value):
    loudness, own = 1.0, jax.random.fold_in(stream_key, 6)
    for dim, blocks in shards:
        draws = jnp.exp(jax.random.uniform(jax.random.fold_in(own, dim), (blocks,), jnp.float32, low / len(shards), top_value / len(shards)))
        loudness = loudness * jnp.repeat(draws, shape[dim] // blocks).reshape([-1 if axis == dim else 1 for axis in range(len(shape))])
    return loudness


def profile(count, total, reach, lean):
    portions = [(1 << 20) // math.isqrt(standing ** lean) + 1 for standing in range(2, count + 1)]
    rest, holding = total - reach - (count - 1), [1] * (count - 1)
    while rest > 0:
        movable = [i for i in range(count - 1) if holding[i] < reach]
        mass, budget = sum([portions[i] for i in movable]), rest
        for i in movable:
            more = min(reach - holding[i], max(1, budget * portions[i] // mass), rest)
            holding[i] = holding[i] + more
            rest = rest - more
    return np.array([reach] + holding)


def ragged_sizes(own_key, amount, total, bound, slope):
    if amount == 2:
        one = jax.random.randint(own_key, (), max(1, total - bound), min(bound, total - 1) + 1)
        return jnp.stack([one, total - one])
    lengths = jnp.asarray(profile(amount, total, bound, slope), jnp.int32)
    twos = (amount - 1) // 2
    donor, taker = lengths[1:1 + 2 * twos:2], lengths[2:2 + 2 * twos:2]
    room = jnp.minimum(donor - 1, bound - taker)
    shifted = jax.random.randint(jax.random.fold_in(own_key, 1), (twos,), 0, 1 << 20) % (room + 1)
    lengths = lengths.at[1:1 + 2 * twos:2].set(donor - shifted).at[2:2 + 2 * twos:2].set(taker + shifted)
    return lengths[jax.random.permutation(jax.random.fold_in(own_key, 2), amount)]


def scatter_about(own_key, extent, width, limit, cuts=(), kind=jnp.bfloat16):
    factor_of = block_scale(own_key, extent, cuts, -0.22, 0.18) if cuts else 1.0
    result = jax.random.normal(own_key, extent, jnp.float32) * width * factor_of
    return jnp.minimum(jnp.maximum(result, -limit), limit).astype(kind)


def heavy_noise(own_key, dims, deviation, most, cuts, heavy, kind=jnp.bfloat16):
    result = deviation * jax.random.normal(own_key, dims, jnp.float32)
    if cuts:
        result = result * block_scale(own_key, dims, cuts, -0.22, 0.18)
    return jnp.clip(strengthened(result, jax.random.fold_in(own_key, 3), *heavy), -most, most).astype(kind)


def setup_inputs(seed: int = 0) -> dict:
    seeds = jax.random.split(jax.random.key(seed), 21)
    tokens = scatter_about(seeds[0], (TOKENS, D), 1.0, 6.0, ((0, 32),))
    segment_ids = jax.vmap(lambda own: jnp.searchsorted(jnp.cumsum(ragged_sizes(own, max(LEN // 128, 4), LEN, LEN // 2, 1)), jnp.arange(LEN), side="right"))(jax.random.split(seeds[1], SEQS)).reshape((SEQS, LEN)).astype(jnp.int32)
    padding = plant((jax.random.randint(seeds[2], (SEQS, LEN), 0, 8) < 1).astype(jnp.int32), jax.random.fold_in(seeds[2], 1), 0, 1)
    qkv_weight = scatter_about(seeds[3], (D, 3 * D), D ** -0.5, 0.21875, ((1, 16),))
    query_bias = scatter_about(seeds[4], (D,), 0.2, 1.25, ((0, 16),))
    value_bias = scatter_about(seeds[5], (D,), 0.2, 1.25, ((0, 16),))
    out_weight = scatter_about(seeds[6], (D, D), (D // 16) ** -0.5, 0.875, ((0, 16),))
    out_bias = scatter_about(seeds[7], (D,), 0.2, 1.25, ((0, 16),))
    first_gain = jnp.clip(1.0 + 0.1 * jax.random.normal(seeds[8], (D,), jnp.float32), 0.5, 1.5).astype(jnp.bfloat16)
    first_shift = scatter_about(seeds[9], (D,), 0.2, 1.25, ((0, 16),))
    second_gain = jnp.clip(1.0 + 0.1 * jax.random.normal(seeds[10], (D,), jnp.float32), 0.5, 1.5).astype(jnp.bfloat16)
    second_shift = scatter_about(seeds[11], (D,), 0.2, 1.25, ((0, 16),))
    up_weight = scatter_about(seeds[12], (D, FF), D ** -0.5, 0.21875, ((1, 16),))
    up_bias = scatter_about(seeds[13], (FF,), 0.2, 1.25, ((0, 16),))
    down_weight = scatter_about(seeds[14], (FF, D), FF ** -0.5, 0.109375, ((0, 16),))
    down_bias = scatter_about(seeds[15], (D,), 0.2, 1.25, ((0, 16),))
    align_weight = scatter_about(seeds[16], (D, AL), D ** -0.5, 0.21875, ((1, 16),))
    align_bias = scatter_about(seeds[17], (AL,), 0.2, 1.25, ((0, 16),))
    grad_output = heavy_noise(seeds[18], (TOKENS, D), 1.0, 12.0, ((0, 32),), (0, 1, 32, 2.75))
    grad_aligned = scatter_about(seeds[19], (TOKENS, AL), 1.0, 6.0, ((0, 32),))
    return {"tokens": tokens, "segment_ids": segment_ids, "padding": padding, "qkv_weight": qkv_weight, "query_bias": query_bias, "value_bias": value_bias, "out_weight": out_weight, "out_bias": out_bias, "first_gain": first_gain, "first_shift": first_shift, "second_gain": second_gain, "second_shift": second_shift, "up_weight": up_weight, "up_bias": up_bias, "down_weight": down_weight, "down_bias": down_bias, "align_weight": align_weight, "align_bias": align_bias, "grad_output": grad_output, "grad_aligned": grad_aligned}


@jax.custom_vjp
def low(v):
    return lax.optimization_barrier(v.astype(jnp.bfloat16)).astype(jnp.float32)

@jax.custom_vjp
def low_back(v):
    return v

def low_keep(v):
    return (low(v), None)

def low_pass(kept, grad):
    return (grad,)

def back_keep(v):
    return (v, None)

def back_low(kept, grad):
    return (low(grad),)
low.defvjp(low_keep, low_pass)
low_back.defvjp(back_keep, back_low)

def matmul_high(left, right):
    return jnp.dot(left, right, precision=lax.Precision.HIGHEST, preferred_element_type=jnp.float32)

def layer_norm(values, norm_gain, norm_shift):
    row_mean = lax.optimization_barrier(jnp.mean(values, -1, keepdims=True))
    centered = values - row_mean
    variance = lax.optimization_barrier(jnp.mean(centered * centered, -1, keepdims=True))
    return centered * lax.rsqrt(variance + 1e-05) * norm_gain + norm_shift

def sequence_layer(params, seq_tokens, segment, is_valid):
    qkv_w, query_b, value_b, out_w, out_b, gain_one, shift_one, gain_two, shift_two, up_w, up_b, down_w, down_b, align_w, align_b = params
    length, model_width = seq_tokens.shape
    head_count = HEADS
    head_size = model_width // head_count
    scale = head_size ** (-0.5)
    normed_one = low(layer_norm(seq_tokens, gain_one, shift_one))
    qkv_out = matmul_high(normed_one, qkv_w)
    query = low_back(low(qkv_out[:, :model_width] + query_b))
    keys = low_back(low(qkv_out[:, model_width:2 * model_width]))
    values = low_back(low(qkv_out[:, 2 * model_width:] + value_b))
    block_rows = min(512, length)
    block_count = length // block_rows
    query_blocks = query.reshape(block_count, block_rows, head_count, head_size)
    key_heads = keys.reshape(length, head_count, head_size)
    value_heads = values.reshape(length, head_count, head_size)
    key_ids = jnp.arange(length, dtype=jnp.int32)
    starts = jnp.arange(block_count, dtype=jnp.int32) * block_rows

    def attend(block_item):
        query_block, row_start = block_item
        row_ids = row_start + jnp.arange(block_rows, dtype=jnp.int32)
        seg_rows = lax.dynamic_slice_in_dim(segment, row_start, block_rows)
        keep_mask = (seg_rows[:, None] == segment[None, :]) & ((is_valid[None, :] > 0.5) | (row_ids[:, None] == key_ids[None, :]))
        scores = jnp.einsum('qhd,khd->hqk', query_block, key_heads, precision=lax.Precision.HIGHEST) * scale
        scores = low_back(scores)
        scores = jnp.where(keep_mask[None], scores, -1e+30)
        row_max = lax.optimization_barrier(jnp.max(scores, -1, keepdims=True))
        row_lse = jnp.log(lax.optimization_barrier(jnp.sum(jnp.exp(scores - row_max), -1, keepdims=True))) + row_max
        attn_probs = low(jnp.exp(scores - row_lse))
        return jnp.einsum('hqk,khd->qhd', attn_probs, value_heads, precision=lax.Precision.HIGHEST)
    mixed = lax.map(jax.checkpoint(attend), (query_blocks, starts))
    mixed = low_back(low(mixed.reshape(length, model_width)))
    attn_out = low_back(matmul_high(mixed, out_w) + out_b)
    resid = seq_tokens + attn_out
    normed_two = low(layer_norm(resid, gain_two, shift_two))
    upper = low_back(matmul_high(normed_two, up_w) + up_b)
    active = low(jax.nn.gelu(upper, approximate=False))
    branch = low_back(matmul_high(active, down_w) + down_b)
    layer_out = is_valid[:, None] * (resid + branch)
    aligned = matmul_high(low(layer_out), align_w) + align_b
    return (layer_out, aligned)

def reference(tokens, segment_ids, padding, qkv_weight, query_bias, value_bias, out_weight, out_bias, first_gain, first_shift, second_gain, second_shift, up_weight, up_bias, down_weight, down_bias, align_weight, align_bias, grad_output, grad_aligned):
    params = tuple((item.astype(jnp.float32) for item in (qkv_weight, query_bias, value_bias, out_weight, out_bias, first_gain, first_shift, second_gain, second_shift, up_weight, up_bias, down_weight, down_bias, align_weight, align_bias)))
    seq_count = segment_ids.shape[0]
    length = segment_ids.shape[1]
    model_width = tokens.shape[1]
    valid_all = 1.0 - padding.astype(jnp.float32)
    sequences = tokens.astype(jnp.float32).reshape(seq_count, length, model_width)

    def forward(seq_inputs, weights):

        def one_sequence(seq_item):
            return sequence_layer(weights, seq_item[0], seq_item[1], seq_item[2])
        return lax.map(jax.checkpoint(one_sequence), (seq_inputs, segment_ids, valid_all))
    (layer_out, aligned), pull_back = jax.vjp(forward, sequences, params)
    cot_out = grad_output.astype(jnp.float32).reshape(layer_out.shape)
    cot_aligned = grad_aligned.astype(jnp.float32).reshape(aligned.shape)
    grad_seq, grad_params = pull_back((cot_out, cot_aligned))
    return (layer_out.reshape(-1, model_width).astype(jnp.bfloat16), aligned.reshape(-1, aligned.shape[-1]).astype(jnp.bfloat16), grad_seq.reshape(-1, model_width).astype(jnp.bfloat16), grad_params[0], grad_params[1], grad_params[2], grad_params[3], grad_params[4], grad_params[5], grad_params[6], grad_params[7], grad_params[8], grad_params[9], grad_params[10], grad_params[11], grad_params[12], grad_params[13], grad_params[14])
```

```python
import functools

import jax
import jax.numpy as jnp
from jax import lax
from jax.experimental import pallas as pl
from jax.experimental.pallas import tpu as pltpu
from jax.sharding import PartitionSpec as P

HEADS = 12
F32 = jnp.float32
BF16 = jnp.bfloat16
NEG = -1e30


def nn(a, b):
    return lax.dot_general(a, b, (((1,), (0,)), ((), ())), preferred_element_type=F32)


def nt(a, b):
    return lax.dot_general(a, b, (((1,), (1,)), ((), ())), preferred_element_type=F32)


def tn(a, b):
    return lax.dot_general(a, b, (((0,), (0,)), ((), ())), preferred_element_type=F32)


def col_sum(v):
    return jnp.sum(v, 0, keepdims=True)


def gelu_parts(u):
    z = jnp.abs(u) * (0.5 ** 0.5)
    ez = jnp.exp(-(z * z))
    t = 1.0 / (1.0 + 0.33 * z)
    poly = -0.13593485572044933
    for coef in (0.46271278142719047, -0.3554798541586114, 0.412577688277986, 0.044992638979585504,
                 0.2019288303128453, 0.18283654298343202, 0.18636614548593147):
        poly = poly * t + coef
    half_erfc = (0.5 * t) * poly * ez
    cdf = jnp.where(u > 0, 1.0 - half_erfc, half_erfc)
    return u * cdf, cdf + u * ez * 0.3989422804014327


def row_stats(x):
    mean = jnp.mean(x, -1, keepdims=True)
    centered = x - mean
    rstd = lax.rsqrt(jnp.mean(centered * centered, -1, keepdims=True) + 1e-05)
    return centered * rstd, rstd


def norm_back(grad_hat, hat, rstd):
    return rstd * (grad_hat - jnp.mean(grad_hat, -1, keepdims=True)
                   - hat * jnp.mean(grad_hat * hat, -1, keepdims=True))


def call(kernel, grid, ins, outs, scratch=(), name=None, prefetch=(), limit=60):
    return pl.pallas_call(
        kernel,
        grid_spec=pltpu.PrefetchScalarGridSpec(
            num_scalar_prefetch=len(prefetch), grid=grid,
            in_specs=[pl.BlockSpec(b, m, **({"pipeline_mode": pl.Buffered(1)} if once else {}))
                      for _, b, m, once in ins],
            out_specs=[pl.BlockSpec(b, m) for _, _, b, m in outs],
            scratch_shapes=list(scratch)),
        out_shape=[jax.ShapeDtypeStruct(s, d) for s, d, _, _ in outs],
        compiler_params=pltpu.CompilerParams(
            dimension_semantics=("arbitrary",) * len(grid), vmem_limit_bytes=limit << 20),
        name=name,
    )(*prefetch, *[a for a, _, _, _ in ins])


def whole(a):
    n = a.ndim
    return (a, a.shape, lambda *_: (0,) * n, True)


def rows(a, tile):
    return (a, (tile, a.shape[1]), lambda i, *_: (i, 0), False)


def rows_out(n, width, dtype, tile):
    return ((n, width), dtype, (tile, width), lambda i, *_: (i, 0))


def fixed_out(shape, dtype):
    n = len(shape)
    return (shape, dtype, shape, lambda *_: (0,) * n)


def project(tokens, vecs, qkv_bias, qkv_t, tile=256):
    n, d = tokens.shape

    def kernel(x_ref, v_ref, b_ref, w_ref, n_ref, o_ref):
        hat, _ = row_stats(x_ref[...].astype(F32))
        low = (hat * v_ref[4:5, :] + v_ref[5:6, :]).astype(BF16)
        n_ref[...] = low
        for part in range(3):
            cols = pl.ds(part * d, d)
            o_ref[:, cols] = (nt(low, w_ref[cols, :]) + b_ref[:, cols]).astype(BF16)

    return call(
        kernel, (n // tile,),
        [rows(tokens, tile), whole(vecs), whole(qkv_bias), whole(qkv_t)],
        [rows_out(n, d, BF16, tile), rows_out(n, 3 * d, BF16, tile)],
        name="project")


def pair_masks(shape):
    lane = lax.broadcasted_iota(jnp.int32, shape, 1)
    return lane < 64


def attend(qkv, seg_col, key_row, ranges, tq=128, tk=256):
    n = qkv.shape[0]
    d = qkv.shape[1] // 3
    pairs = d // 128

    def kernel(rng, q_ref, k_ref, v_ref, sc_ref, kr_ref, o_ref, lse_ref, mask, sa, sb, va, vb):
        @pl.when(pl.program_id(0) == 0)
        def _():
            @pl.loop(0, n // tq)
            def _(t):
                r = pl.ds(pl.multiple_of(t * tq, tq), tq)
                row_id = t * tq + lax.broadcasted_iota(jnp.int32, (tq, n), 0)
                col_id = lax.broadcasted_iota(jnp.int32, (tq, n), 1)
                keep = (sc_ref[r, :] == kr_ref[...]) | (row_id == col_id)
                m = jnp.where(keep, 0.0, NEG).astype(F32)
                for j in range(n // tk):
                    mask[j, r, :] = m[:, j * tk:(j + 1) * tk]

        v = v_ref[...]
        low_half = pair_masks((n, 128))
        zero = jnp.zeros_like(v)
        va[...] = jnp.where(low_half, v, zero)
        vb[...] = jnp.where(low_half, zero, v)
        half = pair_masks((tq, 128))

        @pl.loop(0, n // tq)
        def _(t):
            r = pl.ds(pl.multiple_of(t * tq, tq), tq)
            q = q_ref[r, :] * jnp.asarray(0.125, BF16)
            qz = jnp.zeros_like(q)
            qa = jnp.where(half, q, qz)
            qb = jnp.where(half, qz, q)
            lo, hi = rng[0, t], rng[1, t]

            def score(j, carry):
                ma, mb = carry
                kk = k_ref[pl.ds(pl.multiple_of(j * tk, tk), tk), :]
                m = mask[j, r, :]
                s = nt(qa, kk) + m
                sa[j] = s
                for e in range(0, tk, 128):
                    ma = jnp.maximum(ma, s[:, e:e + 128])
                s = nt(qb, kk) + m
                sb[j] = s
                for e in range(0, tk, 128):
                    mb = jnp.maximum(mb, s[:, e:e + 128])
                return ma, mb

            start = jnp.full((tq, 128), NEG, F32)
            ma, mb = lax.fori_loop(lo, hi, score, (start, start))
            ma = jnp.max(ma, 1, keepdims=True)
            mb = jnp.max(mb, 1, keepdims=True)

            def mix(j, carry):
                la, lb, acc = carry
                keys = pl.ds(pl.multiple_of(j * tk, tk), tk)
                p = jnp.exp(sa[j] - ma)
                for e in range(0, tk, 128):
                    la = la + p[:, e:e + 128]
                a1 = nn(p.astype(BF16), va[keys, :])
                p = jnp.exp(sb[j] - mb)
                for e in range(0, tk, 128):
                    lb = lb + p[:, e:e + 128]
                return la, lb, acc + a1 + nn(p.astype(BF16), vb[keys, :])

            nil = jnp.zeros((tq, 128), F32)
            la, lb, acc = lax.fori_loop(lo, hi, mix, (nil, nil, nil))
            la = jnp.sum(la, 1, keepdims=True)
            lb = jnp.sum(lb, 1, keepdims=True)
            o_ref[r, :] = (acc * jnp.where(half, 1.0 / la, 1.0 / lb)).astype(BF16)
            lse = jnp.where(half, ma + jnp.log(la), mb + jnp.log(lb)).T
            lse_ref[0:1, r] = lse[0:1, :]
            lse_ref[1:2, r] = lse[64:65, :]

    def block(first):
        return (qkv, (n, 128), lambda p, *_: (0, first * pairs + p), False)

    return call(
        kernel, (pairs,),
        [block(0), block(1), block(2), whole(seg_col), whole(key_row)],
        [((n, d), BF16, (n, 128), lambda p, *_: (0, p)),
         ((8 * pairs, n), F32, (8, n), lambda p, *_: (p, 0))],
        [pltpu.VMEM((n // tk, n, tk), F32), pltpu.VMEM((n // tk, tq, tk), F32),
         pltpu.VMEM((n // tk, tq, tk), F32), pltpu.VMEM((n, 128), BF16), pltpu.VMEM((n, 128), BF16)],
        name="attend", prefetch=(ranges,))


def attend_back(qkv, mixed, grad_mixed, lse, seg_row, key_col, ranges, tk=256, tq=256):
    n = qkv.shape[0]
    d = qkv.shape[1] // 3
    pairs = d // 128

    def kernel(rng, q_ref, k_ref, v_ref, o_ref, g_ref, lse_ref, sr_ref, kc_ref,
               dq_ref, dk_ref, dv_ref, bq_ref, bv_ref, mask, qa, qb, ga, gb, kt, dot_rows, dqt):
        @pl.when(pl.program_id(0) == 0)
        def _():
            @pl.loop(0, n // tk)
            def _(t):
                r = pl.ds(pl.multiple_of(t * tk, tk), tk)
                row_id = t * tk + lax.broadcasted_iota(jnp.int32, (tk, n), 0)
                col_id = lax.broadcasted_iota(jnp.int32, (tk, n), 1)
                keep = (kc_ref[r, :] == sr_ref[...]) | (row_id == col_id)
                m = jnp.where(keep, 0.0, NEG).astype(F32)
                for j in range(n // tq):
                    mask[j, r, :] = m[:, j * tq:(j + 1) * tq]

        half = pair_masks((n, 128))
        q = q_ref[...] * jnp.asarray(0.125, BF16)
        zero = jnp.zeros_like(q)
        qa[...] = jnp.where(half, q, zero)
        qb[...] = jnp.where(half, zero, q)
        g = g_ref[...]
        ga[...] = jnp.where(half, g, zero)
        gb[...] = jnp.where(half, zero, g)
        kt[...] = k_ref[...].astype(F32).T.astype(BF16)
        prod = (g.astype(F32) * o_ref[...].astype(F32)).T
        dot_rows[0:1, :] = col_sum(prod[:64])
        dot_rows[1:2, :] = col_sum(prod[64:])
        dqt[...] = jnp.zeros_like(dqt)

        @pl.loop(0, n // tk)
        def _(t):
            keys = pl.ds(pl.multiple_of(t * tk, tk), tk)
            kk = k_ref[keys, :]
            vv = v_ref[keys, :]

            def step(j, carry):
                dk, dv = carry
                cols = pl.ds(pl.multiple_of(j * tq, tq), tq)
                m = mask[j, keys, :]
                for h, (qh, gh) in enumerate(((qa, ga), (qb, gb))):
                    qq = qh[cols, :]
                    gg = gh[cols, :]
                    p = jnp.exp(nt(kk, qq) + m - lse_ref[h:h + 1, cols])
                    ds = (p * (nt(vv, gg) - dot_rows[h:h + 1, cols])).astype(BF16)
                    dv = dv + nn(p.astype(BF16), gg)
                    dk = dk + nn(ds, qq)
                    part = pl.ds(64 * h, 64)
                    dqt[part, cols] += nn(kt[part, keys], ds)
                return dk, dv

            nil = jnp.zeros((tk, 128), F32)
            dk, dv = lax.fori_loop(rng[0, t], rng[1, t], step, (nil, nil))
            dk_ref[keys, :] = dk.astype(BF16)
            dv_ref[keys, :] = dv.astype(BF16)

        dq = (dqt[...].T * 0.125).astype(BF16)
        dq_ref[...] = dq
        bq_ref[...] = jnp.broadcast_to(col_sum(dq.astype(F32)), (8, 128))
        bv_ref[...] = jnp.broadcast_to(col_sum(dv_ref[...].astype(F32)), (8, 128))

    def block(a, first=0):
        return (a, (n, 128), lambda p, *_: (0, first * pairs + p), False)

    cols = ((n, d), BF16, (n, 128), lambda p, *_: (0, p))
    sums = ((8, d), F32, (8, 128), lambda p, *_: (0, p))
    return call(
        kernel, (pairs,),
        [block(qkv, 0), block(qkv, 1), block(qkv, 2), block(mixed), block(grad_mixed),
         (lse, (8, n), lambda p, *_: (p, 0), False), whole(seg_row), whole(key_col)],
        [cols, cols, cols, sums, sums],
        [pltpu.VMEM((n // tq, n, tq), F32)] + [pltpu.VMEM((n, 128), BF16)] * 4
        + [pltpu.VMEM((128, n), BF16), pltpu.VMEM((8, n), F32), pltpu.VMEM((128, n), F32)],
        name="attend_back", prefetch=(ranges,))


def middle(tokens, mixed, grad_output, grad_aligned, valid_col, vecs, up_b, align_b,
           out_w, up_t, down_w, align_t, tile=256, chunk=768):
    n, d = tokens.shape
    ff, al = up_t.shape[0], align_t.shape[0]

    def kernel(x_ref, m_ref, go_ref, ga_ref, v_ref, vec_ref, ub_ref, ab_ref, wo_ref, wu_ref, wd_ref, wa_ref,
               n_ref, act_ref, du_ref, gb_ref, out_ref, al_ref, r_ref, rb_ref, dm_ref,
               s768_ref, sff_ref, sal_ref, branch, dn):
        @pl.when(pl.program_id(0) == 0)
        def _():
            s768_ref[...] = jnp.zeros_like(s768_ref)
            sff_ref[...] = jnp.zeros_like(sff_ref)
            sal_ref[...] = jnp.zeros_like(sal_ref)

        resid = x_ref[...].astype(F32) + nn(m_ref[...], wo_ref[...]) + vec_ref[2:3, :]
        hat, rstd = row_stats(resid)
        low = (hat * vec_ref[6:7, :] + vec_ref[7:8, :]).astype(BF16)
        n_ref[...] = low
        valid = v_ref[...]
        ga = ga_ref[...]
        sal_ref[0:1, :] += col_sum(ga.astype(F32))
        grad = valid * (go_ref[...].astype(F32) + nn(ga, wa_ref[...]))
        gb = grad.astype(BF16)
        gb_ref[...] = gb
        branch[...] = jnp.zeros_like(branch)
        dn[...] = jnp.zeros_like(dn)

        @pl.loop(0, ff // chunk)
        def _(t):
            part = pl.ds(pl.multiple_of(t * chunk, chunk), chunk)
            wu = wu_ref[part, :]
            wd = wd_ref[part, :]
            act, slope = gelu_parts(nt(n_ref[...], wu) + ub_ref[0:1, part])
            act = act.astype(BF16)
            act_ref[:, part] = act
            branch[...] += nn(act, wd)
            du = slope * nt(gb_ref[...], wd)
            du = du.astype(BF16)
            du_ref[:, part] = du
            sff_ref[0:1, part] += col_sum(du.astype(F32))
            dn[...] += nn(du, wu)

        out = (valid * (resid + branch[...] + vec_ref[3:4, :])).astype(BF16)
        out_ref[...] = out
        al_ref[...] = (nt(out, wa_ref[...]) + ab_ref[...]).astype(BF16)
        dn2 = dn[...]
        res = grad + norm_back(dn2 * vec_ref[6:7, :], hat, rstd)
        r_ref[...] = res
        rb = res.astype(BF16)
        rb_ref[...] = rb
        dm_ref[...] = nt(rb, wo_ref[...]).astype(BF16)
        s768_ref[0:1, :] += col_sum(gb.astype(F32))
        s768_ref[1:2, :] += col_sum(rb.astype(F32))
        s768_ref[2:3, :] += col_sum(dn2 * hat)
        s768_ref[3:4, :] += col_sum(dn2)

    r = functools.partial(rows_out, n, tile=tile)
    return call(
        kernel, (n // tile,),
        [rows(tokens, tile), rows(mixed, tile), rows(grad_output, tile), rows(grad_aligned, tile),
         rows(valid_col, tile), whole(vecs), whole(up_b), whole(align_b), whole(out_w), whole(up_t),
         whole(down_w), whole(align_t)],
        [r(d, BF16), r(ff, BF16), r(ff, BF16), r(d, BF16), r(d, BF16), r(al, BF16), r(d, F32), r(d, BF16),
         r(d, BF16), fixed_out((8, d), F32), fixed_out((8, ff), F32), fixed_out((8, al), F32)],
        [pltpu.VMEM((tile, d), F32), pltpu.VMEM((tile, d), F32)],
        name="middle")


def finish(tokens, resid_grad, dq, dk, dv, vecs, qkv_t, tile=256):
    n, d = tokens.shape

    def kernel(x_ref, r_ref, dq_ref, dk_ref, dv_ref, vec_ref, w_ref, o_ref, s_ref):
        @pl.when(pl.program_id(0) == 0)
        def _():
            s_ref[...] = jnp.zeros_like(s_ref)

        dn = nn(dq_ref[...], w_ref[0:d, :]) + nn(dk_ref[...], w_ref[d:2 * d, :]) + nn(dv_ref[...], w_ref[2 * d:, :])
        hat, rstd = row_stats(x_ref[...].astype(F32))
        o_ref[...] = (r_ref[...] + norm_back(dn * vec_ref[4:5, :], hat, rstd)).astype(BF16)
        s_ref[0:1, :] += col_sum(dn * hat)
        s_ref[1:2, :] += col_sum(dn)

    return call(
        kernel, (n // tile,),
        [rows(tokens, tile), rows(resid_grad, tile), rows(dq, tile), rows(dk, tile), rows(dv, tile),
         whole(vecs), whole(qkv_t)],
        [rows_out(n, d, BF16, tile), fixed_out((8, d), F32)],
        name="finish")
MESHID = pl.DeviceIdType.MESH


def coords():
    y = lax.axis_index("dp")
    f = lax.axis_index("fsdp")
    return y, f // 4, lax.rem(f // 2, 2), lax.rem(f, 2)


def fs(z, x, c):
    return z * 4 + x * 2 + c


def gather_body(items, nz, ins, outs, ssem, rsem, lsem):
    y, z, x, c = coords()
    me = fs(z, x, c)

    def dev(yy, zz, xx, cc):
        return (yy, fs(zz, xx, cc))

    zp = [lax.rem(z + d, nz) for d in range(nz)]
    zm = [lax.rem(z - d + nz, nz) for d in range(nz)]
    sib = dev(y, z, x, 1 - c)
    xn = dev(y, z, 1 - x, c)
    yn = dev(1 - y, z, x, c)

    barrier = pltpu.get_barrier_semaphore()
    peers = [sib, xn, yn] + [dev(y, zp[d], x, c) for d in range(1, nz)]
    for p in peers:
        pl.semaphore_signal(barrier, inc=1, device_id=p, device_id_type=MESHID)
    pl.semaphore_wait(barrier, len(peers))

    started = []
    NS = 6 * nz + 8

    class It:
        pass

    def rowspan(i, kind):
        a, r0, rows, third = items[i]
        if kind == "all":
            return r0, rows
        if kind == "plane":
            return r0 + y * third, rows - third
        if kind == "mine":
            return r0 + y * (rows - third), third
        if kind == "theirs":
            return r0 + (1 - y) * (rows - third), third

    def full(i, shard, kind):
        a = items[i][0]
        rw = ins[a].shape[0]
        r0, n = rowspan(i, kind)
        return outs[a].at[pl.ds(pl.multiple_of(shard * rw + r0, 8), n)]

    def own(i, kind):
        a = items[i][0]
        r0, n = rowspan(i, kind)
        return ins[a].at[pl.ds(pl.multiple_of(r0, 8), n)]

    COL, OTH, YY, SIB = 0, nz, 2 * nz, 4 * nz

    def copy(i, src, dst, slot, to):
        n = len([1 for s in started if s[0] == i])
        cp = pltpu.make_async_remote_copy(
            src_ref=src, dst_ref=dst, send_sem=ssem.at[i, n], recv_sem=rsem.at[i, slot],
            device_id=to, device_id_type=MESHID)
        cp.start()
        started.append((i, cp))

    def wait_in(i, shard, kind, slot):
        ref = full(i, shard, kind)
        pltpu.make_async_remote_copy(
            src_ref=ref, dst_ref=ref, send_sem=ssem.at[i, 0], recv_sem=rsem.at[i, slot],
            device_id=sib, device_id_type=MESHID).wait_recv()

    locals_ = []

    def start_own(i):
        cp = pltpu.make_async_copy(own(i, "all"), full(i, me, "all"), lsem.at[i])
        cp.start()
        locals_.append(cp)
        for d in range(1, nz):
            copy(i, own(i, "plane"), full(i, me, "plane"), COL + d, dev(y, zp[d], x, c))
        copy(i, own(i, "plane"), full(i, me, "plane"), OTH + 0, xn)
        copy(i, own(i, "all"), full(i, me, "all"), SIB + 0, sib)

    def stage_col(i):
        for d in range(1, nz):
            sh = fs(zm[d], x, c)
            wait_in(i, sh, "plane", COL + d)
            copy(i, full(i, sh, "plane"), full(i, sh, "plane"), OTH + d, xn)
            copy(i, full(i, sh, "mine"), full(i, sh, "mine"), YY + d, yn)
            copy(i, full(i, sh, "plane"), full(i, sh, "plane"), SIB + d, sib)

    def stage_oth(i):
        for d in range(nz):
            sh = fs(zm[d], 1 - x, c)
            wait_in(i, sh, "plane", OTH + d)
            copy(i, full(i, sh, "mine"), full(i, sh, "mine"), YY + nz + d, yn)
            copy(i, full(i, sh, "plane"), full(i, sh, "plane"), SIB + nz + d, sib)

    def stage_y(i):
        for d in range(1, 2 * nz):
            sh = fs(zm[d % nz], x if d < nz else 1 - x, c)
            wait_in(i, sh, "theirs", YY + d)
            copy(i, full(i, sh, "theirs"), full(i, sh, "theirs"), SIB + 2 * nz + d, sib)

    def stage_sib(i):
        wait_in(i, fs(z, x, 1 - c), "all", SIB + 0)
        for d in range(1, 2 * nz):
            sh = fs(zm[d % nz], x if d < nz else 1 - x, 1 - c)
            wait_in(i, sh, "plane", SIB + d)
            wait_in(i, sh, "theirs", SIB + 2 * nz + d)

    n = len(items)
    for i in range(n):
        start_own(i)
    for t in range(n + 3):
        if t < n:
            stage_col(t)
        if 0 <= t - 1 < n:
            stage_oth(t - 1)
        if 0 <= t - 2 < n:
            stage_y(t - 2)
        if 0 <= t - 3 < n:
            stage_sib(t - 3)
    for cp in locals_:
        cp.wait()
    for _, cp in started:
        cp.wait_send()


def gather_call(items, shards, nz, cid=0):
    n_in = len(shards)

    def kern(*refs):
        ins, outs = refs[:n_in], refs[n_in:2 * n_in]
        ssem, rsem, lsem = refs[2 * n_in:]
        gather_body(items, nz, ins, outs, ssem, rsem, lsem)

    n_items = len(items)
    return pl.pallas_call(
        kern,
        out_shape=[jax.ShapeDtypeStruct((4 * nz * s.shape[0], s.shape[1]), s.dtype) for s in shards],
        in_specs=[pl.BlockSpec(memory_space=pltpu.VMEM)] * n_in,
        out_specs=[pl.BlockSpec(memory_space=pl.ANY)] * n_in,
        scratch_shapes=[
            pltpu.SemaphoreType.DMA((n_items, 8 * nz)),
            pltpu.SemaphoreType.DMA((n_items, 8 * nz)),
            pltpu.SemaphoreType.DMA((n_items,)),
        ],
        compiler_params=pltpu.CompilerParams(collective_id=cid, has_side_effects=True),
        name="gather_weights",
    )(*shards)


def third_of(n):
    return max(16, n // 3 // 16 * 16)


def gather_all(shards, fast):
    if not fast:
        return [lax.all_gather(s, "fsdp", axis=0, tiled=True) for s in shards]
    *big, pack = shards
    nz = 4
    order = [(5, 0, pack.shape[0], 8 if pack.shape[0] >= 24 else 0)]
    return gather_call(GATHER_ITEMS(shards), shards, nz)


def GATHER_ITEMS(shards):
    items = []
    for i in (5, 0, 1, 2, 3, 4):
        r = shards[i].shape[0]
        items.append((i, 0, r, third_of(r)))
    return items
def weight_grads_reduced(pairs, pack, shard_rows, cuts, blocks, nz, collective):
    nw = len(pairs)
    lefts = [a for ls, _ in pairs for a in ls]
    rights = [r for _, r in pairs]
    n = rights[0].shape[0]
    width = rights[0].shape[1]
    max_left = max(sum(a.shape[1] for a in ls) for ls, _ in pairs)
    items = [(w, j) for w in range(nw) for j in range(width // blocks[w])]
    ni = len(items)

    def kernel(*refs):
        left_refs = refs[:len(lefts)]
        right_refs = refs[len(lefts):len(lefts) + nw]
        pos = len(lefts) + nw
        pack_ref = refs[pos]
        out_refs = refs[pos + 1:pos + 1 + nw]
        pack_out = refs[pos + 1 + nw]
        pos += 2 + nw
        lbuf, rbuf = refs[pos:pos + 2]
        part, sibb, yb, xb, zb, fin, finb = [refs[pos + 2 + k * nw:pos + 2 + (k + 1) * nw] for k in range(7)]
        pos += 2 + 7 * nw
        pbuf, ssem, rsem, psem, prsem, lsem = refs[pos:]

        y, z, x, c = coords()

        def dev(yy, zz, xx, cc):
            return (yy, zz * 4 + xx * 2 + cc)

        sib, xn, yn = dev(y, z, x, 1 - c), dev(y, z, 1 - x, c), dev(1 - y, z, x, c)
        zp = [lax.rem(z + d, nz) for d in range(nz)]
        zd = [dev(y, zp[d], x, c) for d in range(nz)]

        barrier = pltpu.get_barrier_semaphore()
        peers = [sib, xn, yn] + zd[1:]
        for p in peers:
            pl.semaphore_signal(barrier, inc=1, device_id=p, device_id_type=MESHID)

        loads = {}

        def load(w):
            at = 0
            got = []
            first = sum(len(ls) for ls, _ in pairs[:w])
            for k in range(len(pairs[w][0])):
                ref = left_refs[first + k]
                cols = ref.shape[1]
                cp = pltpu.make_async_copy(ref, lbuf.at[w % 2, :, pl.ds(at, cols)], lsem.at[w, k])
                cp.start()
                got.append(cp)
                at += cols
            cp = pltpu.make_async_copy(right_refs[w], rbuf.at[w % 2], lsem.at[w, 3])
            cp.start()
            got.append(cp)
            loads[w] = got

        started = []

        def send(i, k, src, dst, to):
            cp = pltpu.make_async_remote_copy(
                src_ref=src, dst_ref=dst, send_sem=ssem.at[i, k], recv_sem=rsem.at[i, k],
                device_id=to, device_id_type=MESHID)
            cp.start()
            started.append(cp)
            return cp

        flight = {}

        def spans(w):
            rw, a = shard_rows[w], cuts[w]
            return dict(plane=(y * a, rw - a), mine=(y * (rw - a), a), theirs=((1 - y) * (rw - a), a))

        def rows_of(w, kind):
            r0, k = spans(w)[kind]
            return pl.ds(pl.multiple_of(r0, 16), k)

        def compute(i):
            w, j = items[i]
            rw, lb = shard_rows[w], blocks[w]
            if j == 0:
                for cp in loads[w]:
                    cp.wait()
            cols = pl.ds(j * lb, lb)
            right = rbuf[w % 2, :, cols]
            for half in range(nz // 2):
                left = lbuf[w % 2, :, pl.ds(half * 8 * rw, 8 * rw)]
                g = tn(left, right).astype(BF16)
                for k in range(8):
                    part[w][j, k % 2, (k // 2) % 2, 2 * half + k // 4] = g[k * rw:(k + 1) * rw]
            if j == width // lb - 1 and w + 2 < nw:
                load(w + 2)
            flight[i, 0] = send(i, 0, part[w].at[j, 1 - c], sibb[w].at[j], sib)

        def stage_sib(i):
            w, j = items[i]
            flight[i, 0].wait_recv()
            mine = part[w].at[j, c]
            for xx in range(2):
                for zz in range(nz):
                    mine[xx, zz] = (mine[xx, zz].astype(F32) + sibb[w][j, xx, zz].astype(F32)).astype(BF16)
            flight[i, 1] = send(i, 1, mine.at[:, :, rows_of(w, "theirs")], yb[w].at[j], yn)

        def stage_y(i):
            w, j = items[i]
            flight[i, 1].wait_recv()
            mine = part[w].at[j, c]
            r = rows_of(w, "mine")
            for xx in range(2):
                for zz in range(nz):
                    mine[xx, zz, r] = (mine[xx, zz, r].astype(F32) + yb[w][j, xx, zz].astype(F32)).astype(BF16)
            flight[i, 2] = send(i, 2, mine.at[1 - x, :, rows_of(w, "plane")], xb[w].at[j], xn)

        def stage_x(i):
            w, j = items[i]
            flight[i, 2].wait_recv()
            mine = part[w].at[j, c, x]
            r = rows_of(w, "plane")
            for zz in range(nz):
                mine[zz, r] = (mine[zz, r].astype(F32) + xb[w][j, zz].astype(F32)).astype(BF16)
            for d in range(1, nz):
                flight[i, 2 + d] = send(i, 2 + d, mine.at[zp[d], r], zb[w].at[j, d - 1], zd[d])

        def stage_z(i):
            w, j = items[i]
            total = part[w][j, c, x, z, rows_of(w, "plane")].astype(F32)
            for d in range(1, nz):
                flight[i, 2 + d].wait_recv()
                total = total + zb[w][j, d - 1].astype(F32)
            fin[w][j] = total.astype(BF16)
            flight[i, 2 + nz] = send(i, 2 + nz, fin[w].at[j], finb[w].at[j], yn)

        def stage_out(i):
            w, j = items[i]
            rw, a, lb = shard_rows[w], cuts[w], blocks[w]
            cols = pl.ds(j * lb, lb)
            flight[i, 2 + nz].wait_recv()
            here, there = fin[w].at[j], finb[w].at[j]

            def at(r0, k):
                return pl.ds(pl.multiple_of(r0, 16), k)

            out_refs[w][at(y * (rw - a), a), cols] = here[at(y * (rw - 2 * a), a)].astype(F32)
            out_refs[w][at((1 - y) * (rw - a), a), cols] = there[at((1 - y) * (rw - 2 * a), a)].astype(F32)
            if rw > 2 * a:
                out_refs[w][pl.ds(a, rw - 2 * a), cols] = (
                    here[at((1 - y) * a, rw - 2 * a)].astype(F32) + there[at(y * a, rw - 2 * a)].astype(F32))

        pack_to = [sib, yn, xn, dev(y, z + 1 - 2 * lax.rem(z, 2), x, c), dev(y, lax.rem(z + 2, 4), x, c)]
        pack_cp = {}

        def pack_step(k):
            if k > 0:
                pack_cp[k - 1].wait()
                pbuf[0, k] = pbuf[0, k - 1] + pbuf[1, k - 1]
            else:
                pbuf[0, 0] = pack_ref[...]
            if k < len(pack_to):
                cp = pltpu.make_async_remote_copy(
                    src_ref=pbuf.at[0, k], dst_ref=pbuf.at[1, k], send_sem=psem.at[k], recv_sem=prsem.at[k],
                    device_id=pack_to[k], device_id_type=MESHID)
                cp.start()
                pack_cp[k] = cp
            else:
                pack_out[...] = pbuf[0, k]

        load(0)
        load(1)
        pl.semaphore_wait(barrier, len(peers))
        stages = [compute, stage_sib, stage_y, stage_x, stage_z, stage_out]
        for t in range(ni + len(stages) - 1):
            for k, stage in enumerate(stages):
                if 0 <= t - k < ni:
                    stage(t - k)
            if t <= len(pack_to):
                pack_step(t)
        for cp in started:
            cp.wait_send()

    any_spec = pl.BlockSpec(memory_space=pl.ANY)
    vm = pl.BlockSpec(memory_space=pltpu.VMEM)

    def per_weight(make):
        return [pltpu.VMEM(make(width // b, shard_rows[w], cuts[w], b), BF16) for w, b in enumerate(blocks)]

    scratch = [pltpu.VMEM((2, n, max_left), BF16), pltpu.VMEM((2, n, width), BF16)]
    scratch += per_weight(lambda j, rw, a, b: (j, 2, 2, nz, rw, b))
    scratch += per_weight(lambda j, rw, a, b: (j, 2, nz, rw, b))
    scratch += per_weight(lambda j, rw, a, b: (j, 2, nz, a, b))
    scratch += per_weight(lambda j, rw, a, b: (j, nz, rw - a, b))
    scratch += per_weight(lambda j, rw, a, b: (j, nz - 1, rw - a, b))
    scratch += per_weight(lambda j, rw, a, b: (j, rw - a, b))
    scratch += per_weight(lambda j, rw, a, b: (j, rw - a, b))
    scratch += [
        pltpu.VMEM((2, 6) + pack.shape, F32),
        pltpu.SemaphoreType.DMA((ni, 3 + nz)), pltpu.SemaphoreType.DMA((ni, 3 + nz)),
        pltpu.SemaphoreType.DMA((6,)), pltpu.SemaphoreType.DMA((6,)), pltpu.SemaphoreType.DMA((nw, 4)),
    ]
    outs = pl.pallas_call(
        kernel,
        out_shape=[jax.ShapeDtypeStruct((rw, width), F32) for rw in shard_rows]
        + [jax.ShapeDtypeStruct(pack.shape, F32)],
        in_specs=[any_spec] * (len(lefts) + nw) + [vm],
        out_specs=[vm] * (nw + 1),
        scratch_shapes=scratch,
        compiler_params=pltpu.CompilerParams(
            collective_id=collective, has_side_effects=True, vmem_limit_bytes=63 << 20),
        name="reduce_grads",
    )(*lefts, *rights, pack)
    return outs[:nw], outs[nw]


def reduce_all(pairs, pack, fast):
    if fast:
        left_rows = [sum(a.shape[1] for a in ls) for ls, _ in pairs]
        shard_rows = [r // 16 for r in left_rows]
        cuts = [max(16, (r * 5 // 16) // 16 * 16) for r in shard_rows]
        blocks = [384, 256, 256, 768, 256]
        return weight_grads_reduced(pairs, pack, shard_rows, cuts, blocks, 4, 1)
    terms = [jnp.concatenate([tn(a, r).astype(BF16) for a in ls], 0) for ls, r in pairs]
    got = [lax.psum(lax.psum_scatter(t, "fsdp", scatter_dimension=0, tiled=True), "dp").astype(F32) for t in terms]
    return got, lax.psum(pack, ("dp", "fsdp"))
def per_device(mesh_shape, *args):
    (tokens, segment_ids, padding, qkv_weight, query_bias, value_bias, out_weight, out_bias,
     first_gain, first_shift, second_gain, second_shift, up_weight, up_bias, down_weight, down_bias,
     align_weight, align_bias, grad_output, grad_aligned) = args
    n, d = tokens.shape
    shards = [qkv_weight.T, out_weight, up_weight.T, down_weight, align_weight.T]
    small = [query_bias, value_bias, out_bias, down_bias, first_gain, first_shift, second_gain, second_shift]
    fast = mesh_shape["dp"] == 2 and mesh_shape["fsdp"] == 16
    own = query_bias.shape[0]
    pack = jnp.concatenate(small + [up_bias, align_bias])
    pad = -pack.shape[0] % (48 * 128)
    pack = jnp.pad(pack, (0, pad)).reshape(-1, 128)
    gathered = gather_all(shards + [pack], fast)
    qkv_t, out_w, up_t, down_w, align_t, packs = gathered
    members = mesh_shape["fsdp"]
    packs = packs.reshape(members, -1).astype(F32)
    vecs = packs[:, :8 * own].reshape(members, 8, own).transpose(1, 0, 2).reshape(8, d)
    ub, ab = up_bias.shape[0], align_bias.shape[0]
    up_b = packs[:, 8 * own:8 * own + ub].reshape(1, -1)
    align_b = packs[:, 8 * own + ub:8 * own + ub + ab].reshape(1, -1)
    qkv_b = jnp.concatenate([vecs[0:1], jnp.zeros((1, d), F32), vecs[1:2]], 1)

    seg = segment_ids[0]
    pad_row = padding[0]
    keys = jnp.where(pad_row == 0, seg, -1)
    valid_col = (1.0 - pad_row.astype(F32))[:, None]

    def ranges(tile, block):
        first = seg[::tile]
        last = seg[tile - 1::tile]
        lo = jnp.sum(seg[None, :] < first[:, None], 1, dtype=jnp.int32) // block
        hi = (jnp.sum(seg[None, :] <= last[:, None], 1, dtype=jnp.int32) + block - 1) // block
        return jnp.stack([lo, hi])

    normed, qkv = project(tokens, vecs, qkv_b, qkv_t)
    mixed, lse = attend(qkv, seg[:, None], keys[None, :], ranges(128, 256))
    (n2, act, du, gb, block_out, aligned, res, rb, dm, s768, sff, sal) = middle(
        tokens, mixed, grad_output, grad_aligned, valid_col, vecs, up_b, align_b, out_w, up_t, down_w, align_t)
    dq, dk, dv, bq, bv = attend_back(qkv, mixed, dm, lse, seg[None, :], keys[:, None], ranges(256, 256))
    grad_tokens, s1 = finish(tokens, res, dq, dk, dv, vecs, qkv_t)

    sums = jnp.concatenate(
        [bq[0:1], bv[0:1], s768[1:2], s768[0:1], s1[0:2], s768[2:4]], 0)
    pack = jnp.concatenate([sums.reshape(-1), sff[0], sal[0]]).reshape(-1, 128)
    pairs = [([grad_aligned], block_out), ([act], gb), ([du], n2), ([mixed], rb), ([dq, dk, dv], normed)]
    (g_align, g_down, g_up, g_out, g_qkv), pack = reduce_all(pairs, pack, fast)
    me = lax.axis_index("fsdp")
    pack = pack.reshape(-1)
    vec = lax.dynamic_slice(pack[:8 * d].reshape(8, d), (0, me * own), (8, own))
    ff, al = up_t.shape[0], align_t.shape[0]
    g_ub = lax.dynamic_slice(pack, (8 * d + me * ub,), (ub,))
    g_ab = lax.dynamic_slice(pack, (8 * d + ff + me * ab,), (ab,))
    return (block_out, aligned, grad_tokens, g_qkv.T, vec[0], vec[1], g_out, vec[2], vec[4], vec[5], vec[6],
            vec[7], g_up.T, g_ub, g_down, vec[3], g_align.T, g_ab)


def solution(mesh):
    rows_spec = P(("dp", "fsdp"), None)
    vec, by_col, by_row = P("fsdp"), P(None, "fsdp"), P("fsdp", None)
    in_specs = (rows_spec, rows_spec, rows_spec, by_col, vec, vec, by_row, vec, vec, vec, vec, vec,
                by_col, vec, by_row, vec, by_col, vec, rows_spec, rows_spec)
    out_specs = (rows_spec, rows_spec, rows_spec, by_col, vec, vec, by_row, vec, vec, vec, vec, vec,
                 by_col, vec, by_row, vec, by_col, vec)
    return jax.shard_map(functools.partial(per_device, dict(mesh.shape)), mesh=mesh, in_specs=in_specs,
                         out_specs=out_specs, check_vma=False)
```

```python
import functools

import jax
import jax.numpy as jnp
from jax import lax
from jax.experimental import pallas as pl
from jax.experimental.pallas import tpu as pltpu
from jax.sharding import PartitionSpec as P

HEADS = 12
F32 = jnp.float32
BF16 = jnp.bfloat16
NEG = -1e30


def nn(a, b):
    return lax.dot_general(a, b, (((1,), (0,)), ((), ())), preferred_element_type=F32)


def nt(a, b):
    return lax.dot_general(a, b, (((1,), (1,)), ((), ())), preferred_element_type=F32)


def tn(a, b):
    return lax.dot_general(a, b, (((0,), (0,)), ((), ())), preferred_element_type=F32)


def col_sum(v):
    return jnp.sum(v, 0, keepdims=True)


def gelu_parts(u):
    z = jnp.abs(u) * (0.5 ** 0.5)
    ez = jnp.exp(-(z * z))
    t = 1.0 / (1.0 + 0.33 * z)
    poly = -0.13593485572044933
    for coef in (0.46271278142719047, -0.3554798541586114, 0.412577688277986, 0.044992638979585504,
                 0.2019288303128453, 0.18283654298343202, 0.18636614548593147):
        poly = poly * t + coef
    half_erfc = (0.5 * t) * poly * ez
    cdf = jnp.where(u > 0, 1.0 - half_erfc, half_erfc)
    return u * cdf, cdf + u * ez * 0.3989422804014327


def row_stats(x):
    mean = jnp.mean(x, -1, keepdims=True)
    centered = x - mean
    rstd = lax.rsqrt(jnp.mean(centered * centered, -1, keepdims=True) + 1e-05)
    return centered * rstd, rstd


def norm_back(grad_hat, hat, rstd):
    return rstd * (grad_hat - jnp.mean(grad_hat, -1, keepdims=True)
                   - hat * jnp.mean(grad_hat * hat, -1, keepdims=True))


def call(kernel, grid, ins, outs, scratch=(), name=None, prefetch=(), limit=60):
    return pl.pallas_call(
        kernel,
        grid_spec=pltpu.PrefetchScalarGridSpec(
            num_scalar_prefetch=len(prefetch), grid=grid,
            in_specs=[pl.BlockSpec(b, m, **({"pipeline_mode": pl.Buffered(1)} if once else {}))
                      for _, b, m, once in ins],
            out_specs=[pl.BlockSpec(b, m) for _, _, b, m in outs],
            scratch_shapes=list(scratch)),
        out_shape=[jax.ShapeDtypeStruct(s, d) for s, d, _, _ in outs],
        compiler_params=pltpu.CompilerParams(
            dimension_semantics=("arbitrary",) * len(grid), vmem_limit_bytes=limit << 20),
        name=name,
    )(*prefetch, *[a for a, _, _, _ in ins])


def whole(a):
    n = a.ndim
    return (a, a.shape, lambda *_: (0,) * n, True)


def rows(a, tile):
    return (a, (tile, a.shape[1]), lambda i, *_: (i, 0), False)


def rows_out(n, width, dtype, tile):
    return ((n, width), dtype, (tile, width), lambda i, *_: (i, 0))


def fixed_out(shape, dtype):
    n = len(shape)
    return (shape, dtype, shape, lambda *_: (0,) * n)


def project(tokens, vecs, qkv_bias, qkv_t, tile=256):
    n, d = tokens.shape

    def kernel(x_ref, v_ref, b_ref, w_ref, n_ref, o_ref):
        hat, _ = row_stats(x_ref[...].astype(F32))
        low = (hat * v_ref[4:5, :] + v_ref[5:6, :]).astype(BF16)
        n_ref[...] = low
        for part in range(3):
            cols = pl.ds(part * d, d)
            o_ref[:, cols] = (nt(low, w_ref[cols, :]) + b_ref[:, cols]).astype(BF16)

    return call(
        kernel, (n // tile,),
        [rows(tokens, tile), whole(vecs), whole(qkv_bias), whole(qkv_t)],
        [rows_out(n, d, BF16, tile), rows_out(n, 3 * d, BF16, tile)],
        name="project")


def pair_masks(shape):
    lane = lax.broadcasted_iota(jnp.int32, shape, 1)
    return lane < 64


def windows(seg, tile, step=256):
    n = seg.shape[0]
    first = seg[::tile]
    last = seg[tile - 1::tile]
    lo = jnp.sum(seg[None, :] < first[:, None], 1, dtype=jnp.int32) // 128 * 128
    hi = jnp.sum(seg[None, :] <= last[:, None], 1, dtype=jnp.int32)
    count = (hi - lo + step - 1) // step
    return jnp.stack([jnp.minimum(lo, n - count * step), count])


def fill_mask(mask, rows_ref, cols_ref, n, tile=256):
    @pl.when(pl.program_id(0) == 0)
    def _():
        @pl.loop(0, n // tile)
        def _(t):
            r = pl.ds(pl.multiple_of(t * tile, tile), tile)
            row_id = t * tile + lax.broadcasted_iota(jnp.int32, (tile, n), 0)
            col_id = lax.broadcasted_iota(jnp.int32, (tile, n), 1)
            keep = (rows_ref[r, :] == cols_ref[...]) | (row_id == col_id)
            mask[r, :] = jnp.where(keep, 0.0, NEG).astype(F32)


def attend(qkv, seg_col, key_row, wins, tq=256, step=256):
    n = qkv.shape[0]
    d = qkv.shape[1] // 3
    pairs = d // 128

    def kernel(win, q_ref, k_ref, v_ref, sc_ref, kr_ref, o_ref, lse_ref, mask, va, vb):
        fill_mask(mask, sc_ref, kr_ref, n)
        v = v_ref[...]
        low_half = pair_masks((n, 128))
        zero = jnp.zeros_like(v)
        va[...] = jnp.where(low_half, v, zero)
        vb[...] = jnp.where(low_half, zero, v)
        half = pair_masks((tq, 128))

        @pl.loop(0, n // tq)
        def _(t):
            r = pl.ds(pl.multiple_of(t * tq, tq), tq)
            first = pl.multiple_of(win[0, t], 128)

            for count in range(1, n // step + 1):
                @pl.when(win[1, t] == count)
                def _():
                    keys = pl.ds(first, count * step)
                    q = q_ref[r, :] * jnp.asarray(0.125, BF16)
                    qz = jnp.zeros_like(q)
                    kk = k_ref[keys, :]
                    outs, tops, sums = [], [], []
                    for qh, vh in ((jnp.where(half, q, qz), va), (jnp.where(half, qz, q), vb)):
                        s = nt(qh, kk) + mask[r, keys]
                        top = jnp.max(s, 1, keepdims=True)
                        p = jnp.exp(s - top)
                        sums.append(jnp.sum(p, 1, keepdims=True))
                        tops.append(top)
                        outs.append(nn(p.astype(BF16), vh[keys, :]))
                    (la, lb), (ma, mb) = sums, tops
                    o_ref[r, :] = ((outs[0] + outs[1]) * jnp.where(half, 1.0 / la, 1.0 / lb)).astype(BF16)
                    lse = jnp.where(half, ma + jnp.log(la), mb + jnp.log(lb)).T
                    lse_ref[0:1, r] = lse[0:1, :]
                    lse_ref[1:2, r] = lse[64:65, :]

    def block(first):
        return (qkv, (n, 128), lambda p, *_: (0, first * pairs + p), False)

    return call(
        kernel, (pairs,),
        [block(0), block(1), block(2), whole(seg_col), whole(key_row)],
        [((n, d), BF16, (n, 128), lambda p, *_: (0, p)),
         ((8 * pairs, n), F32, (8, n), lambda p, *_: (p, 0))],
        [pltpu.VMEM((n, n), F32), pltpu.VMEM((n, 128), BF16), pltpu.VMEM((n, 128), BF16)],
        name="attend", prefetch=(wins,))


def attend_back(qkv, mixed, grad_mixed, lse, seg_row, key_col, wins, tk=256, step=256):
    n = qkv.shape[0]
    d = qkv.shape[1] // 3
    pairs = d // 128

    def kernel(win, q_ref, k_ref, v_ref, o_ref, g_ref, lse_ref, sr_ref, kc_ref,
               dq_ref, dk_ref, dv_ref, bq_ref, bv_ref, mask, qa, qb, ga, gb, kt, dots, dqt):
        fill_mask(mask, kc_ref, sr_ref, n)
        half = pair_masks((n, 128))
        q = q_ref[...] * jnp.asarray(0.125, BF16)
        zero = jnp.zeros_like(q)
        qa[...] = jnp.where(half, q, zero)
        qb[...] = jnp.where(half, zero, q)
        g = g_ref[...]
        ga[...] = jnp.where(half, g, zero)
        gb[...] = jnp.where(half, zero, g)
        kt[...] = k_ref[...].astype(F32).T.astype(BF16)
        prod = (g.astype(F32) * o_ref[...].astype(F32)).T
        dots[0:1, :] = col_sum(prod[:64])
        dots[1:2, :] = col_sum(prod[64:])
        dqt[...] = jnp.zeros_like(dqt)

        @pl.loop(0, n // tk)
        def _(t):
            keys = pl.ds(pl.multiple_of(t * tk, tk), tk)
            first = pl.multiple_of(win[0, t], 128)

            for count in range(1, n // step + 1):
                @pl.when(win[1, t] == count)
                def _():
                    kk = k_ref[keys, :]
                    vv = v_ref[keys, :]
                    dk = dv = None
                    for e in range(count):
                        cols = pl.ds(pl.multiple_of(first + e * step, 128), step)
                        m = mask[keys, cols]
                        for h, (qh, gh) in enumerate(((qa, ga), (qb, gb))):
                            qq = qh[cols, :]
                            gg = gh[cols, :]
                            p = jnp.exp(nt(kk, qq) + m - lse_ref[h:h + 1, cols])
                            ds = (p * (nt(vv, gg) - dots[h:h + 1, cols])).astype(BF16)
                            pv = nn(p.astype(BF16), gg)
                            pk = nn(ds, qq)
                            dv = pv if dv is None else dv + pv
                            dk = pk if dk is None else dk + pk
                            part = pl.ds(64 * h, 64)
                            dqt[part, cols] += nn(kt[part, keys], ds)
                    dk_ref[keys, :] = dk.astype(BF16)
                    dv_ref[keys, :] = dv.astype(BF16)

        dq = (dqt[...].T * 0.125).astype(BF16)
        dq_ref[...] = dq
        bq_ref[...] = jnp.broadcast_to(col_sum(dq.astype(F32)), (8, 128))
        bv_ref[...] = jnp.broadcast_to(col_sum(dv_ref[...].astype(F32)), (8, 128))

    def block(a, first=0):
        return (a, (n, 128), lambda p, *_: (0, first * pairs + p), False)

    cols = ((n, d), BF16, (n, 128), lambda p, *_: (0, p))
    sums = ((8, d), F32, (8, 128), lambda p, *_: (0, p))
    return call(
        kernel, (pairs,),
        [block(qkv, 0), block(qkv, 1), block(qkv, 2), block(mixed), block(grad_mixed),
         (lse, (8, n), lambda p, *_: (p, 0), False), whole(seg_row), whole(key_col)],
        [cols, cols, cols, sums, sums],
        [pltpu.VMEM((n, n), F32)] + [pltpu.VMEM((n, 128), BF16)] * 4
        + [pltpu.VMEM((128, n), BF16), pltpu.VMEM((8, n), F32), pltpu.VMEM((128, n), F32)],
        name="attend_back", prefetch=(wins,))


def middle(tokens, mixed, grad_output, grad_aligned, valid_col, vecs, up_b, align_b,
           out_w, up_t, down_w, align_t, tile=256, chunk=768):
    n, d = tokens.shape
    ff, al = up_t.shape[0], align_t.shape[0]

    def kernel(x_ref, m_ref, go_ref, ga_ref, v_ref, vec_ref, ub_ref, ab_ref, wo_ref, wu_ref, wd_ref, wa_ref,
               n_ref, act_ref, du_ref, gb_ref, out_ref, al_ref, r_ref, rb_ref, dm_ref,
               s768_ref, sff_ref, sal_ref, branch, dn):
        @pl.when(pl.program_id(0) == 0)
        def _():
            s768_ref[...] = jnp.zeros_like(s768_ref)
            sff_ref[...] = jnp.zeros_like(sff_ref)
            sal_ref[...] = jnp.zeros_like(sal_ref)

        resid = x_ref[...].astype(F32) + nn(m_ref[...], wo_ref[...]) + vec_ref[2:3, :]
        hat, rstd = row_stats(resid)
        low = (hat * vec_ref[6:7, :] + vec_ref[7:8, :]).astype(BF16)
        n_ref[...] = low
        valid = v_ref[...]
        ga = ga_ref[...]
        sal_ref[0:1, :] += col_sum(ga.astype(F32))
        grad = valid * (go_ref[...].astype(F32) + nn(ga, wa_ref[...]))
        gb = grad.astype(BF16)
        gb_ref[...] = gb
        branch[...] = jnp.zeros_like(branch)
        dn[...] = jnp.zeros_like(dn)

        @pl.loop(0, ff // chunk)
        def _(t):
            part = pl.ds(pl.multiple_of(t * chunk, chunk), chunk)
            wu = wu_ref[part, :]
            wd = wd_ref[part, :]
            act, slope = gelu_parts(nt(n_ref[...], wu) + ub_ref[0:1, part])
            act = act.astype(BF16)
            act_ref[:, part] = act
            branch[...] += nn(act, wd)
            du = slope * nt(gb_ref[...], wd)
            du = du.astype(BF16)
            du_ref[:, part] = du
            sff_ref[0:1, part] += col_sum(du.astype(F32))
            dn[...] += nn(du, wu)

        out = (valid * (resid + branch[...] + vec_ref[3:4, :])).astype(BF16)
        out_ref[...] = out
        al_ref[...] = (nt(out, wa_ref[...]) + ab_ref[...]).astype(BF16)
        dn2 = dn[...]
        res = grad + norm_back(dn2 * vec_ref[6:7, :], hat, rstd)
        r_ref[...] = res
        rb = res.astype(BF16)
        rb_ref[...] = rb
        dm_ref[...] = nt(rb, wo_ref[...]).astype(BF16)
        s768_ref[0:1, :] += col_sum(gb.astype(F32))
        s768_ref[1:2, :] += col_sum(rb.astype(F32))
        s768_ref[2:3, :] += col_sum(dn2 * hat)
        s768_ref[3:4, :] += col_sum(dn2)

    r = functools.partial(rows_out, n, tile=tile)
    return call(
        kernel, (n // tile,),
        [rows(tokens, tile), rows(mixed, tile), rows(grad_output, tile), rows(grad_aligned, tile),
         rows(valid_col, tile), whole(vecs), whole(up_b), whole(align_b), whole(out_w), whole(up_t),
         whole(down_w), whole(align_t)],
        [r(d, BF16), r(ff, BF16), r(ff, BF16), r(d, BF16), r(d, BF16), r(al, BF16), r(d, F32), r(d, BF16),
         r(d, BF16), fixed_out((8, d), F32), fixed_out((8, ff), F32), fixed_out((8, al), F32)],
        [pltpu.VMEM((tile, d), F32), pltpu.VMEM((tile, d), F32)],
        name="middle")


def finish(tokens, resid_grad, dq, dk, dv, vecs, qkv_t, tile=256):
    n, d = tokens.shape

    def kernel(x_ref, r_ref, dq_ref, dk_ref, dv_ref, vec_ref, w_ref, o_ref, s_ref):
        @pl.when(pl.program_id(0) == 0)
        def _():
            s_ref[...] = jnp.zeros_like(s_ref)

        dn = nn(dq_ref[...], w_ref[0:d, :]) + nn(dk_ref[...], w_ref[d:2 * d, :]) + nn(dv_ref[...], w_ref[2 * d:, :])
        hat, rstd = row_stats(x_ref[...].astype(F32))
        o_ref[...] = (r_ref[...] + norm_back(dn * vec_ref[4:5, :], hat, rstd)).astype(BF16)
        s_ref[0:1, :] += col_sum(dn * hat)
        s_ref[1:2, :] += col_sum(dn)

    return call(
        kernel, (n // tile,),
        [rows(tokens, tile), rows(resid_grad, tile), rows(dq, tile), rows(dk, tile), rows(dv, tile),
         whole(vecs), whole(qkv_t)],
        [rows_out(n, d, BF16, tile), fixed_out((8, d), F32)],
        name="finish")
MESHID = pl.DeviceIdType.MESH


def coords():
    y = lax.axis_index("dp")
    f = lax.axis_index("fsdp")
    return y, f // 4, lax.rem(f // 2, 2), lax.rem(f, 2)


def third_of(n):
    return max(16, n // 3 // 16 * 16)


class Gather:
    KINDS = ("Z", "X", "Yc", "Yo", "Sc", "So", "Syc", "Syo")

    def __init__(self, items, nz, ssem, rsem):
        self.items, self.nz, self.ssem, self.rsem = items, nz, ssem, rsem
        self.y, self.z, self.x, self.c = coords()

    def shard(self, z, x, c):
        return z * 4 + x * 2 + c

    def behind(self, d):
        return lax.rem(self.z - d + self.nz, self.nz)

    def order(self, k):
        z, nz = self.z, self.nz
        near = jnp.minimum(z, nz - 1 - z)
        paired = jnp.where(lax.rem(k, 2) == 1, (k + 1) // 2, nz - k // 2)
        rest = jnp.where(z > nz - 1 - z, k - near, nz - (k - near))
        return lax.rem(jnp.where(k <= 2 * near, paired, rest), nz)

    def device(self, kind, d):
        y, z, x, c = self.y, self.z, self.x, self.c
        if kind == "Z":
            z = d
        elif kind == "X":
            x = 1 - x
        elif kind[0] == "Y":
            y = 1 - y
        else:
            c = 1 - c
        return (y, self.shard(z, x, c))

    def enter(self):
        barrier = pltpu.get_barrier_semaphore()
        peers = [("Sc", 0), ("X", 0), ("Yc", 0)] + [("Z", lax.rem(self.z + d, self.nz)) for d in range(1, self.nz)]
        for kind, d in peers:
            pl.semaphore_signal(barrier, inc=1, device_id=self.device(kind, d), device_id_type=MESHID)
        pl.semaphore_wait(barrier, len(peers))

    def span(self, i, rows):
        n, third = self.items[i][0], self.items[i][1]
        return {"all": (0, n), "plane": (self.y * third, n - third), "mine": (self.y * (n - third), third),
                "theirs": ((1 - self.y) * (n - third), third)}[rows]

    def what(self, kind, own_step):
        rows = {"Z": "plane", "X": "plane", "Yc": "mine", "Yo": "mine", "Sc": "plane", "So": "plane",
                "Syc": "theirs", "Syo": "theirs"}[kind]
        if kind == "Sc" and own_step:
            rows = "all"
        return rows, kind in ("Yo", "So", "Syo")

    def slot(self, kind, d):
        return self.KINDS.index(kind) * self.nz + d

    def full(self, i, shard, rows):
        first, count = self.span(i, rows)
        return self.items[i][3](shard, first, count)

    def along(self, i, d, own_step, up):
        k_from = (0 if up else self.nz * len(self.KINDS)) if own_step else self.slot("Z", d)
        to = self.z + (1 if up else -1) if own_step else self.z + jnp.where(d <= self.z, 1, -1)
        k_to = self.slot("Z", (1 if up else self.nz - 1) if own_step else d + jnp.where(d <= self.z, 1, -1))
        valid = (to >= 0) & (to < self.nz)
        to = jnp.clip(to, 0, self.nz - 1)
        shard = self.shard(self.z if own_step else self.behind(d), self.x, self.c)
        dst = self.full(i, shard, "plane")
        src = self.items[i][2](*self.span(i, "plane")) if own_step else dst
        return valid, pltpu.make_async_remote_copy(
            src_ref=src, dst_ref=dst, send_sem=self.ssem.at[i, k_from],
            recv_sem=self.rsem.at[i, jnp.clip(k_to, 0, self.nz * len(self.KINDS) - 1)],
            device_id=self.device("Z", to), device_id_type=MESHID)

    def send_z(self, i, d, own_step=False, up=None):
        valid, copy = self.along(i, d, own_step, up)

        @pl.when(valid)
        def _():
            copy.start()

    def send(self, i, kind, d, own_step=False):
        rows, other = self.what(kind, own_step)
        z = self.z if own_step else self.behind(d)
        shard = self.shard(z, 1 - self.x if other else self.x, self.c)
        dst = self.full(i, shard, rows)
        if own_step and not other:
            first, count = self.span(i, rows)
            src = self.items[i][2](first, count)
        else:
            src = dst
        k = self.slot(kind, d)
        pltpu.make_async_remote_copy(src_ref=src, dst_ref=dst, send_sem=self.ssem.at[i, k],
                                     recv_sem=self.rsem.at[i, k], device_id=self.device(kind, d),
                                     device_id_type=MESHID).start()

    def arrival(self, i, kind, d, own_step=False):
        rows, other = self.what(kind, own_step)
        if kind in ("Yc", "Yo"):
            rows = "theirs"
        z = self.z if own_step else self.behind(d)
        side = 1 - self.x if other or kind == "X" else self.x
        ref = self.full(i, self.shard(z, side, 1 - self.c if kind[0] == "S" else self.c), rows)
        k = self.slot(kind, d)
        return pltpu.make_async_remote_copy(src_ref=ref, dst_ref=ref, send_sem=self.ssem.at[i, k],
                                            recv_sem=self.rsem.at[i, k], device_id=self.device("Sc", d),
                                            device_id_type=MESHID)

    def take(self, i, kind, d, own_step=False):
        self.arrival(i, kind, d, own_step).wait_recv()

    def start_z(self, i):
        self.send_z(i, 0, True, True)
        self.send_z(i, 0, True, False)

    def start_rest(self, i):
        self.send(i, "X", 0, True)
        self.send(i, "Sc", 0, True)

    def start(self, i):
        self.start_z(i)
        self.start_rest(i)

    def pass_z(self, i, k):
        d = self.order(k)
        self.take(i, "Z", d)
        self.send_z(i, d)
        self.send(i, "X", d)
        self.send(i, "Yc", d)
        self.send(i, "Sc", d)

    def pass_x(self, i, k):
        d = self.order(k)
        self.take(i, "X", d)
        self.send(i, "Yo", d)
        self.send(i, "So", d)

    def pass_y(self, i, k, own_step=False):
        d = self.order(k)
        if not own_step:
            self.take(i, "Yc", d)
            self.send(i, "Syc", d)
        self.take(i, "Yo", d)
        self.send(i, "Syo", d)

    def ready(self, i, k, own_step=False):
        d = self.order(k)
        self.take(i, "Sc", 0 if own_step else d, own_step)
        self.take(i, "So", d)
        if not own_step:
            self.take(i, "Syc", d)
        self.take(i, "Syo", d)

    def leave(self):
        for i in range(len(self.items)):
            def done(kind, d, own_step=False):
                rows, _ = self.what(kind, own_step)
                ref = self.full(i, 0, rows)
                pltpu.make_async_remote_copy(
                    src_ref=ref, dst_ref=ref, send_sem=self.ssem.at[i, self.slot(kind, d)],
                    recv_sem=self.rsem.at[i, self.slot(kind, d)], device_id=self.device("Sc", d),
                    device_id_type=MESHID).wait_send()

            def done_z(d, own_step=False, up=None):
                valid, copy = self.along(i, d, own_step, up)

                @pl.when(valid)
                def _():
                    copy.wait_send()

            for kind in ("X", "Yo", "So", "Syo"):
                done(kind, 0)
            done("Sc", 0, True)
            done_z(0, True, True)
            done_z(0, True, False)

            @pl.loop(1, self.nz)
            def _(d):
                for kind in self.KINDS[1:]:
                    done(kind, d)
                done_z(d)


def row_slice(ref, first, count):
    return ref.at[pl.ds(pl.multiple_of(first, 16), count)]


def gather_project(tokens, pack, qkv_shard, own, nz, tile=512):
    n, d = tokens.shape
    rw = qkv_shard.shape[0]
    members = 4 * nz
    pr = pack.shape[0]

    def kernel(x_ref, p_ref, w_ref, n_ref, o_ref, full_ref, packs_ref, vec_ref, ssem, rsem, lsem):
        half = rw // 3 // 16 * 16
        spans = [(0, half), (half, rw - half)]
        items = [(pr, 16, lambda r, k: row_slice(p_ref, r, k),
                  lambda s, r, k: row_slice(packs_ref, s * pr + r, k))]
        for lo, count in spans:
            items.append((count, third_of(count),
                          lambda r, k, lo=lo: row_slice(w_ref, lo + r, k),
                          lambda s, r, k, lo=lo: row_slice(full_ref, s * rw + lo + r, k)))
        g = Gather(items, nz, ssem, rsem)
        me = g.shard(g.z, g.x, g.c)
        mine = pltpu.make_async_copy(w_ref, row_slice(full_ref, me * rw, rw), lsem.at[0])
        mine.start()
        mine_pack = pltpu.make_async_copy(p_ref, row_slice(packs_ref, me * pr, pr), lsem.at[1])
        mine_pack.start()
        g.enter()
        for i in range(len(items)):
            g.start(i)
        last = len(items)
        for t in range(last + 3):
            for lag, step in enumerate((g.pass_z, g.pass_x, g.pass_y)):
                i = t - lag
                if 0 <= i < last:
                    for e in range(0 if lag else 1, nz):
                        if lag == 2:
                            step(i, e, e == 0)
                        else:
                            step(i, e)
            if 0 <= t - 3 < last:
                for e in range(nz):
                    g.ready(t - 3, e, e == 0)
        mine.wait()
        mine_pack.wait()
        total = jnp.zeros((16, d), F32)
        row = lax.broadcasted_iota(jnp.int32, (128, d), 0)
        col = lax.broadcasted_iota(jnp.int32, (128, d), 1)
        for s in range(members):
            place = jnp.where((col == row + s * own) & (row < own), 1.0, 0.0).astype(BF16)
            total = total + nn(packs_ref[s * pr:s * pr + 16, :], place)
        vec_ref[...] = total[:8]

        @pl.loop(0, n // tile)
        def _(t):
            r = pl.ds(pl.multiple_of(t * tile, tile), tile)
            hat, _ = row_stats(x_ref[r, :].astype(F32))
            n_ref[r, :] = (hat * vec_ref[4:5, :] + vec_ref[5:6, :]).astype(BF16)

            @pl.loop(0, 3)
            def _(part):
                cols = pl.ds(pl.multiple_of(part * d, d), d)
                bias = jnp.where(part == 0, 1.0, 0.0) * vec_ref[0:1, :] + jnp.where(part == 2, 1.0, 0.0) * vec_ref[1:2, :]
                o_ref[r, cols] = (nt(n_ref[r, :], full_ref[cols, :]) + bias).astype(BF16)

        g.leave()

    vm = pl.BlockSpec(memory_space=pltpu.VMEM)
    return pl.pallas_call(
        kernel,
        out_shape=[jax.ShapeDtypeStruct((n, d), BF16), jax.ShapeDtypeStruct((n, 3 * d), BF16),
                   jax.ShapeDtypeStruct((members * rw, d), BF16), jax.ShapeDtypeStruct((members * pr, 128), BF16),
                   jax.ShapeDtypeStruct((8, d), F32)],
        in_specs=[vm] * 3, out_specs=[vm] * 5,
        scratch_shapes=[pltpu.SemaphoreType.DMA((3, 8 * nz + 1)), pltpu.SemaphoreType.DMA((3, 8 * nz)),
                        pltpu.SemaphoreType.DMA((2,))],
        compiler_params=pltpu.CompilerParams(collective_id=0, has_side_effects=True, vmem_limit_bytes=60 << 20),
        name="gather_project",
    )(tokens, pack, qkv_shard)


def gather_middle(tokens, mixed, grad_output, grad_aligned, valid_col, vecs, up_b, align_b,
                  out_shard, ffn_shard, align_shard, nz, tile=512, last_tile=256):
    n, d = tokens.shape
    members = 4 * nz
    ro, rf, ra = out_shard.shape[0], ffn_shard.shape[1], align_shard.shape[0]
    ff, al = members * rf, members * ra
    chunk = 4 * rf
    tiles = n // tile

    def kernel(x_hbm, m_hbm, go_hbm, ga_hbm, v_ref, vec_ref, ub_ref, ab_ref, so_ref, sf_ref, sa_ref,
               n_out, act_out, du_out, gb_out, out_out, al_out, r_out, rb_out, dm_out, s768_ref, sff_ref, sal_ref,
               x_ref, m_ref, go_ref, ga_ref, wo_ref, wf_ref, wa_ref, resid_ref, n_ref, grad_ref, gb_ref, branch, dn,
               act_buf, du_buf, out_buf, al_buf, r_buf, rb_buf, dm_buf, ssem, rsem, lsem, osem, csem):
        half = rf // 2
        items = [
            (ro, third_of(ro), lambda r, k: row_slice(so_ref, r, k), lambda s, r, k: row_slice(wo_ref, s * ro + r, k)),
            (ra, third_of(ra), lambda r, k: row_slice(sa_ref, r, k), lambda s, r, k: row_slice(wa_ref, s * ra + r, k))]
        for lo in (0, half):
            items.append((half, third_of(half),
                          lambda r, k, lo=lo: sf_ref.at[:, pl.ds(pl.multiple_of(lo + r, 16), k)],
                          lambda s, r, k, lo=lo: wf_ref.at[:, pl.ds(pl.multiple_of(s * rf + lo + r, 16), k)]))
        g = Gather(items, nz, ssem, rsem)
        me = g.shard(g.z, g.x, g.c)
        ins = [pltpu.make_async_copy(a, b, lsem.at[k]) for k, (a, b) in enumerate(
            [(m_hbm, m_ref), (x_hbm, x_ref), (ga_hbm, ga_ref), (go_hbm, go_ref),
             (so_ref, row_slice(wo_ref, me * ro, ro)), (sa_ref, row_slice(wa_ref, me * ra, ra)),
             (sf_ref, wf_ref.at[:, pl.ds(pl.multiple_of(me * rf, 16), rf)])])]
        for cp in ins:
            cp.start()
        g.enter()
        for i in range(len(items)):
            g.start(i)
        s768_ref[...] = jnp.zeros_like(s768_ref)
        sff_ref[...] = jnp.zeros_like(sff_ref)
        sal_ref[...] = jnp.zeros_like(sal_ref)
        branch[...] = jnp.zeros_like(branch)
        dn[...] = jnp.zeros_like(dn)
        ins[2].wait()

        @pl.loop(0, n // last_tile)
        def _(t):
            sal_ref[0:1, :] += col_sum(ga_ref[pl.ds(pl.multiple_of(t * last_tile, last_tile), last_tile), :].astype(F32))

        for e in range(1, nz):
            for i in (0, 1):
                g.pass_z(i, e)
        for e in range(nz):
            for i in (0, 1):
                g.pass_x(i, e)
        for e in range(nz):
            for i in (0, 1):
                g.pass_y(i, e, e == 0)
        for i in (2, 3):
            g.pass_x(i, 0)
        for i in (2, 3):
            g.pass_z(i, 1)
        for i in (2, 3):
            g.pass_y(i, 0, True)
        for i in (0, 1):
            for e in range(nz):
                g.ready(i, e, e == 0)
        for k in (0, 1, 3, 4, 5, 6):
            ins[k].wait()

        def rows_at(t, size):
            return pl.ds(pl.multiple_of(t * size, size), size)

        @pl.loop(0, tiles)
        def _(t):
            r = rows_at(t, tile)
            resid = x_ref[r, :].astype(F32) + nn(m_ref[r, :], wo_ref[...]) + vec_ref[2:3, :]
            resid_ref[r, :] = resid
            hat, _ = row_stats(resid)
            n_ref[r, :] = (hat * vec_ref[6:7, :] + vec_ref[7:8, :]).astype(BF16)
            grad = v_ref[r, :] * (go_ref[r, :].astype(F32) + nn(ga_ref[r, :], wa_ref[...]))
            grad_ref[r, :] = grad
            gb = grad.astype(BF16)
            gb_ref[r, :] = gb
            s768_ref[0:1, :] += col_sum(gb.astype(F32))

        early = [pltpu.make_async_copy(n_ref, n_out, osem.at[0, 0]), pltpu.make_async_copy(gb_ref, gb_out, osem.at[1, 0])]
        for cp in early:
            cp.start()

        def flush(e, t):
            slot = lax.rem(e * tiles + t, 2)
            part = pl.ds(pl.multiple_of(g.behind(g.order(e)) * chunk, chunk), chunk)
            return [pltpu.make_async_copy(act_buf.at[slot], act_out.at[rows_at(t, tile), part], csem.at[0, slot]),
                    pltpu.make_async_copy(du_buf.at[slot], du_out.at[rows_at(t, tile), part], csem.at[1, slot])]

        @pl.loop(0, nz)
        def _(e):
            for i in (2, 3):
                @pl.when(e == 0)
                def _():
                    g.ready(i, 0, True)

                @pl.when(e > 0)
                def _():
                    g.ready(i, e)

            part = pl.ds(pl.multiple_of(g.behind(g.order(e)) * chunk, chunk), chunk)

            @pl.loop(0, tiles)
            def _(t):
                r = rows_at(t, tile)
                step = e * tiles + t
                slot = lax.rem(step, 2)

                @pl.when(step >= 2)
                def _():
                    for cp in flush(e, t):
                        cp.wait()

                act, slope = gelu_parts(nt(n_ref[r, :], wf_ref[0, part, :]) + ub_ref[0:1, part])
                act_buf[slot] = act.astype(BF16)
                du = (slope * nt(gb_ref[r, :], wf_ref[1, part, :])).astype(BF16)
                du_buf[slot] = du
                sff_ref[0:1, part] += col_sum(du.astype(F32))
                branch[r, :] += nn(act_buf[slot], wf_ref[1, part, :])
                dn[r, :] += nn(du_buf[slot], wf_ref[0, part, :])
                for cp in flush(e, t):
                    cp.start()

                @pl.when((e < nz - 2) & (t == 0))
                def _():
                    for i in (2, 3):
                        g.pass_z(i, e + 2)

                @pl.when((e < nz - 1) & (t == tiles - 1))
                def _():
                    for i in (2, 3):
                        g.pass_x(i, e + 1)
                    for i in (2, 3):
                        g.pass_y(i, e + 1)

        for t in range(max(0, tiles - 2), tiles):
            for cp in flush(nz - 1, t):
                cp.wait()

        def late(t):
            slot = lax.rem(t, 2)
            return [pltpu.make_async_copy(b.at[slot], o.at[rows_at(t, last_tile)], osem.at[2 + k, slot])
                    for k, (b, o) in enumerate(((out_buf, out_out), (al_buf, al_out), (r_buf, r_out),
                                                (rb_buf, rb_out), (dm_buf, dm_out)))]

        steps = n // last_tile

        @pl.loop(0, steps)
        def _(t):
            r = rows_at(t, last_tile)
            slot = lax.rem(t, 2)

            @pl.when(t >= 2)
            def _():
                for cp in late(t):
                    cp.wait()

            resid = resid_ref[r, :]
            out = (v_ref[r, :] * (resid + branch[r, :] + vec_ref[3:4, :])).astype(BF16)
            out_buf[slot] = out
            al_buf[slot] = (nt(out, wa_ref[...]) + ab_ref[...]).astype(BF16)
            hat, rstd = row_stats(resid)
            dn2 = dn[r, :]
            res = grad_ref[r, :] + norm_back(dn2 * vec_ref[6:7, :], hat, rstd)
            r_buf[slot] = res
            rb = res.astype(BF16)
            rb_buf[slot] = rb
            dm_buf[slot] = nt(rb, wo_ref[...]).astype(BF16)
            s768_ref[1:2, :] += col_sum(rb.astype(F32))
            s768_ref[2:3, :] += col_sum(dn2 * hat)
            s768_ref[3:4, :] += col_sum(dn2)
            for cp in late(t):
                cp.start()

        for t in range(max(0, steps - 2), steps):
            for cp in late(t):
                cp.wait()
        for cp in early:
            cp.wait()
        g.leave()

    vm = pl.BlockSpec(memory_space=pltpu.VMEM)
    hbm = pl.BlockSpec(memory_space=pl.ANY)
    sds = jax.ShapeDtypeStruct
    return pl.pallas_call(
        kernel,
        out_shape=[sds((n, d), BF16), sds((n, ff), BF16), sds((n, ff), BF16), sds((n, d), BF16), sds((n, d), BF16),
                   sds((n, al), BF16), sds((n, d), F32), sds((n, d), BF16), sds((n, d), BF16),
                   sds((8, d), F32), sds((8, ff), F32), sds((8, al), F32)],
        in_specs=[hbm] * 4 + [vm] * 7,
        out_specs=[hbm] * 9 + [vm] * 3,
        scratch_shapes=[
            pltpu.VMEM((n, d), BF16), pltpu.VMEM((n, d), BF16), pltpu.VMEM((n, d), BF16), pltpu.VMEM((n, al), BF16),
            pltpu.VMEM((members * ro, d), BF16), pltpu.VMEM((2, ff, d), BF16), pltpu.VMEM((al, d), BF16),
            pltpu.VMEM((n, d), F32), pltpu.VMEM((n, d), BF16), pltpu.VMEM((n, d), F32), pltpu.VMEM((n, d), BF16),
            pltpu.VMEM((n, d), F32), pltpu.VMEM((n, d), F32),
            pltpu.VMEM((2, tile, chunk), BF16), pltpu.VMEM((2, tile, chunk), BF16),
            pltpu.VMEM((2, last_tile, d), BF16), pltpu.VMEM((2, last_tile, al), BF16),
            pltpu.VMEM((2, last_tile, d), F32), pltpu.VMEM((2, last_tile, d), BF16), pltpu.VMEM((2, last_tile, d), BF16),
            pltpu.SemaphoreType.DMA((4, 8 * nz + 1)), pltpu.SemaphoreType.DMA((4, 8 * nz)),
            pltpu.SemaphoreType.DMA((7,)), pltpu.SemaphoreType.DMA((7, 2)), pltpu.SemaphoreType.DMA((2, 2)),
        ],
        compiler_params=pltpu.CompilerParams(collective_id=2, has_side_effects=True, vmem_limit_bytes=63 << 20),
        name="gather_middle",
    )(tokens, mixed, grad_output, grad_aligned, valid_col, vecs, up_b, align_b, out_shard, ffn_shard, align_shard)


def weight_grads_reduced(pairs, pack, shard_rows, cuts, blocks, nz, collective):
    nw = len(pairs)
    lefts = [a for ls, _ in pairs for a in ls]
    rights = [r for _, r in pairs]
    n = rights[0].shape[0]
    width = rights[0].shape[1]
    max_left = max(sum(a.shape[1] for a in ls) for ls, _ in pairs)
    items = [(w, j) for w in range(nw) for j in range(width // blocks[w])]
    ni = len(items)

    def kernel(*refs):
        left_refs = refs[:len(lefts)]
        right_refs = refs[len(lefts):len(lefts) + nw]
        pos = len(lefts) + nw
        pack_ref = refs[pos]
        out_refs = refs[pos + 1:pos + 1 + nw]
        pack_out = refs[pos + 1 + nw]
        pos += 2 + nw
        lbuf, rbuf = refs[pos:pos + 2]
        part, sibb, yb, xb, zb, fin, finb = [refs[pos + 2 + k * nw:pos + 2 + (k + 1) * nw] for k in range(7)]
        pos += 2 + 7 * nw
        pbuf, ssem, rsem, psem, prsem, lsem = refs[pos:]

        y, z, x, c = coords()

        def dev(yy, zz, xx, cc):
            return (yy, zz * 4 + xx * 2 + cc)

        sib, xn, yn = dev(y, z, x, 1 - c), dev(y, z, 1 - x, c), dev(1 - y, z, x, c)
        zp = [lax.rem(z + d, nz) for d in range(nz)]
        zd = [dev(y, zp[d], x, c) for d in range(nz)]

        barrier = pltpu.get_barrier_semaphore()
        peers = [sib, xn, yn] + zd[1:]
        for p in peers:
            pl.semaphore_signal(barrier, inc=1, device_id=p, device_id_type=MESHID)

        loads = {}

        def load(w):
            at = 0
            got = []
            first = sum(len(ls) for ls, _ in pairs[:w])
            for k in range(len(pairs[w][0])):
                ref = left_refs[first + k]
                cols = ref.shape[1]
                cp = pltpu.make_async_copy(ref, lbuf.at[w % 2, :, pl.ds(at, cols)], lsem.at[w, k])
                cp.start()
                got.append(cp)
                at += cols
            cp = pltpu.make_async_copy(right_refs[w], rbuf.at[w % 2], lsem.at[w, 3])
            cp.start()
            got.append(cp)
            loads[w] = got

        started = []

        def send(i, k, src, dst, to):
            cp = pltpu.make_async_remote_copy(
                src_ref=src, dst_ref=dst, send_sem=ssem.at[i, k], recv_sem=rsem.at[i, k],
                device_id=to, device_id_type=MESHID)
            cp.start()
            started.append(cp)
            return cp

        flight = {}

        def spans(w):
            rw, a = shard_rows[w], cuts[w]
            return dict(plane=(y * a, rw - a), mine=(y * (rw - a), a), theirs=((1 - y) * (rw - a), a))

        def rows_of(w, kind):
            r0, k = spans(w)[kind]
            return pl.ds(pl.multiple_of(r0, 16), k)

        def compute(i):
            w, j = items[i]
            rw, lb = shard_rows[w], blocks[w]
            if j == 0:
                for cp in loads[w]:
                    cp.wait()
            cols = pl.ds(j * lb, lb)
            right = rbuf[w % 2, :, cols]
            for half in range(nz // 2):
                left = lbuf[w % 2, :, pl.ds(half * 8 * rw, 8 * rw)]
                g = tn(left, right).astype(BF16)
                for k in range(8):
                    part[w][j, k % 2, (k // 2) % 2, 2 * half + k // 4] = g[k * rw:(k + 1) * rw]
            if j == width // lb - 1 and w + 2 < nw:
                load(w + 2)
            flight[i, 0] = send(i, 0, part[w].at[j, 1 - c], sibb[w].at[j], sib)

        def stage_sib(i):
            w, j = items[i]
            flight[i, 0].wait_recv()
            mine = part[w].at[j, c]
            for xx in range(2):
                for zz in range(nz):
                    mine[xx, zz] = (mine[xx, zz].astype(F32) + sibb[w][j, xx, zz].astype(F32)).astype(BF16)
            flight[i, 1] = send(i, 1, mine.at[:, :, rows_of(w, "theirs")], yb[w].at[j], yn)

        def stage_y(i):
            w, j = items[i]
            flight[i, 1].wait_recv()
            mine = part[w].at[j, c]
            r = rows_of(w, "mine")
            for xx in range(2):
                for zz in range(nz):
                    mine[xx, zz, r] = (mine[xx, zz, r].astype(F32) + yb[w][j, xx, zz].astype(F32)).astype(BF16)
            flight[i, 2] = send(i, 2, mine.at[1 - x, :, rows_of(w, "plane")], xb[w].at[j], xn)

        def stage_x(i):
            w, j = items[i]
            flight[i, 2].wait_recv()
            mine = part[w].at[j, c, x]
            r = rows_of(w, "plane")
            for zz in range(nz):
                mine[zz, r] = (mine[zz, r].astype(F32) + xb[w][j, zz].astype(F32)).astype(BF16)
            for d in range(1, nz):
                flight[i, 2 + d] = send(i, 2 + d, mine.at[zp[d], r], zb[w].at[j, d - 1], zd[d])

        def stage_z(i):
            w, j = items[i]
            total = part[w][j, c, x, z, rows_of(w, "plane")].astype(F32)
            for d in range(1, nz):
                flight[i, 2 + d].wait_recv()
                total = total + zb[w][j, d - 1].astype(F32)
            fin[w][j] = total.astype(BF16)
            flight[i, 2 + nz] = send(i, 2 + nz, fin[w].at[j], finb[w].at[j], yn)

        def stage_out(i):
            w, j = items[i]
            rw, a, lb = shard_rows[w], cuts[w], blocks[w]
            cols = pl.ds(j * lb, lb)
            flight[i, 2 + nz].wait_recv()
            here, there = fin[w].at[j], finb[w].at[j]

            def at(r0, k):
                return pl.ds(pl.multiple_of(r0, 16), k)

            out_refs[w][at(y * (rw - a), a), cols] = here[at(y * (rw - 2 * a), a)].astype(F32)
            out_refs[w][at((1 - y) * (rw - a), a), cols] = there[at((1 - y) * (rw - 2 * a), a)].astype(F32)
            if rw > 2 * a:
                out_refs[w][pl.ds(a, rw - 2 * a), cols] = (
                    here[at((1 - y) * a, rw - 2 * a)].astype(F32) + there[at(y * a, rw - 2 * a)].astype(F32))

        pack_to = [sib, yn, xn, dev(y, z + 1 - 2 * lax.rem(z, 2), x, c), dev(y, lax.rem(z + 2, 4), x, c)]
        pack_cp = {}

        def pack_step(k):
            if k > 0:
                pack_cp[k - 1].wait()
                pbuf[0, k] = pbuf[0, k - 1] + pbuf[1, k - 1]
            else:
                pbuf[0, 0] = pack_ref[...]
            if k < len(pack_to):
                cp = pltpu.make_async_remote_copy(
                    src_ref=pbuf.at[0, k], dst_ref=pbuf.at[1, k], send_sem=psem.at[k], recv_sem=prsem.at[k],
                    device_id=pack_to[k], device_id_type=MESHID)
                cp.start()
                pack_cp[k] = cp
            else:
                pack_out[...] = pbuf[0, k]

        load(0)
        load(1)
        pl.semaphore_wait(barrier, len(peers))
        stages = [compute, stage_sib, stage_y, stage_x, stage_z, stage_out]
        for t in range(ni + len(stages) - 1):
            for k, stage in enumerate(stages):
                if 0 <= t - k < ni:
                    stage(t - k)
            if t <= len(pack_to):
                pack_step(t)
        for cp in started:
            cp.wait_send()

    any_spec = pl.BlockSpec(memory_space=pl.ANY)
    vm = pl.BlockSpec(memory_space=pltpu.VMEM)

    def per_weight(make):
        return [pltpu.VMEM(make(width // b, shard_rows[w], cuts[w], b), BF16) for w, b in enumerate(blocks)]

    scratch = [pltpu.VMEM((2, n, max_left), BF16), pltpu.VMEM((2, n, width), BF16)]
    scratch += per_weight(lambda j, rw, a, b: (j, 2, 2, nz, rw, b))
    scratch += per_weight(lambda j, rw, a, b: (j, 2, nz, rw, b))
    scratch += per_weight(lambda j, rw, a, b: (j, 2, nz, a, b))
    scratch += per_weight(lambda j, rw, a, b: (j, nz, rw - a, b))
    scratch += per_weight(lambda j, rw, a, b: (j, nz - 1, rw - a, b))
    scratch += per_weight(lambda j, rw, a, b: (j, rw - a, b))
    scratch += per_weight(lambda j, rw, a, b: (j, rw - a, b))
    scratch += [
        pltpu.VMEM((2, 6) + pack.shape, F32),
        pltpu.SemaphoreType.DMA((ni, 3 + nz)), pltpu.SemaphoreType.DMA((ni, 3 + nz)),
        pltpu.SemaphoreType.DMA((6,)), pltpu.SemaphoreType.DMA((6,)), pltpu.SemaphoreType.DMA((nw, 4)),
    ]
    outs = pl.pallas_call(
        kernel,
        out_shape=[jax.ShapeDtypeStruct((rw, width), F32) for rw in shard_rows]
        + [jax.ShapeDtypeStruct(pack.shape, F32)],
        in_specs=[any_spec] * (len(lefts) + nw) + [vm],
        out_specs=[vm] * (nw + 1),
        scratch_shapes=scratch,
        compiler_params=pltpu.CompilerParams(
            collective_id=collective, has_side_effects=True, vmem_limit_bytes=63 << 20),
        name="reduce_grads",
    )(*lefts, *rights, pack)
    return outs[:nw], outs[nw]


def reduce_all(pairs, pack, fast):
    if fast:
        left_rows = [sum(a.shape[1] for a in ls) for ls, _ in pairs]
        shard_rows = [r // 16 for r in left_rows]
        cuts = [max(16, (r * 5 // 16) // 16 * 16) for r in shard_rows]
        blocks = [384, 256, 256, 768, 256]
        return weight_grads_reduced(pairs, pack, shard_rows, cuts, blocks, 4, 1)
    terms = [jnp.concatenate([tn(a, r).astype(BF16) for a in ls], 0) for ls, r in pairs]
    got = [lax.psum(lax.psum_scatter(t, "fsdp", scatter_dimension=0, tiled=True), "dp").astype(F32) for t in terms]
    return got, lax.psum(pack, ("dp", "fsdp"))
def per_device(mesh_shape, *args):
    (tokens, segment_ids, padding, qkv_weight, query_bias, value_bias, out_weight, out_bias,
     first_gain, first_shift, second_gain, second_shift, up_weight, up_bias, down_weight, down_bias,
     align_weight, align_bias, grad_output, grad_aligned) = args
    n, d = tokens.shape
    small = [query_bias, value_bias, out_bias, down_bias, first_gain, first_shift, second_gain, second_shift]
    members = mesh_shape["fsdp"]
    own, ub, ab = query_bias.shape[0], up_bias.shape[0], align_bias.shape[0]
    ff, al = ub * members, ab * members
    fast = mesh_shape["dp"] == 2 and members == 16

    seg = segment_ids[0]
    pad_row = padding[0]
    keys = jnp.where(pad_row == 0, seg, -1)
    valid_col = (1.0 - pad_row.astype(F32))[:, None]
    wins = windows(seg, 256)

    if fast:
        nz = members // 4
        lines = [jnp.pad(v, (0, 128 - own)) for v in small]
        lines += [up_bias[:128], jnp.pad(up_bias[128:], (0, 256 - ub)), jnp.pad(align_bias, (0, 128 - ab))]
        pack = jnp.pad(jnp.stack(lines), ((0, 48 - len(lines)), (0, 0)))
        normed, qkv, qkv_t, packs, vecs = gather_project(tokens, pack, qkv_weight.T, own, nz)
        packs = packs.reshape(members, 48, 128)
        up_b = packs[:, 8:10].reshape(members, 256)[:, :ub].reshape(1, ff).astype(F32)
        align_b = packs[:, 10, :ab].reshape(1, al).astype(F32)
    else:
        def gathered(a):
            return lax.all_gather(a, "fsdp", axis=0, tiled=True)

        qkv_t = gathered(qkv_weight.T)
        vecs = jnp.stack([gathered(v) for v in small]).astype(F32)
        up_b = gathered(up_bias).astype(F32)[None]
        align_b = gathered(align_bias).astype(F32)[None]
        qkv_b = jnp.concatenate([vecs[0:1], jnp.zeros((1, d), F32), vecs[1:2]], 1)
        normed, qkv = project(tokens, vecs, qkv_b, qkv_t)

    mixed, lse = attend(qkv, seg[:, None], keys[None, :], wins)
    if fast:
        (n2, act, du, gb, block_out, aligned, res, rb, dm, s768, sff, sal) = gather_middle(
            tokens, mixed, grad_output, grad_aligned, valid_col, vecs, up_b, align_b, out_weight,
            jnp.stack([up_weight.T, down_weight]), align_weight.T, nz)
    else:
        (n2, act, du, gb, block_out, aligned, res, rb, dm, s768, sff, sal) = middle(
            tokens, mixed, grad_output, grad_aligned, valid_col, vecs, up_b, align_b, gathered(out_weight),
            gathered(up_weight.T), gathered(down_weight), gathered(align_weight.T))
    dq, dk, dv, bq, bv = attend_back(qkv, mixed, dm, lse, seg[None, :], keys[:, None], wins)
    grad_tokens, s1 = finish(tokens, res, dq, dk, dv, vecs, qkv_t)

    sums = jnp.concatenate(
        [bq[0:1], bv[0:1], s768[1:2], s768[0:1], s1[0:2], s768[2:4]], 0)
    pack = jnp.concatenate([sums.reshape(-1), sff[0], sal[0]]).reshape(-1, 128)
    pairs = [([grad_aligned], block_out), ([act], gb), ([du], n2), ([mixed], rb), ([dq, dk, dv], normed)]
    (g_align, g_down, g_up, g_out, g_qkv), pack = reduce_all(pairs, pack, fast)
    me = lax.axis_index("fsdp")
    pack = pack.reshape(-1)
    vec = lax.dynamic_slice(pack[:8 * d].reshape(8, d), (0, me * own), (8, own))
    g_ub = lax.dynamic_slice(pack, (8 * d + me * ub,), (ub,))
    g_ab = lax.dynamic_slice(pack, (8 * d + ff + me * ab,), (ab,))
    return (block_out, aligned, grad_tokens, g_qkv.T, vec[0], vec[1], g_out, vec[2], vec[4], vec[5], vec[6],
            vec[7], g_up.T, g_ub, g_down, vec[3], g_align.T, g_ab)


def solution(mesh):
    rows_spec = P(("dp", "fsdp"), None)
    vec, by_col, by_row = P("fsdp"), P(None, "fsdp"), P("fsdp", None)
    in_specs = (rows_spec, rows_spec, rows_spec, by_col, vec, vec, by_row, vec, vec, vec, vec, vec,
                by_col, vec, by_row, vec, by_col, vec, rows_spec, rows_spec)
    out_specs = (rows_spec, rows_spec, rows_spec, by_col, vec, vec, by_row, vec, vec, vec, vec, vec,
                 by_col, vec, by_row, vec, by_col, vec)
    return jax.shard_map(functools.partial(per_device, dict(mesh.shape)), mesh=mesh, in_specs=in_specs,
                         out_specs=out_specs, check_vma=False)
```

```python
import functools

import jax
import jax.numpy as jnp
from jax import lax
from jax.experimental import pallas as pl
from jax.experimental.pallas import tpu as pltpu
from jax.sharding import PartitionSpec as P

HEADS = 12
F32 = jnp.float32
BF16 = jnp.bfloat16
NEG = -1e30


def nn(a, b):
    return lax.dot_general(a, b, (((1,), (0,)), ((), ())), preferred_element_type=F32)


def nt(a, b):
    return lax.dot_general(a, b, (((1,), (1,)), ((), ())), preferred_element_type=F32)


def tn(a, b):
    return lax.dot_general(a, b, (((0,), (0,)), ((), ())), preferred_element_type=F32)


def col_sum(v):
    return jnp.sum(v, 0, keepdims=True)


def gelu_parts(u):
    z = jnp.abs(u) * (0.5 ** 0.5)
    ez = jnp.exp(-(z * z))
    t = 1.0 / (1.0 + 0.33 * z)
    poly = -0.13593485572044933
    for coef in (0.46271278142719047, -0.3554798541586114, 0.412577688277986, 0.044992638979585504,
                 0.2019288303128453, 0.18283654298343202, 0.18636614548593147):
        poly = poly * t + coef
    half_erfc = (0.5 * t) * poly * ez
    cdf = jnp.where(u > 0, 1.0 - half_erfc, half_erfc)
    return u * cdf, cdf + u * ez * 0.3989422804014327


def row_stats(x):
    mean = jnp.mean(x, -1, keepdims=True)
    centered = x - mean
    rstd = lax.rsqrt(jnp.mean(centered * centered, -1, keepdims=True) + 1e-05)
    return centered * rstd, rstd


def norm_back(grad_hat, hat, rstd):
    return rstd * (grad_hat - jnp.mean(grad_hat, -1, keepdims=True)
                   - hat * jnp.mean(grad_hat * hat, -1, keepdims=True))


def call(kernel, grid, ins, outs, scratch=(), name=None, prefetch=(), limit=60):
    return pl.pallas_call(
        kernel,
        grid_spec=pltpu.PrefetchScalarGridSpec(
            num_scalar_prefetch=len(prefetch), grid=grid,
            in_specs=[pl.BlockSpec(b, m, **({"pipeline_mode": pl.Buffered(1)} if once else {}))
                      for _, b, m, once in ins],
            out_specs=[pl.BlockSpec(b, m) for _, _, b, m in outs],
            scratch_shapes=list(scratch)),
        out_shape=[jax.ShapeDtypeStruct(s, d) for s, d, _, _ in outs],
        compiler_params=pltpu.CompilerParams(
            dimension_semantics=("arbitrary",) * len(grid), vmem_limit_bytes=limit << 20),
        name=name,
    )(*prefetch, *[a for a, _, _, _ in ins])


def whole(a):
    n = a.ndim
    return (a, a.shape, lambda *_: (0,) * n, True)


def rows(a, tile):
    return (a, (tile, a.shape[1]), lambda i, *_: (i, 0), False)


def rows_out(n, width, dtype, tile):
    return ((n, width), dtype, (tile, width), lambda i, *_: (i, 0))


def fixed_out(shape, dtype):
    n = len(shape)
    return (shape, dtype, shape, lambda *_: (0,) * n)


def project(tokens, vecs, qkv_bias, qkv_t, tile=256):
    n, d = tokens.shape

    def kernel(x_ref, v_ref, b_ref, w_ref, n_ref, o_ref):
        hat, _ = row_stats(x_ref[...].astype(F32))
        low = (hat * v_ref[4:5, :] + v_ref[5:6, :]).astype(BF16)
        n_ref[...] = low
        for part in range(3):
            cols = pl.ds(part * d, d)
            o_ref[:, cols] = (nt(low, w_ref[cols, :]) + b_ref[:, cols]).astype(BF16)

    return call(
        kernel, (n // tile,),
        [rows(tokens, tile), whole(vecs), whole(qkv_bias), whole(qkv_t)],
        [rows_out(n, d, BF16, tile), rows_out(n, 3 * d, BF16, tile)],
        name="project")


def pair_masks(shape):
    lane = lax.broadcasted_iota(jnp.int32, shape, 1)
    return lane < 64


def windows(seg, tile, step=256):
    n = seg.shape[0]
    first = seg[::tile]
    last = seg[tile - 1::tile]
    lo = jnp.sum(seg[None, :] < first[:, None], 1, dtype=jnp.int32) // 128 * 128
    hi = jnp.sum(seg[None, :] <= last[:, None], 1, dtype=jnp.int32)
    count = (hi - lo + step - 1) // step
    return jnp.stack([jnp.minimum(lo, n - count * step), count])


def fill_mask(mask, rows_ref, cols_ref, n, tile=256):
    @pl.when(pl.program_id(0) == 0)
    def _():
        @pl.loop(0, n // tile)
        def _(t):
            r = pl.ds(pl.multiple_of(t * tile, tile), tile)
            row_id = t * tile + lax.broadcasted_iota(jnp.int32, (tile, n), 0)
            col_id = lax.broadcasted_iota(jnp.int32, (tile, n), 1)
            keep = (rows_ref[r, :] == cols_ref[...]) | (row_id == col_id)
            mask[r, :] = jnp.where(keep, 0.0, NEG).astype(F32)


def attend(qkv, seg_col, key_row, wins, tq=256, step=256):
    n = qkv.shape[0]
    d = qkv.shape[1] // 3
    pairs = d // 128

    def kernel(win, q_ref, k_ref, v_ref, sc_ref, kr_ref, o_ref, lse_ref, mask, va, vb):
        fill_mask(mask, sc_ref, kr_ref, n)
        v = v_ref[...]
        low_half = pair_masks((n, 128))
        zero = jnp.zeros_like(v)
        va[...] = jnp.where(low_half, v, zero)
        vb[...] = jnp.where(low_half, zero, v)
        half = pair_masks((tq, 128))

        @pl.loop(0, n // tq)
        def _(t):
            r = pl.ds(pl.multiple_of(t * tq, tq), tq)
            first = pl.multiple_of(win[0, t], 128)

            for count in range(1, n // step + 1):
                @pl.when(win[1, t] == count)
                def _():
                    keys = pl.ds(first, count * step)
                    q = q_ref[r, :] * jnp.asarray(0.125, BF16)
                    qz = jnp.zeros_like(q)
                    kk = k_ref[keys, :]
                    outs, tops, sums = [], [], []
                    for qh, vh in ((jnp.where(half, q, qz), va), (jnp.where(half, qz, q), vb)):
                        s = nt(qh, kk) + mask[r, keys]
                        top = jnp.max(s, 1, keepdims=True)
                        p = jnp.exp(s - top)
                        sums.append(jnp.sum(p, 1, keepdims=True))
                        tops.append(top)
                        outs.append(nn(p.astype(BF16), vh[keys, :]))
                    (la, lb), (ma, mb) = sums, tops
                    o_ref[r, :] = ((outs[0] + outs[1]) * jnp.where(half, 1.0 / la, 1.0 / lb)).astype(BF16)
                    lse = jnp.where(half, ma + jnp.log(la), mb + jnp.log(lb)).T
                    lse_ref[0:1, r] = lse[0:1, :]
                    lse_ref[1:2, r] = lse[64:65, :]

    def block(first):
        return (qkv, (n, 128), lambda p, *_: (0, first * pairs + p), False)

    return call(
        kernel, (pairs,),
        [block(0), block(1), block(2), whole(seg_col), whole(key_row)],
        [((n, d), BF16, (n, 128), lambda p, *_: (0, p)),
         ((8 * pairs, n), F32, (8, n), lambda p, *_: (p, 0))],
        [pltpu.VMEM((n, n), F32), pltpu.VMEM((n, 128), BF16), pltpu.VMEM((n, 128), BF16)],
        name="attend", prefetch=(wins,))


def attend_back(qkv, mixed, grad_mixed, lse, seg_row, key_col, wins, tk=256, step=256):
    n = qkv.shape[0]
    d = qkv.shape[1] // 3
    pairs = d // 128

    def kernel(win, q_ref, k_ref, v_ref, o_ref, g_ref, lse_ref, sr_ref, kc_ref,
               dq_ref, dk_ref, dv_ref, bq_ref, bv_ref, mask, qa, qb, ga, gb, kt, dots, dqt):
        fill_mask(mask, kc_ref, sr_ref, n)
        half = pair_masks((n, 128))
        q = q_ref[...] * jnp.asarray(0.125, BF16)
        zero = jnp.zeros_like(q)
        qa[...] = jnp.where(half, q, zero)
        qb[...] = jnp.where(half, zero, q)
        g = g_ref[...]
        ga[...] = jnp.where(half, g, zero)
        gb[...] = jnp.where(half, zero, g)
        kt[...] = k_ref[...].astype(F32).T.astype(BF16)
        prod = (g.astype(F32) * o_ref[...].astype(F32)).T
        dots[0:1, :] = col_sum(prod[:64])
        dots[1:2, :] = col_sum(prod[64:])
        dqt[...] = jnp.zeros_like(dqt)

        @pl.loop(0, n // tk)
        def _(t):
            keys = pl.ds(pl.multiple_of(t * tk, tk), tk)
            first = pl.multiple_of(win[0, t], 128)

            for count in range(1, n // step + 1):
                @pl.when(win[1, t] == count)
                def _():
                    kk = k_ref[keys, :]
                    vv = v_ref[keys, :]
                    dk = dv = None
                    for e in range(count):
                        cols = pl.ds(pl.multiple_of(first + e * step, 128), step)
                        m = mask[keys, cols]
                        for h, (qh, gh) in enumerate(((qa, ga), (qb, gb))):
                            qq = qh[cols, :]
                            gg = gh[cols, :]
                            p = jnp.exp(nt(kk, qq) + m - lse_ref[h:h + 1, cols])
                            ds = (p * (nt(vv, gg) - dots[h:h + 1, cols])).astype(BF16)
                            pv = nn(p.astype(BF16), gg)
                            pk = nn(ds, qq)
                            dv = pv if dv is None else dv + pv
                            dk = pk if dk is None else dk + pk
                            part = pl.ds(64 * h, 64)
                            dqt[part, cols] += nn(kt[part, keys], ds)
                    dk_ref[keys, :] = dk.astype(BF16)
                    dv_ref[keys, :] = dv.astype(BF16)

        dq = (dqt[...].T * 0.125).astype(BF16)
        dq_ref[...] = dq
        bq_ref[...] = jnp.broadcast_to(col_sum(dq.astype(F32)), (8, 128))
        bv_ref[...] = jnp.broadcast_to(col_sum(dv_ref[...].astype(F32)), (8, 128))

    def block(a, first=0):
        return (a, (n, 128), lambda p, *_: (0, first * pairs + p), False)

    cols = ((n, d), BF16, (n, 128), lambda p, *_: (0, p))
    sums = ((8, d), F32, (8, 128), lambda p, *_: (0, p))
    return call(
        kernel, (pairs,),
        [block(qkv, 0), block(qkv, 1), block(qkv, 2), block(mixed), block(grad_mixed),
         (lse, (8, n), lambda p, *_: (p, 0), False), whole(seg_row), whole(key_col)],
        [cols, cols, cols, sums, sums],
        [pltpu.VMEM((n, n), F32)] + [pltpu.VMEM((n, 128), BF16)] * 4
        + [pltpu.VMEM((128, n), BF16), pltpu.VMEM((8, n), F32), pltpu.VMEM((128, n), F32)],
        name="attend_back", prefetch=(wins,))


def middle(tokens, mixed, grad_output, grad_aligned, valid_col, vecs, up_b, align_b,
           out_w, up_t, down_w, align_t, tile=512, chunk=768):
    n, d = tokens.shape
    ff, al = up_t.shape[0], align_t.shape[0]

    def kernel(x_ref, m_ref, go_ref, ga_ref, v_ref, vec_ref, ub_ref, ab_ref, wo_ref, wu_ref, wd_ref, wa_ref,
               n_ref, act_ref, du_ref, gb_ref, out_ref, al_ref, r_ref, rb_ref, dm_ref,
               s768_ref, sff_ref, sal_ref, branch, dn):
        @pl.when(pl.program_id(0) == 0)
        def _():
            s768_ref[...] = jnp.zeros_like(s768_ref)
            sff_ref[...] = jnp.zeros_like(sff_ref)
            sal_ref[...] = jnp.zeros_like(sal_ref)

        resid = x_ref[...].astype(F32) + nn(m_ref[...], wo_ref[...]) + vec_ref[2:3, :]
        hat, rstd = row_stats(resid)
        low = (hat * vec_ref[6:7, :] + vec_ref[7:8, :]).astype(BF16)
        n_ref[...] = low
        valid = v_ref[...]
        ga = ga_ref[...]
        sal_ref[0:1, :] += col_sum(ga.astype(F32))
        grad = valid * (go_ref[...].astype(F32) + nn(ga, wa_ref[...]))
        gb = grad.astype(BF16)
        gb_ref[...] = gb
        branch[...] = jnp.zeros_like(branch)
        dn[...] = jnp.zeros_like(dn)

        @pl.loop(0, ff // chunk)
        def _(t):
            part = pl.ds(pl.multiple_of(t * chunk, chunk), chunk)
            wu = wu_ref[part, :]
            wd = wd_ref[part, :]
            act, slope = gelu_parts(nt(n_ref[...], wu) + ub_ref[0:1, part])
            act = act.astype(BF16)
            act_ref[:, part] = act
            branch[...] += nn(act, wd)
            du = slope * nt(gb_ref[...], wd)
            du = du.astype(BF16)
            du_ref[:, part] = du
            sff_ref[0:1, part] += col_sum(du.astype(F32))
            dn[...] += nn(du, wu)

        out = (valid * (resid + branch[...] + vec_ref[3:4, :])).astype(BF16)
        out_ref[...] = out
        al_ref[...] = (nt(out, wa_ref[...]) + ab_ref[...]).astype(BF16)
        dn2 = dn[...]
        res = grad + norm_back(dn2 * vec_ref[6:7, :], hat, rstd)
        r_ref[...] = res
        rb = res.astype(BF16)
        rb_ref[...] = rb
        dm_ref[...] = nt(rb, wo_ref[...]).astype(BF16)
        s768_ref[0:1, :] += col_sum(gb.astype(F32))
        s768_ref[1:2, :] += col_sum(rb.astype(F32))
        s768_ref[2:3, :] += col_sum(dn2 * hat)
        s768_ref[3:4, :] += col_sum(dn2)

    r = functools.partial(rows_out, n, tile=tile)
    return call(
        kernel, (n // tile,),
        [rows(tokens, tile), rows(mixed, tile), rows(grad_output, tile), rows(grad_aligned, tile),
         rows(valid_col, tile), whole(vecs), whole(up_b), whole(align_b), whole(out_w), whole(up_t),
         whole(down_w), whole(align_t)],
        [r(d, BF16), r(ff, BF16), r(ff, BF16), r(d, BF16), r(d, BF16), r(al, BF16), r(d, F32), r(d, BF16),
         r(d, BF16), fixed_out((8, d), F32), fixed_out((8, ff), F32), fixed_out((8, al), F32)],
        [pltpu.VMEM((tile, d), F32), pltpu.VMEM((tile, d), F32)],
        name="middle")


def finish(tokens, resid_grad, dq, dk, dv, vecs, qkv_t, tile=256):
    n, d = tokens.shape

    def kernel(x_ref, r_ref, dq_ref, dk_ref, dv_ref, vec_ref, w_ref, o_ref, s_ref):
        @pl.when(pl.program_id(0) == 0)
        def _():
            s_ref[...] = jnp.zeros_like(s_ref)

        dn = nn(dq_ref[...], w_ref[0:d, :]) + nn(dk_ref[...], w_ref[d:2 * d, :]) + nn(dv_ref[...], w_ref[2 * d:, :])
        hat, rstd = row_stats(x_ref[...].astype(F32))
        o_ref[...] = (r_ref[...] + norm_back(dn * vec_ref[4:5, :], hat, rstd)).astype(BF16)
        s_ref[0:1, :] += col_sum(dn * hat)
        s_ref[1:2, :] += col_sum(dn)

    return call(
        kernel, (n // tile,),
        [rows(tokens, tile), rows(resid_grad, tile), rows(dq, tile), rows(dk, tile), rows(dv, tile),
         whole(vecs), whole(qkv_t)],
        [rows_out(n, d, BF16, tile), fixed_out((8, d), F32)],
        name="finish")
MESHID = pl.DeviceIdType.MESH


def coords():
    y = lax.axis_index("dp")
    f = lax.axis_index("fsdp")
    return y, f // 4, lax.rem(f // 2, 2), lax.rem(f, 2)


def at_rows(first, count):
    return pl.ds(pl.multiple_of(first, 16), count)


class Gather:
    def __init__(self, items, nz, ssem, rsem, lsem):
        self.items, self.nz, self.ssem, self.rsem, self.lsem = items, nz, ssem, rsem, lsem
        self.y, self.z, self.x, self.c = coords()

    def device(self, y=None, z=None, x=None, c=None):
        pick = [own if new is None else new for own, new in zip((self.y, self.z, self.x, self.c), (y, z, x, c))]
        return (pick[0], pick[1] * 4 + pick[2] * 2 + pick[3])

    def ahead(self, d):
        return lax.rem(self.z + d, self.nz)

    def enter(self):
        barrier = pltpu.get_barrier_semaphore()
        peers = [self.device(c=1 - self.c), self.device(x=1 - self.x), self.device(y=1 - self.y)]
        peers += [self.device(z=self.ahead(d)) for d in range(1, self.nz)]
        for peer in peers:
            pl.semaphore_signal(barrier, inc=1, device_id=peer, device_id_type=MESHID)
        pl.semaphore_wait(barrier, len(peers))

    def span(self, i, which):
        _, _, lo, n, third = self.items[i]
        return {"all": (lo, n), "plane": (lo + self.y * third, n - third),
                "mine": (lo + self.y * (n - third), third)}[which]

    def local(self, i):
        own, full = self.items[i][:2]
        r = at_rows(*self.span(i, "plane"))
        return pltpu.make_async_copy(own.at[r], full.at[self.z, self.x, self.c, r], self.lsem.at[i])

    def copy(self, i, k):
        own, full = self.items[i][:2]
        every = pl.ds(0, self.nz)
        if k == 0:
            ref = full.at[every, self.x, self.c, at_rows(*self.span(i, "plane"))]
            src, to = ref, self.device(x=1 - self.x)
        elif k == 1:
            ref = full.at[every, :, self.c, at_rows(*self.span(i, "mine"))]
            src, to = ref, self.device(y=1 - self.y)
        elif k == 2:
            ref = full.at[every, :, self.c, at_rows(*self.span(i, "all"))]
            src, to = ref, self.device(c=1 - self.c)
        else:
            r = at_rows(*self.span(i, "plane"))
            src, ref, to = own.at[r], full.at[self.z, self.x, self.c, r], self.device(z=self.ahead(k - 2))
        return pltpu.make_async_remote_copy(
            src_ref=src, dst_ref=ref, send_sem=self.ssem.at[i, k], recv_sem=self.rsem.at[i, k],
            device_id=to, device_id_type=MESHID)

    def start(self, i):
        self.local(i).start()
        for d in range(1, self.nz):
            self.copy(i, 2 + d).start()

    def pass_z(self, i):
        for d in range(1, self.nz):
            self.copy(i, 2 + d).wait_recv()
        self.local(i).wait()
        self.copy(i, 0).start()

    def pass_x(self, i):
        self.copy(i, 0).wait_recv()
        self.copy(i, 1).start()

    def pass_y(self, i):
        self.copy(i, 1).wait_recv()
        self.copy(i, 2).start()

    def ready(self, i):
        self.copy(i, 2).wait_recv()

    def leave(self):
        for i in range(len(self.items)):
            for k in range(2 + self.nz):
                self.copy(i, k).wait_send()

    def events(self, link, hop):
        sizes = [full.shape[-1] * n for _, full, _, n, _ in self.items]
        out = []
        z = x = y = 0.0
        for i, size in enumerate(sizes):
            t = link * size / sum(sizes)
            z += t
            x = max(x, z + hop) + t
            y = max(y, x + hop) + t
            out += [(z + hop, self.pass_z, i), (x + hop, self.pass_x, i), (y + hop, self.pass_y, i),
                    (y + 2 * hop + t / 4, self.ready, i)]
        return sorted(out, key=lambda e: (e[0], e[2]))


def gather_attend(tokens, pack, shards, seg_col, key_row, own, nz, tile=512, tq=256, link=62.0, hop=2.0,
                  start=5.0, slots=(4.8, 1.45)):
    n, d = tokens.shape
    members = 4 * nz
    pairs = d // 128
    heights = [s.shape[0] for s in shards]
    cuts = [(1 + w, lo, min(48, h - lo) if h != 64 else 64) for w, h in enumerate(heights)
            for lo in range(0, h if h != 64 else 1, 48)]
    cuts = [(0, 0, pack.shape[0])] + cuts
    first_use = 1 + len([c for c in cuts if c[0] == 1])
    ni = len(cuts)

    def kernel(x_ref, sc_ref, kr_ref, p_ref, *refs):
        owns = (p_ref,) + refs[:5]
        n_ref, qkv_ref, vec_ref, o_ref, lse_ref = refs[5:10]
        fulls = refs[10:16]
        mask, va, vb, ssem, rsem, lsem = refs[16:]
        packs_ref, w_ref = fulls[:2]
        g = Gather([(owns[w], fulls[w], lo, k, max(16, k // 3 // 16 * 16)) for w, lo, k in cuts], nz, ssem, rsem, lsem)
        g.enter()
        for i in range(ni):
            g.start(i)

        @pl.loop(0, n // tq)
        def _(t):
            r = pl.ds(pl.multiple_of(t * tq, tq), tq)
            row_id = t * tq + lax.broadcasted_iota(jnp.int32, (tq, n), 0)
            col_id = lax.broadcasted_iota(jnp.int32, (tq, n), 1)
            keep = (sc_ref[r, :] == kr_ref[...]) | (row_id == col_id)
            mask[r, :] = jnp.where(keep, 0.0, NEG).astype(F32)

        events = g.events(link, hop)
        now = start + max(t for t, f, i in events if i < first_use and f == g.ready)

        def pump(until):
            while events and start + events[0][0] <= until:
                _, f, i = events.pop(0)
                f(i)

        pump(now)
        plan = []
        for k in range(n // tile + pairs * (n // tq)):
            now += slots[0] if k < n // tile else slots[1]
            mark = len([e for e in events if start + e[0] <= now])
            plan.append(events[:mark])
            del events[:mark]
        total = jnp.zeros((16, d), F32)
        row = lax.broadcasted_iota(jnp.int32, (128, d), 0)
        col = lax.broadcasted_iota(jnp.int32, (128, d), 1)
        for s in range(members):
            place = jnp.where((col == row + s * own) & (row < own), 1.0, 0.0).astype(BF16)
            total = total + nn(packs_ref[s // 4, s // 2 % 2, s % 2, 0:16, :], place)
        vec_ref[...] = total[:8]
        part = 3 * d // 2
        gap = jnp.zeros((1, d // 2), F32)
        biases = [jnp.concatenate([vec_ref[0:1, :], gap], 1), jnp.concatenate([gap, vec_ref[1:2, :]], 1)]

        @pl.loop(0, n // tile)
        def _(t):
            r = pl.ds(pl.multiple_of(t * tile, tile), tile)
            hat, _ = row_stats(x_ref[r, :].astype(F32))
            n_ref[r, :] = (hat * vec_ref[4:5, :] + vec_ref[5:6, :]).astype(BF16)
            for k in range(2):
                w = w_ref[k * (nz // 2):(k + 1) * (nz // 2)].reshape(part, d)
                qkv_ref[r, k * part:(k + 1) * part] = (nt(n_ref[r, :], w) + biases[k]).astype(BF16)
            for k in range(n // tile):
                if plan[k]:
                    @pl.when(t == k)
                    def _():
                        for _, f, i in plan[k]:
                            f(i)

        pumped = plan[n // tile:]
        low_half = pair_masks((n, 128))
        half = pair_masks((tq, 128))
        tiles = n // tq

        @pl.loop(0, pairs)
        def _(p):
            def cols(k):
                return pl.ds(pl.multiple_of(k * d + p * 128, 128), 128)

            v = qkv_ref[:, cols(2)]
            zero = jnp.zeros_like(v)
            va[...] = jnp.where(low_half, v, zero)
            vb[...] = jnp.where(low_half, zero, v)

            @pl.loop(0, tiles)
            def _(t):
                r = pl.ds(pl.multiple_of(t * tq, tq), tq)
                q = qkv_ref[r, cols(0)] * jnp.asarray(0.125, BF16)
                qz = jnp.zeros_like(q)
                kk = qkv_ref[:, cols(1)]
                outs, tops, sums = [], [], []
                for qh, vh in ((jnp.where(half, q, qz), va), (jnp.where(half, qz, q), vb)):
                    s = nt(qh, kk) + mask[r, :]
                    top = jnp.max(s, 1, keepdims=True)
                    e = jnp.exp(s - top)
                    sums.append(jnp.sum(e, 1, keepdims=True))
                    tops.append(top)
                    outs.append(nn(e.astype(BF16), vh[...]))
                (la, lb), (ma, mb) = sums, tops
                o_ref[r, cols(0)] = ((outs[0] + outs[1]) * jnp.where(half, 1.0 / la, 1.0 / lb)).astype(BF16)
                lse = jnp.where(half, ma + jnp.log(la), mb + jnp.log(lb)).T
                lse_ref[p, 0:1, r] = lse[0:1, :]
                lse_ref[p, 1:2, r] = lse[64:65, :]
                for k, step in enumerate(pumped):
                    if step:
                        @pl.when(p * tiles + t == k)
                        def _():
                            for _, f, i in step:
                                f(i)

        for _, f, i in events:
            f(i)
        g.leave()

    vm = pl.BlockSpec(memory_space=pltpu.VMEM)
    hbm = pl.BlockSpec(memory_space=pl.ANY)
    sds = jax.ShapeDtypeStruct

    def full(h, width):
        return sds((nz, 2, 2, h, width), BF16)

    outs = pl.pallas_call(
        kernel,
        out_shape=[sds((n, d), BF16), sds((n, 3 * d), BF16), sds((8, d), F32), sds((n, d), BF16),
                   sds((pairs, 8, n), F32), full(pack.shape[0], 128)] + [full(h, d) for h in heights],
        in_specs=[vm] * 9, out_specs=[vm] * 7 + [hbm] * 4,
        scratch_shapes=[pltpu.VMEM((n, n), F32), pltpu.VMEM((n, 128), BF16), pltpu.VMEM((n, 128), BF16),
                        pltpu.SemaphoreType.DMA((ni, 2 + nz)), pltpu.SemaphoreType.DMA((ni, 2 + nz)),
                        pltpu.SemaphoreType.DMA((ni,))],
        compiler_params=pltpu.CompilerParams(collective_id=0, has_side_effects=True, vmem_limit_bytes=60 << 20),
        name="gather_attend",
    )(tokens, seg_col, key_row, pack, *shards)
    normed, qkv, vecs, mixed, lse, packs = outs[:6]
    return (normed, qkv, vecs, mixed, lse.reshape(8 * pairs, n), packs.reshape(members, -1, 128),
            [w.reshape(-1, d) for w in outs[6:]])


def weight_grads_reduced(pairs, pack, shard_rows, cuts, blocks, nz, collective):
    nw = len(pairs)
    lefts = [a for ls, _ in pairs for a in ls]
    rights = [r for _, r in pairs]
    n = rights[0].shape[0]
    width = rights[0].shape[1]
    max_left = max(sum(a.shape[1] for a in ls) for ls, _ in pairs)
    items = [(w, j) for w in range(nw) for j in range(width // blocks[w])]
    ni = len(items)

    def kernel(*refs):
        left_refs = refs[:len(lefts)]
        right_refs = refs[len(lefts):len(lefts) + nw]
        pos = len(lefts) + nw
        pack_ref = refs[pos]
        out_refs = refs[pos + 1:pos + 1 + nw]
        pack_out = refs[pos + 1 + nw]
        pos += 2 + nw
        lbuf, rbuf = refs[pos:pos + 2]
        part, sibb, yb, xb, zb, fin, finb = [refs[pos + 2 + k * nw:pos + 2 + (k + 1) * nw] for k in range(7)]
        pos += 2 + 7 * nw
        pbuf, ssem, rsem, psem, prsem, lsem = refs[pos:]

        y, z, x, c = coords()

        def dev(yy, zz, xx, cc):
            return (yy, zz * 4 + xx * 2 + cc)

        sib, xn, yn = dev(y, z, x, 1 - c), dev(y, z, 1 - x, c), dev(1 - y, z, x, c)
        zp = [lax.rem(z + d, nz) for d in range(nz)]
        zd = [dev(y, zp[d], x, c) for d in range(nz)]

        barrier = pltpu.get_barrier_semaphore()
        peers = [sib, xn, yn] + zd[1:]
        for p in peers:
            pl.semaphore_signal(barrier, inc=1, device_id=p, device_id_type=MESHID)

        loads = {}

        def load(w):
            at = 0
            got = []
            first = sum(len(ls) for ls, _ in pairs[:w])
            for k in range(len(pairs[w][0])):
                ref = left_refs[first + k]
                cols = ref.shape[1]
                cp = pltpu.make_async_copy(ref, lbuf.at[w % 2, :, pl.ds(at, cols)], lsem.at[w, k])
                cp.start()
                got.append(cp)
                at += cols
            cp = pltpu.make_async_copy(right_refs[w], rbuf.at[w % 2], lsem.at[w, 3])
            cp.start()
            got.append(cp)
            loads[w] = got

        started = []

        def send(i, k, src, dst, to):
            cp = pltpu.make_async_remote_copy(
                src_ref=src, dst_ref=dst, send_sem=ssem.at[i, k], recv_sem=rsem.at[i, k],
                device_id=to, device_id_type=MESHID)
            cp.start()
            started.append(cp)
            return cp

        flight = {}

        def spans(w):
            rw, a = shard_rows[w], cuts[w]
            return dict(plane=(y * a, rw - a), mine=(y * (rw - a), a), theirs=((1 - y) * (rw - a), a))

        def rows_of(w, kind):
            r0, k = spans(w)[kind]
            return pl.ds(pl.multiple_of(r0, 16), k)

        def compute(i):
            w, j = items[i]
            rw, lb = shard_rows[w], blocks[w]
            if j == 0:
                for cp in loads[w]:
                    cp.wait()
            cols = pl.ds(j * lb, lb)
            right = rbuf[w % 2, :, cols]
            for half in range(nz // 2):
                left = lbuf[w % 2, :, pl.ds(half * 8 * rw, 8 * rw)]
                g = tn(left, right).astype(BF16)
                for k in range(8):
                    part[w][j, k % 2, (k // 2) % 2, 2 * half + k // 4] = g[k * rw:(k + 1) * rw]
            if j == width // lb - 1 and w + 2 < nw:
                load(w + 2)
            flight[i, 0] = send(i, 0, part[w].at[j, 1 - c], sibb[w].at[j], sib)

        def stage_sib(i):
            w, j = items[i]
            flight[i, 0].wait_recv()
            mine = part[w].at[j, c]
            for xx in range(2):
                for zz in range(nz):
                    mine[xx, zz] = (mine[xx, zz].astype(F32) + sibb[w][j, xx, zz].astype(F32)).astype(BF16)
            flight[i, 1] = send(i, 1, mine.at[:, :, rows_of(w, "theirs")], yb[w].at[j], yn)

        def stage_y(i):
            w, j = items[i]
            flight[i, 1].wait_recv()
            mine = part[w].at[j, c]
            r = rows_of(w, "mine")
            for xx in range(2):
                for zz in range(nz):
                    mine[xx, zz, r] = (mine[xx, zz, r].astype(F32) + yb[w][j, xx, zz].astype(F32)).astype(BF16)
            flight[i, 2] = send(i, 2, mine.at[1 - x, :, rows_of(w, "plane")], xb[w].at[j], xn)

        def stage_x(i):
            w, j = items[i]
            flight[i, 2].wait_recv()
            mine = part[w].at[j, c, x]
            r = rows_of(w, "plane")
            for zz in range(nz):
                mine[zz, r] = (mine[zz, r].astype(F32) + xb[w][j, zz].astype(F32)).astype(BF16)
            for d in range(1, nz):
                flight[i, 2 + d] = send(i, 2 + d, mine.at[zp[d], r], zb[w].at[j, d - 1], zd[d])

        def stage_z(i):
            w, j = items[i]
            total = part[w][j, c, x, z, rows_of(w, "plane")].astype(F32)
            for d in range(1, nz):
                flight[i, 2 + d].wait_recv()
                total = total + zb[w][j, d - 1].astype(F32)
            fin[w][j] = total.astype(BF16)
            flight[i, 2 + nz] = send(i, 2 + nz, fin[w].at[j], finb[w].at[j], yn)

        def stage_out(i):
            w, j = items[i]
            rw, a, lb = shard_rows[w], cuts[w], blocks[w]
            cols = pl.ds(j * lb, lb)
            flight[i, 2 + nz].wait_recv()
            here, there = fin[w].at[j], finb[w].at[j]

            def at(r0, k):
                return pl.ds(pl.multiple_of(r0, 16), k)

            out_refs[w][at(y * (rw - a), a), cols] = here[at(y * (rw - 2 * a), a)].astype(F32)
            out_refs[w][at((1 - y) * (rw - a), a), cols] = there[at((1 - y) * (rw - 2 * a), a)].astype(F32)
            if rw > 2 * a:
                out_refs[w][pl.ds(a, rw - 2 * a), cols] = (
                    here[at((1 - y) * a, rw - 2 * a)].astype(F32) + there[at(y * a, rw - 2 * a)].astype(F32))

        pack_to = [sib, yn, xn, dev(y, z + 1 - 2 * lax.rem(z, 2), x, c), dev(y, lax.rem(z + 2, 4), x, c)]
        pack_cp = {}

        def pack_step(k):
            if k > 0:
                pack_cp[k - 1].wait()
                pbuf[0, k] = pbuf[0, k - 1] + pbuf[1, k - 1]
            else:
                pbuf[0, 0] = pack_ref[...]
            if k < len(pack_to):
                cp = pltpu.make_async_remote_copy(
                    src_ref=pbuf.at[0, k], dst_ref=pbuf.at[1, k], send_sem=psem.at[k], recv_sem=prsem.at[k],
                    device_id=pack_to[k], device_id_type=MESHID)
                cp.start()
                pack_cp[k] = cp
            else:
                pack_out[...] = pbuf[0, k]

        load(0)
        load(1)
        pl.semaphore_wait(barrier, len(peers))
        stages = [compute, stage_sib, stage_y, stage_x, stage_z, stage_out]
        for t in range(ni + len(stages) - 1):
            for k, stage in enumerate(stages):
                if 0 <= t - k < ni:
                    stage(t - k)
            if t <= len(pack_to):
                pack_step(t)
        for cp in started:
            cp.wait_send()

    any_spec = pl.BlockSpec(memory_space=pl.ANY)
    vm = pl.BlockSpec(memory_space=pltpu.VMEM)

    def per_weight(make):
        return [pltpu.VMEM(make(width // b, shard_rows[w], cuts[w], b), BF16) for w, b in enumerate(blocks)]

    scratch = [pltpu.VMEM((2, n, max_left), BF16), pltpu.VMEM((2, n, width), BF16)]
    scratch += per_weight(lambda j, rw, a, b: (j, 2, 2, nz, rw, b))
    scratch += per_weight(lambda j, rw, a, b: (j, 2, nz, rw, b))
    scratch += per_weight(lambda j, rw, a, b: (j, 2, nz, a, b))
    scratch += per_weight(lambda j, rw, a, b: (j, nz, rw - a, b))
    scratch += per_weight(lambda j, rw, a, b: (j, nz - 1, rw - a, b))
    scratch += per_weight(lambda j, rw, a, b: (j, rw - a, b))
    scratch += per_weight(lambda j, rw, a, b: (j, rw - a, b))
    scratch += [
        pltpu.VMEM((2, 6) + pack.shape, F32),
        pltpu.SemaphoreType.DMA((ni, 3 + nz)), pltpu.SemaphoreType.DMA((ni, 3 + nz)),
        pltpu.SemaphoreType.DMA((6,)), pltpu.SemaphoreType.DMA((6,)), pltpu.SemaphoreType.DMA((nw, 4)),
    ]
    outs = pl.pallas_call(
        kernel,
        out_shape=[jax.ShapeDtypeStruct((rw, width), F32) for rw in shard_rows]
        + [jax.ShapeDtypeStruct(pack.shape, F32)],
        in_specs=[any_spec] * (len(lefts) + nw) + [vm],
        out_specs=[vm] * (nw + 1),
        scratch_shapes=scratch,
        compiler_params=pltpu.CompilerParams(
            collective_id=collective, has_side_effects=True, vmem_limit_bytes=63 << 20),
        name="reduce_grads",
    )(*lefts, *rights, pack)
    return outs[:nw], outs[nw]


def reduce_all(pairs, pack, fast):
    if fast:
        left_rows = [sum(a.shape[1] for a in ls) for ls, _ in pairs]
        shard_rows = [r // 16 for r in left_rows]
        cuts = [max(16, (r * 5 // 16) // 16 * 16) for r in shard_rows]
        blocks = [384, 256, 256, 768, 256]
        return weight_grads_reduced(pairs, pack, shard_rows, cuts, blocks, 4, 1)
    terms = [jnp.concatenate([tn(a, r).astype(BF16) for a in ls], 0) for ls, r in pairs]
    got = [lax.psum(lax.psum_scatter(t, "fsdp", scatter_dimension=0, tiled=True), "dp").astype(F32) for t in terms]
    return got, lax.psum(pack, ("dp", "fsdp"))
def per_device(mesh_shape, *args):
    (tokens, segment_ids, padding, qkv_weight, query_bias, value_bias, out_weight, out_bias,
     first_gain, first_shift, second_gain, second_shift, up_weight, up_bias, down_weight, down_bias,
     align_weight, align_bias, grad_output, grad_aligned) = args
    n, d = tokens.shape
    small = [query_bias, value_bias, out_bias, down_bias, first_gain, first_shift, second_gain, second_shift]
    members = mesh_shape["fsdp"]
    own, ub, ab = query_bias.shape[0], up_bias.shape[0], align_bias.shape[0]
    ff, al = ub * members, ab * members
    fast = mesh_shape["dp"] == 2 and members == 16

    seg = segment_ids[0]
    pad_row = padding[0]
    keys = jnp.where(pad_row == 0, seg, -1)
    valid_col = (1.0 - pad_row.astype(F32))[:, None]
    wins = windows(seg, 256)

    if fast:
        nz = members // 4
        lines = [v[None] for v in small] + [up_bias[None, :128], up_bias[None, 128:], align_bias[None]]
        pack = sum(jnp.pad(v, ((k, 47 - k), (0, 128 - v.shape[1]))) for k, v in enumerate(lines))
        normed, qkv, vecs, mixed, lse, packs, full = gather_attend(
            tokens, pack, [qkv_weight.T, out_weight, align_weight.T, up_weight.T, down_weight],
            seg[:, None], keys[None, :], own, nz)
        qkv_t, out_w, align_t, up_t, down_w = full
        up_b = packs[:, 8:10].reshape(members, 256)[:, :ub].reshape(1, ff).astype(F32)
        align_b = packs[:, 10, :ab].reshape(1, al).astype(F32)
    else:
        def gathered(a):
            return lax.all_gather(a, "fsdp", axis=0, tiled=True)

        qkv_t, out_w, up_t, down_w, align_t = [
            gathered(a) for a in (qkv_weight.T, out_weight, up_weight.T, down_weight, align_weight.T)]
        vecs = jnp.stack([gathered(v) for v in small]).astype(F32)
        up_b = gathered(up_bias).astype(F32)[None]
        align_b = gathered(align_bias).astype(F32)[None]
        qkv_b = jnp.concatenate([vecs[0:1], jnp.zeros((1, d), F32), vecs[1:2]], 1)
        normed, qkv = project(tokens, vecs, qkv_b, qkv_t)
        mixed, lse = attend(qkv, seg[:, None], keys[None, :], wins)
    (n2, act, du, gb, block_out, aligned, res, rb, dm, s768, sff, sal) = middle(
        tokens, mixed, grad_output, grad_aligned, valid_col, vecs, up_b, align_b, out_w, up_t, down_w, align_t)
    dq, dk, dv, bq, bv = attend_back(qkv, mixed, dm, lse, seg[None, :], keys[:, None], wins)
    grad_tokens, s1 = finish(tokens, res, dq, dk, dv, vecs, qkv_t)

    sums = jnp.concatenate(
        [bq[0:1], bv[0:1], s768[1:2], s768[0:1], s1[0:2], s768[2:4]], 0)
    pack = jnp.concatenate([sums.reshape(-1), sff[0], sal[0]]).reshape(-1, 128)
    pairs = [([grad_aligned], block_out), ([act], gb), ([du], n2), ([mixed], rb), ([dq, dk, dv], normed)]
    (g_align, g_down, g_up, g_out, g_qkv), pack = reduce_all(pairs, pack, fast)
    me = lax.axis_index("fsdp")
    pack = pack.reshape(-1)
    vec = lax.dynamic_slice(pack[:8 * d].reshape(8, d), (0, me * own), (8, own))
    g_ub = lax.dynamic_slice(pack, (8 * d + me * ub,), (ub,))
    g_ab = lax.dynamic_slice(pack, (8 * d + ff + me * ab,), (ab,))
    return (block_out, aligned, grad_tokens, g_qkv.T, vec[0], vec[1], g_out, vec[2], vec[4], vec[5], vec[6],
            vec[7], g_up.T, g_ub, g_down, vec[3], g_align.T, g_ab)


def solution(mesh):
    rows_spec = P(("dp", "fsdp"), None)
    vec, by_col, by_row = P("fsdp"), P(None, "fsdp"), P("fsdp", None)
    in_specs = (rows_spec, rows_spec, rows_spec, by_col, vec, vec, by_row, vec, vec, vec, vec, vec,
                by_col, vec, by_row, vec, by_col, vec, rows_spec, rows_spec)
    out_specs = (rows_spec, rows_spec, rows_spec, by_col, vec, vec, by_row, vec, vec, vec, vec, vec,
                 by_col, vec, by_row, vec, by_col, vec)
    return jax.shard_map(functools.partial(per_device, dict(mesh.shape)), mesh=mesh, in_specs=in_specs,
                         out_specs=out_specs, check_vma=False)
```

```python
import functools

import jax
import jax.numpy as jnp
from jax import lax
from jax.experimental import pallas as pl
from jax.experimental.pallas import tpu as pltpu
from jax.sharding import PartitionSpec as P

HEADS = 12
F32 = jnp.float32
BF16 = jnp.bfloat16
NEG = -1e30


def nn(a, b):
    return lax.dot_general(a, b, (((1,), (0,)), ((), ())), preferred_element_type=F32)


def nt(a, b):
    return lax.dot_general(a, b, (((1,), (1,)), ((), ())), preferred_element_type=F32)


def tn(a, b):
    return lax.dot_general(a, b, (((0,), (0,)), ((), ())), preferred_element_type=F32)


def col_sum(v):
    return jnp.sum(v, 0, keepdims=True)


def gelu_parts(u):
    z = jnp.abs(u) * (0.5 ** 0.5)
    ez = jnp.exp(-(z * z))
    t = 1.0 / (1.0 + 0.33 * z)
    poly = -0.13593485572044933
    for coef in (0.46271278142719047, -0.3554798541586114, 0.412577688277986, 0.044992638979585504,
                 0.2019288303128453, 0.18283654298343202, 0.18636614548593147):
        poly = poly * t + coef
    half_erfc = (0.5 * t) * poly * ez
    cdf = jnp.where(u > 0, 1.0 - half_erfc, half_erfc)
    return u * cdf, cdf + u * ez * 0.3989422804014327


def row_stats(x):
    mean = jnp.mean(x, -1, keepdims=True)
    centered = x - mean
    rstd = lax.rsqrt(jnp.mean(centered * centered, -1, keepdims=True) + 1e-05)
    return centered * rstd, rstd


def norm_back(grad_hat, hat, rstd):
    return rstd * (grad_hat - jnp.mean(grad_hat, -1, keepdims=True)
                   - hat * jnp.mean(grad_hat * hat, -1, keepdims=True))


def call(kernel, grid, ins, outs, scratch=(), name=None, prefetch=(), limit=60):
    return pl.pallas_call(
        kernel,
        grid_spec=pltpu.PrefetchScalarGridSpec(
            num_scalar_prefetch=len(prefetch), grid=grid,
            in_specs=[pl.BlockSpec(b, m, **({"pipeline_mode": pl.Buffered(1)} if once else {}))
                      for _, b, m, once in ins],
            out_specs=[pl.BlockSpec(b, m) for _, _, b, m in outs],
            scratch_shapes=list(scratch)),
        out_shape=[jax.ShapeDtypeStruct(s, d) for s, d, _, _ in outs],
        compiler_params=pltpu.CompilerParams(
            dimension_semantics=("arbitrary",) * len(grid), vmem_limit_bytes=limit << 20),
        name=name,
    )(*prefetch, *[a for a, _, _, _ in ins])


def whole(a):
    n = a.ndim
    return (a, a.shape, lambda *_: (0,) * n, True)


def rows(a, tile):
    return (a, (tile, a.shape[1]), lambda i, *_: (i, 0), False)


def rows_out(n, width, dtype, tile):
    return ((n, width), dtype, (tile, width), lambda i, *_: (i, 0))


def fixed_out(shape, dtype):
    n = len(shape)
    return (shape, dtype, shape, lambda *_: (0,) * n)


def project(tokens, vecs, qkv_bias, qkv_t, tile=256):
    n, d = tokens.shape

    def kernel(x_ref, v_ref, b_ref, w_ref, n_ref, o_ref):
        hat, _ = row_stats(x_ref[...].astype(F32))
        low = (hat * v_ref[4:5, :] + v_ref[5:6, :]).astype(BF16)
        n_ref[...] = low
        for part in range(3):
            cols = pl.ds(part * d, d)
            o_ref[:, cols] = (nt(low, w_ref[cols, :]) + b_ref[:, cols]).astype(BF16)

    return call(
        kernel, (n // tile,),
        [rows(tokens, tile), whole(vecs), whole(qkv_bias), whole(qkv_t)],
        [rows_out(n, d, BF16, tile), rows_out(n, 3 * d, BF16, tile)],
        name="project")


def pair_masks(shape):
    lane = lax.broadcasted_iota(jnp.int32, shape, 1)
    return lane < 64


def windows(seg, tile, step=256):
    n = seg.shape[0]
    first = seg[::tile]
    last = seg[tile - 1::tile]
    lo = jnp.sum(seg[None, :] < first[:, None], 1, dtype=jnp.int32) // 128 * 128
    hi = jnp.sum(seg[None, :] <= last[:, None], 1, dtype=jnp.int32)
    count = (hi - lo + step - 1) // step
    return jnp.stack([jnp.minimum(lo, n - count * step), count])


def fill_mask(mask, rows_ref, cols_ref, n, tile=256):
    @pl.when(pl.program_id(0) == 0)
    def _():
        @pl.loop(0, n // tile)
        def _(t):
            r = pl.ds(pl.multiple_of(t * tile, tile), tile)
            row_id = t * tile + lax.broadcasted_iota(jnp.int32, (tile, n), 0)
            col_id = lax.broadcasted_iota(jnp.int32, (tile, n), 1)
            keep = (rows_ref[r, :] == cols_ref[...]) | (row_id == col_id)
            mask[r, :] = jnp.where(keep, 0.0, NEG).astype(F32)


def attend(qkv, seg_col, key_row, wins, tq=256, step=256):
    n = qkv.shape[0]
    d = qkv.shape[1] // 3
    pairs = d // 128

    def kernel(win, q_ref, k_ref, v_ref, sc_ref, kr_ref, o_ref, lse_ref, mask, va, vb):
        fill_mask(mask, sc_ref, kr_ref, n)
        v = v_ref[...]
        low_half = pair_masks((n, 128))
        zero = jnp.zeros_like(v)
        va[...] = jnp.where(low_half, v, zero)
        vb[...] = jnp.where(low_half, zero, v)
        half = pair_masks((tq, 128))

        @pl.loop(0, n // tq)
        def _(t):
            r = pl.ds(pl.multiple_of(t * tq, tq), tq)
            first = pl.multiple_of(win[0, t], 128)

            for count in range(1, n // step + 1):
                @pl.when(win[1, t] == count)
                def _():
                    keys = pl.ds(first, count * step)
                    q = q_ref[r, :] * jnp.asarray(0.125, BF16)
                    qz = jnp.zeros_like(q)
                    kk = k_ref[keys, :]
                    outs, tops, sums = [], [], []
                    for qh, vh in ((jnp.where(half, q, qz), va), (jnp.where(half, qz, q), vb)):
                        s = nt(qh, kk) + mask[r, keys]
                        top = jnp.max(s, 1, keepdims=True)
                        p = jnp.exp(s - top)
                        sums.append(jnp.sum(p, 1, keepdims=True))
                        tops.append(top)
                        outs.append(nn(p.astype(BF16), vh[keys, :]))
                    (la, lb), (ma, mb) = sums, tops
                    o_ref[r, :] = ((outs[0] + outs[1]) * jnp.where(half, 1.0 / la, 1.0 / lb)).astype(BF16)
                    lse = jnp.where(half, ma + jnp.log(la), mb + jnp.log(lb)).T
                    lse_ref[0:1, r] = lse[0:1, :]
                    lse_ref[1:2, r] = lse[64:65, :]

    def block(first):
        return (qkv, (n, 128), lambda p, *_: (0, first * pairs + p), False)

    return call(
        kernel, (pairs,),
        [block(0), block(1), block(2), whole(seg_col), whole(key_row)],
        [((n, d), BF16, (n, 128), lambda p, *_: (0, p)),
         ((8 * pairs, n), F32, (8, n), lambda p, *_: (p, 0))],
        [pltpu.VMEM((n, n), F32), pltpu.VMEM((n, 128), BF16), pltpu.VMEM((n, 128), BF16)],
        name="attend", prefetch=(wins,))


def attend_back(qkv, mixed, grad_mixed, lse, seg_row, key_col, wins, tk=256, step=256):
    n = qkv.shape[0]
    d = qkv.shape[1] // 3
    pairs = d // 128

    def kernel(win, q_ref, k_ref, v_ref, o_ref, g_ref, lse_ref, sr_ref, kc_ref,
               dq_ref, dk_ref, dv_ref, bq_ref, bv_ref, mask, qa, qb, ga, gb, kt, dots, dqt):
        fill_mask(mask, kc_ref, sr_ref, n)
        half = pair_masks((n, 128))
        q = q_ref[...] * jnp.asarray(0.125, BF16)
        zero = jnp.zeros_like(q)
        qa[...] = jnp.where(half, q, zero)
        qb[...] = jnp.where(half, zero, q)
        g = g_ref[...]
        ga[...] = jnp.where(half, g, zero)
        gb[...] = jnp.where(half, zero, g)
        kt[...] = k_ref[...].astype(F32).T.astype(BF16)
        prod = (g.astype(F32) * o_ref[...].astype(F32)).T
        dots[0:1, :] = col_sum(prod[:64])
        dots[1:2, :] = col_sum(prod[64:])
        dqt[...] = jnp.zeros_like(dqt)

        @pl.loop(0, n // tk)
        def _(t):
            keys = pl.ds(pl.multiple_of(t * tk, tk), tk)
            first = pl.multiple_of(win[0, t], 128)

            for count in range(1, n // step + 1):
                @pl.when(win[1, t] == count)
                def _():
                    kk = k_ref[keys, :]
                    vv = v_ref[keys, :]
                    dk = dv = None
                    for e in range(count):
                        cols = pl.ds(pl.multiple_of(first + e * step, 128), step)
                        m = mask[keys, cols]
                        for h, (qh, gh) in enumerate(((qa, ga), (qb, gb))):
                            qq = qh[cols, :]
                            gg = gh[cols, :]
                            p = jnp.exp(nt(kk, qq) + m - lse_ref[h:h + 1, cols])
                            ds = (p * (nt(vv, gg) - dots[h:h + 1, cols])).astype(BF16)
                            pv = nn(p.astype(BF16), gg)
                            pk = nn(ds, qq)
                            dv = pv if dv is None else dv + pv
                            dk = pk if dk is None else dk + pk
                            part = pl.ds(64 * h, 64)
                            dqt[part, cols] += nn(kt[part, keys], ds)
                    dk_ref[keys, :] = dk.astype(BF16)
                    dv_ref[keys, :] = dv.astype(BF16)

        dq = (dqt[...].T * 0.125).astype(BF16)
        dq_ref[...] = dq
        bq_ref[...] = jnp.broadcast_to(col_sum(dq.astype(F32)), (8, 128))
        bv_ref[...] = jnp.broadcast_to(col_sum(dv_ref[...].astype(F32)), (8, 128))

    def block(a, first=0):
        return (a, (n, 128), lambda p, *_: (0, first * pairs + p), False)

    cols = ((n, d), BF16, (n, 128), lambda p, *_: (0, p))
    sums = ((8, d), F32, (8, 128), lambda p, *_: (0, p))
    return call(
        kernel, (pairs,),
        [block(qkv, 0), block(qkv, 1), block(qkv, 2), block(mixed), block(grad_mixed),
         (lse, (8, n), lambda p, *_: (p, 0), False), whole(seg_row), whole(key_col)],
        [cols, cols, cols, sums, sums],
        [pltpu.VMEM((n, n), F32)] + [pltpu.VMEM((n, 128), BF16)] * 4
        + [pltpu.VMEM((128, n), BF16), pltpu.VMEM((8, n), F32), pltpu.VMEM((128, n), F32)],
        name="attend_back", prefetch=(wins,))


def middle(tokens, mixed, grad_output, grad_aligned, valid_col, vecs, up_b, align_b,
           out_w, up_t, down_w, align_t, tile=256, chunk=768):
    n, d = tokens.shape
    ff, al = up_t.shape[0], align_t.shape[0]

    def kernel(x_ref, m_ref, go_ref, ga_ref, v_ref, vec_ref, ub_ref, ab_ref, wo_ref, wu_ref, wd_ref, wa_ref,
               n_ref, act_ref, du_ref, gb_ref, out_ref, al_ref, r_ref, rb_ref, dm_ref,
               s768_ref, sff_ref, sal_ref, branch, dn):
        @pl.when(pl.program_id(0) == 0)
        def _():
            s768_ref[...] = jnp.zeros_like(s768_ref)
            sff_ref[...] = jnp.zeros_like(sff_ref)
            sal_ref[...] = jnp.zeros_like(sal_ref)

        resid = x_ref[...].astype(F32) + nn(m_ref[...], wo_ref[...]) + vec_ref[2:3, :]
        hat, rstd = row_stats(resid)
        low = (hat * vec_ref[6:7, :] + vec_ref[7:8, :]).astype(BF16)
        n_ref[...] = low
        valid = v_ref[...]
        ga = ga_ref[...]
        sal_ref[0:1, :] += col_sum(ga.astype(F32))
        grad = valid * (go_ref[...].astype(F32) + nn(ga, wa_ref[...]))
        gb = grad.astype(BF16)
        gb_ref[...] = gb
        branch[...] = jnp.zeros_like(branch)
        dn[...] = jnp.zeros_like(dn)

        @pl.loop(0, ff // chunk)
        def _(t):
            part = pl.ds(pl.multiple_of(t * chunk, chunk), chunk)
            wu = wu_ref[part, :]
            wd = wd_ref[part, :]
            act, slope = gelu_parts(nt(n_ref[...], wu) + ub_ref[0:1, part])
            act = act.astype(BF16)
            act_ref[:, part] = act
            branch[...] += nn(act, wd)
            du = slope * nt(gb_ref[...], wd)
            du = du.astype(BF16)
            du_ref[:, part] = du
            sff_ref[0:1, part] += col_sum(du.astype(F32))
            dn[...] += nn(du, wu)

        out = (valid * (resid + branch[...] + vec_ref[3:4, :])).astype(BF16)
        out_ref[...] = out
        al_ref[...] = (nt(out, wa_ref[...]) + ab_ref[...]).astype(BF16)
        dn2 = dn[...]
        res = grad + norm_back(dn2 * vec_ref[6:7, :], hat, rstd)
        r_ref[...] = res
        rb = res.astype(BF16)
        rb_ref[...] = rb
        dm_ref[...] = nt(rb, wo_ref[...]).astype(BF16)
        s768_ref[0:1, :] += col_sum(gb.astype(F32))
        s768_ref[1:2, :] += col_sum(rb.astype(F32))
        s768_ref[2:3, :] += col_sum(dn2 * hat)
        s768_ref[3:4, :] += col_sum(dn2)

    r = functools.partial(rows_out, n, tile=tile)
    return call(
        kernel, (n // tile,),
        [rows(tokens, tile), rows(mixed, tile), rows(grad_output, tile), rows(grad_aligned, tile),
         rows(valid_col, tile), whole(vecs), whole(up_b), whole(align_b), whole(out_w), whole(up_t),
         whole(down_w), whole(align_t)],
        [r(d, BF16), r(ff, BF16), r(ff, BF16), r(d, BF16), r(d, BF16), r(al, BF16), r(d, F32), r(d, BF16),
         r(d, BF16), fixed_out((8, d), F32), fixed_out((8, ff), F32), fixed_out((8, al), F32)],
        [pltpu.VMEM((tile, d), F32), pltpu.VMEM((tile, d), F32)],
        name="middle")


def finish(tokens, resid_grad, dq, dk, dv, vecs, qkv_t, tile=256):
    n, d = tokens.shape

    def kernel(x_ref, r_ref, dq_ref, dk_ref, dv_ref, vec_ref, w_ref, o_ref, s_ref):
        @pl.when(pl.program_id(0) == 0)
        def _():
            s_ref[...] = jnp.zeros_like(s_ref)

        dn = nn(dq_ref[...], w_ref[0:d, :]) + nn(dk_ref[...], w_ref[d:2 * d, :]) + nn(dv_ref[...], w_ref[2 * d:, :])
        hat, rstd = row_stats(x_ref[...].astype(F32))
        o_ref[...] = (r_ref[...] + norm_back(dn * vec_ref[4:5, :], hat, rstd)).astype(BF16)
        s_ref[0:1, :] += col_sum(dn * hat)
        s_ref[1:2, :] += col_sum(dn)

    return call(
        kernel, (n // tile,),
        [rows(tokens, tile), rows(resid_grad, tile), rows(dq, tile), rows(dk, tile), rows(dv, tile),
         whole(vecs), whole(qkv_t)],
        [rows_out(n, d, BF16, tile), fixed_out((8, d), F32)],
        name="finish")
MESHID = pl.DeviceIdType.MESH


def coords():
    y = lax.axis_index("dp")
    f = lax.axis_index("fsdp")
    return y, f // 4, lax.rem(f // 2, 2), lax.rem(f, 2)


def at_rows(first, count):
    return pl.ds(pl.multiple_of(first, 16), count)


class Gather:
    def __init__(self, items, nz, ssem, rsem, lsem):
        self.items, self.nz, self.ssem, self.rsem, self.lsem = items, nz, ssem, rsem, lsem
        self.y, self.z, self.x, self.c = coords()

    def device(self, y=None, z=None, x=None, c=None):
        pick = [own if new is None else new for own, new in zip((self.y, self.z, self.x, self.c), (y, z, x, c))]
        return (pick[0], pick[1] * 4 + pick[2] * 2 + pick[3])

    def ahead(self, d):
        return lax.rem(self.z + d, self.nz)

    def enter(self):
        barrier = pltpu.get_barrier_semaphore()
        peers = [self.device(c=1 - self.c), self.device(x=1 - self.x), self.device(y=1 - self.y)]
        peers += [self.device(z=self.ahead(d)) for d in range(1, self.nz)]
        for peer in peers:
            pl.semaphore_signal(barrier, inc=1, device_id=peer, device_id_type=MESHID)
        pl.semaphore_wait(barrier, len(peers))

    def span(self, i, which):
        _, _, lo, n, third = self.items[i]
        return {"all": (lo, n), "plane": (lo + self.y * third, n - third),
                "mine": (lo + self.y * (n - third), third)}[which]

    def local(self, i):
        own, full = self.items[i][:2]
        r = at_rows(*self.span(i, "plane"))
        return pltpu.make_async_copy(own.at[r], full.at[self.z, self.x, self.c, r], self.lsem.at[i])

    def copy(self, i, k):
        own, full = self.items[i][:2]
        every = pl.ds(0, self.nz)
        if k == 0:
            ref = full.at[every, self.x, self.c, at_rows(*self.span(i, "plane"))]
            src, to = ref, self.device(x=1 - self.x)
        elif k == 1:
            ref = full.at[every, :, self.c, at_rows(*self.span(i, "mine"))]
            src, to = ref, self.device(y=1 - self.y)
        elif k == 2:
            ref = full.at[every, :, self.c, at_rows(*self.span(i, "all"))]
            src, to = ref, self.device(c=1 - self.c)
        else:
            r = at_rows(*self.span(i, "plane"))
            src, ref, to = own.at[r], full.at[self.z, self.x, self.c, r], self.device(z=self.ahead(k - 2))
        return pltpu.make_async_remote_copy(
            src_ref=src, dst_ref=ref, send_sem=self.ssem.at[i, k], recv_sem=self.rsem.at[i, k],
            device_id=to, device_id_type=MESHID)

    def start(self, i):
        self.local(i).start()
        for d in range(1, self.nz):
            self.copy(i, 2 + d).start()

    def pass_z(self, i):
        for d in range(1, self.nz):
            self.copy(i, 2 + d).wait_recv()
        self.local(i).wait()
        self.copy(i, 0).start()

    def pass_x(self, i):
        self.copy(i, 0).wait_recv()
        self.copy(i, 1).start()

    def pass_y(self, i):
        self.copy(i, 1).wait_recv()
        self.copy(i, 2).start()

    def ready(self, i):
        self.copy(i, 2).wait_recv()

    def leave(self):
        for i in range(len(self.items)):
            for k in range(2 + self.nz):
                self.copy(i, k).wait_send()

    def events(self, link, hop):
        sizes = [full.shape[-1] * n for _, full, _, n, _ in self.items]
        out = []
        z = x = y = 0.0
        for i, size in enumerate(sizes):
            t = link * size / sum(sizes)
            z += t
            x = max(x, z + hop) + t
            y = max(y, x + hop) + t
            out += [(z + hop, self.pass_z, i), (x + hop, self.pass_x, i), (y + hop, self.pass_y, i),
                    (y + 2 * hop + t / 4, self.ready, i)]
        return sorted(out, key=lambda e: (e[0], e[2]))


def gather_attend(tokens, pack, shards, seg_col, key_row, own, nz, tile=512, tq=256, link=62.0, hop=2.0,
                  start=5.0, slots=(4.8, 1.45)):
    n, d = tokens.shape
    members = 4 * nz
    pairs = d // 128
    heights = [s.shape[0] for s in shards]
    cuts = [(1 + w, lo, min(48, h - lo) if h != 64 else 64) for w, h in enumerate(heights)
            for lo in range(0, h if h != 64 else 1, 48)]
    cuts = [(0, 0, pack.shape[0])] + cuts
    first_use = 1 + len([c for c in cuts if c[0] == 1])
    ni = len(cuts)

    def kernel(x_ref, sc_ref, kr_ref, p_ref, *refs):
        owns = (p_ref,) + refs[:5]
        n_ref, qkv_ref, vec_ref, o_ref, lse_ref = refs[5:10]
        fulls = refs[10:16]
        mask, va, vb, ssem, rsem, lsem = refs[16:]
        packs_ref, w_ref = fulls[:2]
        g = Gather([(owns[w], fulls[w], lo, k, max(16, k // 3 // 16 * 16)) for w, lo, k in cuts], nz, ssem, rsem, lsem)
        g.enter()
        for i in range(ni):
            g.start(i)

        @pl.loop(0, n // tq)
        def _(t):
            r = pl.ds(pl.multiple_of(t * tq, tq), tq)
            row_id = t * tq + lax.broadcasted_iota(jnp.int32, (tq, n), 0)
            col_id = lax.broadcasted_iota(jnp.int32, (tq, n), 1)
            keep = (sc_ref[r, :] == kr_ref[...]) | (row_id == col_id)
            mask[r, :] = jnp.where(keep, 0.0, NEG).astype(F32)

        events = g.events(link, hop)
        now = start + max(t for t, f, i in events if i < first_use and f == g.ready)

        def pump(until):
            while events and start + events[0][0] <= until:
                _, f, i = events.pop(0)
                f(i)

        pump(now)
        plan = []
        for k in range(n // tile + pairs * (n // tq)):
            now += slots[0] if k < n // tile else slots[1]
            mark = len([e for e in events if start + e[0] <= now])
            plan.append(events[:mark])
            del events[:mark]
        total = jnp.zeros((16, d), F32)
        row = lax.broadcasted_iota(jnp.int32, (128, d), 0)
        col = lax.broadcasted_iota(jnp.int32, (128, d), 1)
        for s in range(members):
            place = jnp.where((col == row + s * own) & (row < own), 1.0, 0.0).astype(BF16)
            total = total + nn(packs_ref[s // 4, s // 2 % 2, s % 2, 0:16, :], place)
        vec_ref[...] = total[:8]
        part = 3 * d // 2
        gap = jnp.zeros((1, d // 2), F32)
        biases = [jnp.concatenate([vec_ref[0:1, :], gap], 1), jnp.concatenate([gap, vec_ref[1:2, :]], 1)]

        @pl.loop(0, n // tile)
        def _(t):
            r = pl.ds(pl.multiple_of(t * tile, tile), tile)
            hat, _ = row_stats(x_ref[r, :].astype(F32))
            n_ref[r, :] = (hat * vec_ref[4:5, :] + vec_ref[5:6, :]).astype(BF16)
            for k in range(2):
                w = w_ref[k * (nz // 2):(k + 1) * (nz // 2)].reshape(part, d)
                qkv_ref[r, k * part:(k + 1) * part] = (nt(n_ref[r, :], w) + biases[k]).astype(BF16)
            for k in range(n // tile):
                if plan[k]:
                    @pl.when(t == k)
                    def _():
                        for _, f, i in plan[k]:
                            f(i)

        pumped = plan[n // tile:]
        low_half = pair_masks((n, 128))
        half = pair_masks((tq, 128))
        tiles = n // tq

        @pl.loop(0, pairs)
        def _(p):
            def cols(k):
                return pl.ds(pl.multiple_of(k * d + p * 128, 128), 128)

            v = qkv_ref[:, cols(2)]
            zero = jnp.zeros_like(v)
            va[...] = jnp.where(low_half, v, zero)
            vb[...] = jnp.where(low_half, zero, v)

            @pl.loop(0, tiles)
            def _(t):
                r = pl.ds(pl.multiple_of(t * tq, tq), tq)
                q = qkv_ref[r, cols(0)] * jnp.asarray(0.125, BF16)
                qz = jnp.zeros_like(q)
                kk = qkv_ref[:, cols(1)]
                outs, tops, sums = [], [], []
                for qh, vh in ((jnp.where(half, q, qz), va), (jnp.where(half, qz, q), vb)):
                    s = nt(qh, kk) + mask[r, :]
                    top = jnp.max(s, 1, keepdims=True)
                    e = jnp.exp(s - top)
                    sums.append(jnp.sum(e, 1, keepdims=True))
                    tops.append(top)
                    outs.append(nn(e.astype(BF16), vh[...]))
                (la, lb), (ma, mb) = sums, tops
                o_ref[r, cols(0)] = ((outs[0] + outs[1]) * jnp.where(half, 1.0 / la, 1.0 / lb)).astype(BF16)
                lse = jnp.where(half, ma + jnp.log(la), mb + jnp.log(lb)).T
                lse_ref[p, 0:1, r] = lse[0:1, :]
                lse_ref[p, 1:2, r] = lse[64:65, :]
                for k, step in enumerate(pumped):
                    if step:
                        @pl.when(p * tiles + t == k)
                        def _():
                            for _, f, i in step:
                                f(i)

        for _, f, i in events:
            f(i)
        g.leave()

    vm = pl.BlockSpec(memory_space=pltpu.VMEM)
    hbm = pl.BlockSpec(memory_space=pl.ANY)
    sds = jax.ShapeDtypeStruct

    def full(h, width):
        return sds((nz, 2, 2, h, width), BF16)

    outs = pl.pallas_call(
        kernel,
        out_shape=[sds((n, d), BF16), sds((n, 3 * d), BF16), sds((8, d), F32), sds((n, d), BF16),
                   sds((pairs, 8, n), F32), full(pack.shape[0], 128)] + [full(h, d) for h in heights],
        in_specs=[vm] * 9, out_specs=[vm] * 7 + [hbm] * 4,
        scratch_shapes=[pltpu.VMEM((n, n), F32), pltpu.VMEM((n, 128), BF16), pltpu.VMEM((n, 128), BF16),
                        pltpu.SemaphoreType.DMA((ni, 2 + nz)), pltpu.SemaphoreType.DMA((ni, 2 + nz)),
                        pltpu.SemaphoreType.DMA((ni,))],
        compiler_params=pltpu.CompilerParams(collective_id=0, has_side_effects=True, vmem_limit_bytes=60 << 20),
        name="gather_attend",
    )(tokens, seg_col, key_row, pack, *shards)
    normed, qkv, vecs, mixed, lse, packs = outs[:6]
    return (normed, qkv, vecs, mixed, lse.reshape(8 * pairs, n), packs.reshape(members, -1, 128),
            [w.reshape(-1, d) for w in outs[6:]])


def finish_and_reduce(pairs, tokens, resid_grad, vecs, qkv_t, sums, shard_rows, cuts, blocks, nz, collective, tile=256):
    nw = len(pairs)
    lefts = [a for ls, _ in pairs for a in ls]
    rights = [r for _, r in pairs]
    n = rights[0].shape[0]
    width = rights[0].shape[1]
    max_left = max(sum(a.shape[1] for a in ls) for ls, _ in pairs)
    items = [(w, j) for w in range(nw) for j in range(width // blocks[w])]
    ni = len(items)

    def kernel(*refs):
        left_refs = refs[:len(lefts)]
        right_refs = refs[len(lefts):len(lefts) + nw]
        pos = len(lefts) + nw
        x_hbm, r_hbm, w_hbm, vec_ref = refs[pos:pos + 4]
        sum_refs = refs[pos + 4:pos + 9]
        pos += 9
        out_refs = refs[pos:pos + nw]
        pack_out, g_hbm = refs[pos + nw:pos + nw + 2]
        pos += 2 + nw
        x_ref, r_ref, w_ref, s1_ref, fsem = refs[pos:pos + 5]
        pos += 5
        lbuf, rbuf = refs[pos:pos + 2]
        part, sibb, yb, xb, zb, fin, finb = [refs[pos + 2 + k * nw:pos + 2 + (k + 1) * nw] for k in range(7)]
        pos += 2 + 7 * nw
        pbuf, ssem, rsem, psem, prsem, lsem = refs[pos:]

        y, z, x, c = coords()

        def dev(yy, zz, xx, cc):
            return (yy, zz * 4 + xx * 2 + cc)

        sib, xn, yn = dev(y, z, x, 1 - c), dev(y, z, 1 - x, c), dev(1 - y, z, x, c)
        zp = [lax.rem(z + d, nz) for d in range(nz)]
        zd = [dev(y, zp[d], x, c) for d in range(nz)]

        barrier = pltpu.get_barrier_semaphore()
        peers = [sib, xn, yn] + zd[1:]
        for p in peers:
            pl.semaphore_signal(barrier, inc=1, device_id=p, device_id_type=MESHID)

        loads = {}

        def load(w):
            at = 0
            got = []
            first = sum(len(ls) for ls, _ in pairs[:w])
            for k in range(len(pairs[w][0])):
                ref = left_refs[first + k]
                cols = ref.shape[1]
                cp = pltpu.make_async_copy(ref, lbuf.at[w % 2, :, pl.ds(at, cols)], lsem.at[w, k])
                cp.start()
                got.append(cp)
                at += cols
            cp = pltpu.make_async_copy(right_refs[w], rbuf.at[w % 2], lsem.at[w, 3])
            cp.start()
            got.append(cp)
            loads[w] = got

        started = []

        def send(i, k, src, dst, to):
            cp = pltpu.make_async_remote_copy(
                src_ref=src, dst_ref=dst, send_sem=ssem.at[i, k], recv_sem=rsem.at[i, k],
                device_id=to, device_id_type=MESHID)
            cp.start()
            started.append(cp)
            return cp

        flight = {}

        def spans(w):
            rw, a = shard_rows[w], cuts[w]
            return dict(plane=(y * a, rw - a), mine=(y * (rw - a), a), theirs=((1 - y) * (rw - a), a))

        def rows_of(w, kind):
            r0, k = spans(w)[kind]
            return pl.ds(pl.multiple_of(r0, 16), k)

        def compute(i):
            w, j = items[i]
            rw, lb = shard_rows[w], blocks[w]
            if j == 0:
                for cp in loads[w]:
                    cp.wait()
            cols = pl.ds(j * lb, lb)
            right = rbuf[w % 2, :, cols]

            @pl.loop(0, nz // 2)
            def _(half):
                left = lbuf[w % 2, :, pl.ds(pl.multiple_of(half * 8 * rw, 128), 8 * rw)]
                g = tn(left, right).astype(BF16)
                for k in range(8):
                    part[w][j, k % 2, (k // 2) % 2, 2 * half + k // 4] = g[k * rw:(k + 1) * rw]

            if w > 0 and j == width // lb - 1 and w + 2 < nw:
                load(w + 2)
            flight[i, 0] = send(i, 0, part[w].at[j, 1 - c], sibb[w].at[j], sib)

        def stage_sib(i):
            w, j = items[i]
            flight[i, 0].wait_recv()
            mine = part[w].at[j, c]

            @pl.loop(0, nz)
            def _(zz):
                for xx in range(2):
                    mine[xx, zz] = (mine[xx, zz].astype(F32) + sibb[w][j, xx, zz].astype(F32)).astype(BF16)

            flight[i, 1] = send(i, 1, mine.at[:, :, rows_of(w, "theirs")], yb[w].at[j], yn)

        def stage_y(i):
            w, j = items[i]
            flight[i, 1].wait_recv()
            mine = part[w].at[j, c]
            r = rows_of(w, "mine")

            @pl.loop(0, nz)
            def _(zz):
                for xx in range(2):
                    mine[xx, zz, r] = (mine[xx, zz, r].astype(F32) + yb[w][j, xx, zz].astype(F32)).astype(BF16)

            flight[i, 2] = send(i, 2, mine.at[1 - x, :, rows_of(w, "plane")], xb[w].at[j], xn)

        def stage_x(i):
            w, j = items[i]
            flight[i, 2].wait_recv()
            mine = part[w].at[j, c, x]
            r = rows_of(w, "plane")

            @pl.loop(0, nz)
            def _(zz):
                mine[zz, r] = (mine[zz, r].astype(F32) + xb[w][j, zz].astype(F32)).astype(BF16)

            for d in range(1, nz):
                flight[i, 2 + d] = send(i, 2 + d, mine.at[zp[d], r], zb[w].at[j, d - 1], zd[d])

        def stage_z(i):
            w, j = items[i]
            total = part[w][j, c, x, z, rows_of(w, "plane")].astype(F32)
            for d in range(1, nz):
                flight[i, 2 + d].wait_recv()
                total = total + zb[w][j, d - 1].astype(F32)
            fin[w][j] = total.astype(BF16)
            flight[i, 2 + nz] = send(i, 2 + nz, fin[w].at[j], finb[w].at[j], yn)

        def stage_out(i):
            w, j = items[i]
            rw, a, lb = shard_rows[w], cuts[w], blocks[w]
            cols = pl.ds(j * lb, lb)
            flight[i, 2 + nz].wait_recv()
            here, there = fin[w].at[j], finb[w].at[j]

            def at(r0, k):
                return pl.ds(pl.multiple_of(r0, 16), k)

            out_refs[w][at(y * (rw - a), a), cols] = here[at(y * (rw - 2 * a), a)].astype(F32)
            out_refs[w][at((1 - y) * (rw - a), a), cols] = there[at((1 - y) * (rw - 2 * a), a)].astype(F32)
            if rw > 2 * a:
                out_refs[w][pl.ds(a, rw - 2 * a), cols] = (
                    here[at((1 - y) * a, rw - 2 * a)].astype(F32) + there[at(y * a, rw - 2 * a)].astype(F32))

        pack_to = [sib, yn, xn, dev(y, z + 1 - 2 * lax.rem(z, 2), x, c), dev(y, lax.rem(z + 2, 4), x, c)]
        pack_cp = {}

        def pack_step(k):
            if k > 0:
                pack_cp[k - 1].wait()
                pbuf[0, k] = pbuf[0, k - 1] + pbuf[1, k - 1]
            else:
                pbuf[0, 0] = jnp.zeros_like(pbuf[0, 0])
                for row, col, value in sum_rows(s1_ref[...], *[ref[...] for ref in sum_refs]):
                    pbuf[0, 0, row:row + 1, 0:col] = value
            if k < len(pack_to):
                cp = pltpu.make_async_remote_copy(
                    src_ref=pbuf.at[0, k], dst_ref=pbuf.at[1, k], send_sem=psem.at[k], recv_sem=prsem.at[k],
                    device_id=pack_to[k], device_id_type=MESHID)
                cp.start()
                pack_cp[k] = cp
            else:
                pack_out[...] = pbuf[0, k]

        tiles = n // tile
        held = [pltpu.make_async_copy(w_hbm, w_ref, fsem.at[0]), pltpu.make_async_copy(x_hbm, x_ref, fsem.at[1])]
        written = []

        def resid(k):
            return pltpu.make_async_copy(r_hbm.at[pl.ds(k * tile, tile)], r_ref.at[k % 2], fsem.at[2 + tiles + k])

        def finish_tile(k):
            if k == 0:
                s1_ref[...] = jnp.zeros_like(s1_ref)
                for cp in held:
                    cp.wait()
            r = pl.ds(k * tile, tile)
            resid(k).wait()
            dn = nn(lbuf[0, r, 0:width], w_ref[0:width, :])
            for part in range(1, 3):
                span = slice(part * width, (part + 1) * width)
                dn = dn + nn(lbuf[0, r, span], w_ref[span, :])
            hat, rstd = row_stats(x_ref[r, :].astype(F32))
            x_ref[r, :] = (r_ref[k % 2] + norm_back(dn * vec_ref[4:5, :], hat, rstd)).astype(BF16)
            if k + 2 < tiles:
                resid(k + 2).start()
            s1_ref[0:1, :] += col_sum(dn * hat)
            s1_ref[1:2, :] += col_sum(dn)
            cp = pltpu.make_async_copy(x_ref.at[r], g_hbm.at[r], fsem.at[2 + k])
            cp.start()
            written.append(cp)
            if k == tiles - 1:
                load(2)

        load(0)
        for cp in held + [resid(0), resid(1)]:
            cp.start()
        load(1)
        pl.semaphore_wait(barrier, len(peers))
        stages = [compute, stage_sib, stage_y, stage_x, stage_z, stage_out]
        for t in range(ni + len(stages) - 1):
            for k, stage in enumerate(stages):
                if 0 <= t - k < ni:
                    stage(t - k)
            if t < tiles:
                finish_tile(t)
            elif t - tiles <= len(pack_to):
                pack_step(t - tiles)
        for cp in started:
            cp.wait_send()
        for cp in written:
            cp.wait()

    any_spec = pl.BlockSpec(memory_space=pl.ANY)
    vm = pl.BlockSpec(memory_space=pltpu.VMEM)

    def per_weight(make):
        return [pltpu.VMEM(make(width // b, shard_rows[w], cuts[w], b), BF16) for w, b in enumerate(blocks)]

    tiles = n // tile
    scratch = [pltpu.VMEM((n, width), BF16), pltpu.VMEM((2, tile, width), F32), pltpu.VMEM(qkv_t.shape, BF16),
               pltpu.VMEM((8, width), F32), pltpu.SemaphoreType.DMA((2 + 2 * tiles,)),
               pltpu.VMEM((2, n, max_left), BF16), pltpu.VMEM((2, n, width), BF16)]
    scratch += per_weight(lambda j, rw, a, b: (j, 2, 2, nz, rw, b))
    scratch += per_weight(lambda j, rw, a, b: (j, 2, nz, rw, b))
    scratch += per_weight(lambda j, rw, a, b: (j, 2, nz, a, b))
    scratch += per_weight(lambda j, rw, a, b: (j, nz, rw - a, b))
    scratch += per_weight(lambda j, rw, a, b: (j, nz - 1, rw - a, b))
    scratch += per_weight(lambda j, rw, a, b: (j, rw - a, b))
    scratch += per_weight(lambda j, rw, a, b: (j, rw - a, b))
    scratch += [
        pltpu.VMEM((2, 6, 16, 1024), F32),
        pltpu.SemaphoreType.DMA((ni, 3 + nz)), pltpu.SemaphoreType.DMA((ni, 3 + nz)),
        pltpu.SemaphoreType.DMA((6,)), pltpu.SemaphoreType.DMA((6,)), pltpu.SemaphoreType.DMA((nw, 4)),
    ]
    outs = pl.pallas_call(
        kernel,
        out_shape=[jax.ShapeDtypeStruct((rw, width), F32) for rw in shard_rows]
        + [jax.ShapeDtypeStruct((16, 1024), F32), jax.ShapeDtypeStruct((n, width), BF16)],
        in_specs=[any_spec] * (len(lefts) + nw + 3) + [vm] * 6,
        out_specs=[vm] * (nw + 1) + [any_spec],
        scratch_shapes=scratch,
        compiler_params=pltpu.CompilerParams(
            collective_id=collective, has_side_effects=True, vmem_limit_bytes=63 << 20),
        name="finish_reduce",
    )(*lefts, *rights, tokens, resid_grad, qkv_t, vecs, *sums)
    return outs[:nw], outs[nw], outs[nw + 1]


def sum_rows(s1, bq, bv, s768, sff, sal):
    lines = [bq[0:1], bv[0:1], s768[1:2], s768[0:1], s1[0:1], s1[1:2], s768[2:3], s768[3:4], sal[0:1]]
    lines += [sff[0:1, k:k + 1024] for k in range(0, sff.shape[1], 1024)]
    return [(row, v.shape[1], v) for row, v in enumerate(lines)]


def reduce_all(pairs, tokens, resid_grad, vecs, qkv_t, sums, fast):
    if fast:
        left_rows = [sum(a.shape[1] for a in ls) for ls, _ in pairs]
        shard_rows = [r // 16 for r in left_rows]
        cuts = [max(16, (r * 5 // 16) // 16 * 16) for r in shard_rows]
        blocks = [256, 256, 256, 384, 384]
        return finish_and_reduce(pairs, tokens, resid_grad, vecs, qkv_t, sums, shard_rows, cuts, blocks, 4, 1)
    grad_tokens, s1 = finish(tokens, resid_grad, *pairs[0][0], vecs, qkv_t)
    terms = [jnp.concatenate([tn(a, r).astype(BF16) for a in ls], 0) for ls, r in pairs]
    got = [lax.psum(lax.psum_scatter(t, "fsdp", scatter_dimension=0, tiled=True), "dp").astype(F32) for t in terms]
    lines = [jnp.pad(v, ((0, 0), (0, 1024 - k))) for _, k, v in sum_rows(s1, *sums)]
    pack = jnp.pad(jnp.concatenate(lines, 0), ((0, 16 - len(lines)), (0, 0)))
    return got, lax.psum(pack, ("dp", "fsdp")), grad_tokens


def per_device(mesh_shape, *args):
    (tokens, segment_ids, padding, qkv_weight, query_bias, value_bias, out_weight, out_bias,
     first_gain, first_shift, second_gain, second_shift, up_weight, up_bias, down_weight, down_bias,
     align_weight, align_bias, grad_output, grad_aligned) = args
    n, d = tokens.shape
    small = [query_bias, value_bias, out_bias, down_bias, first_gain, first_shift, second_gain, second_shift]
    members = mesh_shape["fsdp"]
    own, ub, ab = query_bias.shape[0], up_bias.shape[0], align_bias.shape[0]
    ff, al = ub * members, ab * members
    fast = mesh_shape["dp"] == 2 and members == 16

    seg = segment_ids[0]
    pad_row = padding[0]
    keys = jnp.where(pad_row == 0, seg, -1)
    valid_col = (1.0 - pad_row.astype(F32))[:, None]
    wins = windows(seg, 256)

    if fast:
        nz = members // 4
        lines = [v[None] for v in small] + [up_bias[None, :128], up_bias[None, 128:], align_bias[None]]
        pack = sum(jnp.pad(v, ((k, 47 - k), (0, 128 - v.shape[1]))) for k, v in enumerate(lines))
        normed, qkv, vecs, mixed, lse, packs, full = gather_attend(
            tokens, pack, [qkv_weight.T, out_weight, align_weight.T, up_weight.T, down_weight],
            seg[:, None], keys[None, :], own, nz)
        qkv_t, out_w, align_t, up_t, down_w = full
        up_b = packs[:, 8:10].reshape(members, 256)[:, :ub].reshape(1, ff).astype(F32)
        align_b = packs[:, 10, :ab].reshape(1, al).astype(F32)
    else:
        def gathered(a):
            return lax.all_gather(a, "fsdp", axis=0, tiled=True)

        qkv_t, out_w, up_t, down_w, align_t = [
            gathered(a) for a in (qkv_weight.T, out_weight, up_weight.T, down_weight, align_weight.T)]
        vecs = jnp.stack([gathered(v) for v in small]).astype(F32)
        up_b = gathered(up_bias).astype(F32)[None]
        align_b = gathered(align_bias).astype(F32)[None]
        qkv_b = jnp.concatenate([vecs[0:1], jnp.zeros((1, d), F32), vecs[1:2]], 1)
        normed, qkv = project(tokens, vecs, qkv_b, qkv_t)
        mixed, lse = attend(qkv, seg[:, None], keys[None, :], wins)
    (n2, act, du, gb, block_out, aligned, res, rb, dm, s768, sff, sal) = middle(
        tokens, mixed, grad_output, grad_aligned, valid_col, vecs, up_b, align_b, out_w, up_t, down_w, align_t)
    dq, dk, dv, bq, bv = attend_back(qkv, mixed, dm, lse, seg[None, :], keys[:, None], wins)
    pairs = [([dq, dk, dv], normed), ([act], gb), ([du], n2), ([mixed], rb), ([grad_aligned], block_out)]
    (g_qkv, g_down, g_up, g_out, g_align), pack, grad_tokens = reduce_all(
        pairs, tokens, res, vecs, qkv_t, (bq, bv, s768, sff, sal), fast)
    me = lax.axis_index("fsdp")
    vec = lax.dynamic_slice(pack, (0, me * own), (8, own))
    g_ub = lax.dynamic_slice(pack[9:9 + ff // 1024].reshape(ff), (me * ub,), (ub,))
    g_ab = lax.dynamic_slice(pack[8], (me * ab,), (ab,))
    return (block_out, aligned, grad_tokens, g_qkv.T, vec[0], vec[1], g_out, vec[2], vec[4], vec[5], vec[6],
            vec[7], g_up.T, g_ub, g_down, vec[3], g_align.T, g_ab)


def solution(mesh):
    rows_spec = P(("dp", "fsdp"), None)
    vec, by_col, by_row = P("fsdp"), P(None, "fsdp"), P("fsdp", None)
    in_specs = (rows_spec, rows_spec, rows_spec, by_col, vec, vec, by_row, vec, vec, vec, vec, vec,
                by_col, vec, by_row, vec, by_col, vec, rows_spec, rows_spec)
    out_specs = (rows_spec, rows_spec, rows_spec, by_col, vec, vec, by_row, vec, vec, vec, vec, vec,
                 by_col, vec, by_row, vec, by_col, vec)
    return jax.shard_map(functools.partial(per_device, dict(mesh.shape)), mesh=mesh, in_specs=in_specs,
                         out_specs=out_specs, check_vma=False)
```

```python
import functools

import jax
import jax.numpy as jnp
from jax import lax
from jax.experimental import pallas as pl
from jax.experimental.pallas import tpu as pltpu
from jax.sharding import PartitionSpec as P

HEADS = 12
F32 = jnp.float32
BF16 = jnp.bfloat16
NEG = -1e30


def nn(a, b):
    return lax.dot_general(a, b, (((1,), (0,)), ((), ())), preferred_element_type=F32)


def nt(a, b):
    return lax.dot_general(a, b, (((1,), (1,)), ((), ())), preferred_element_type=F32)


def tn(a, b):
    return lax.dot_general(a, b, (((0,), (0,)), ((), ())), preferred_element_type=F32)


def col_sum(v):
    return jnp.sum(v, 0, keepdims=True)


def gelu_parts(u):
    z = jnp.abs(u) * (0.5 ** 0.5)
    ez = jnp.exp(-(z * z))
    t = 1.0 / (1.0 + 0.33 * z)
    poly = -0.13593485572044933
    for coef in (0.46271278142719047, -0.3554798541586114, 0.412577688277986, 0.044992638979585504,
                 0.2019288303128453, 0.18283654298343202, 0.18636614548593147):
        poly = poly * t + coef
    half_erfc = (0.5 * t) * poly * ez
    cdf = jnp.where(u > 0, 1.0 - half_erfc, half_erfc)
    return u * cdf, cdf + u * ez * 0.3989422804014327


def row_stats(x):
    mean = jnp.mean(x, -1, keepdims=True)
    centered = x - mean
    rstd = lax.rsqrt(jnp.mean(centered * centered, -1, keepdims=True) + 1e-05)
    return centered * rstd, rstd


def norm_back(grad_hat, hat, rstd):
    return rstd * (grad_hat - jnp.mean(grad_hat, -1, keepdims=True)
                   - hat * jnp.mean(grad_hat * hat, -1, keepdims=True))


def call(kernel, grid, ins, outs, scratch=(), name=None, prefetch=(), limit=60):
    return pl.pallas_call(
        kernel,
        grid_spec=pltpu.PrefetchScalarGridSpec(
            num_scalar_prefetch=len(prefetch), grid=grid,
            in_specs=[pl.BlockSpec(b, m, **({"pipeline_mode": pl.Buffered(1)} if once else {}))
                      for _, b, m, once in ins],
            out_specs=[pl.BlockSpec(b, m) for _, _, b, m in outs],
            scratch_shapes=list(scratch)),
        out_shape=[jax.ShapeDtypeStruct(s, d) for s, d, _, _ in outs],
        compiler_params=pltpu.CompilerParams(
            dimension_semantics=("arbitrary",) * len(grid), vmem_limit_bytes=limit << 20),
        name=name,
    )(*prefetch, *[a for a, _, _, _ in ins])


def whole(a):
    n = a.ndim
    return (a, a.shape, lambda *_: (0,) * n, True)


def rows(a, tile):
    return (a, (tile, a.shape[1]), lambda i, *_: (i, 0), False)


def rows_out(n, width, dtype, tile):
    return ((n, width), dtype, (tile, width), lambda i, *_: (i, 0))


def fixed_out(shape, dtype):
    n = len(shape)
    return (shape, dtype, shape, lambda *_: (0,) * n)


def project(tokens, vecs, qkv_bias, qkv_t, tile=256):
    n, d = tokens.shape

    def kernel(x_ref, v_ref, b_ref, w_ref, n_ref, o_ref):
        hat, _ = row_stats(x_ref[...].astype(F32))
        low = (hat * v_ref[4:5, :] + v_ref[5:6, :]).astype(BF16)
        n_ref[...] = low
        for part in range(3):
            cols = pl.ds(part * d, d)
            o_ref[:, cols] = (nt(low, w_ref[cols, :]) + b_ref[:, cols]).astype(BF16)

    return call(
        kernel, (n // tile,),
        [rows(tokens, tile), whole(vecs), whole(qkv_bias), whole(qkv_t)],
        [rows_out(n, d, BF16, tile), rows_out(n, 3 * d, BF16, tile)],
        name="project")


def pair_masks(shape):
    lane = lax.broadcasted_iota(jnp.int32, shape, 1)
    return lane < 64


def windows(seg, tile, step=256):
    n = seg.shape[0]
    first = seg[::tile]
    last = seg[tile - 1::tile]
    lo = jnp.sum(seg[None, :] < first[:, None], 1, dtype=jnp.int32) // 128 * 128
    hi = jnp.sum(seg[None, :] <= last[:, None], 1, dtype=jnp.int32)
    count = (hi - lo + step - 1) // step
    return jnp.stack([jnp.minimum(lo, n - count * step), count])


def fill_mask(mask, rows_ref, cols_ref, n, tile=256):
    @pl.when(pl.program_id(0) == 0)
    def _():
        @pl.loop(0, n // tile)
        def _(t):
            r = pl.ds(pl.multiple_of(t * tile, tile), tile)
            row_id = t * tile + lax.broadcasted_iota(jnp.int32, (tile, n), 0)
            col_id = lax.broadcasted_iota(jnp.int32, (tile, n), 1)
            keep = (rows_ref[r, :] == cols_ref[...]) | (row_id == col_id)
            mask[r, :] = jnp.where(keep, 0.0, NEG).astype(F32)


def attend(qkv, seg_col, key_row, wins, tq=256, step=256):
    n = qkv.shape[0]
    d = qkv.shape[1] // 3
    pairs = d // 128

    def kernel(win, q_ref, k_ref, v_ref, sc_ref, kr_ref, o_ref, lse_ref, mask, va, vb):
        fill_mask(mask, sc_ref, kr_ref, n)
        v = v_ref[...]
        low_half = pair_masks((n, 128))
        zero = jnp.zeros_like(v)
        va[...] = jnp.where(low_half, v, zero)
        vb[...] = jnp.where(low_half, zero, v)
        half = pair_masks((tq, 128))

        @pl.loop(0, n // tq)
        def _(t):
            r = pl.ds(pl.multiple_of(t * tq, tq), tq)
            first = pl.multiple_of(win[0, t], 128)

            for count in range(1, n // step + 1):
                @pl.when(win[1, t] == count)
                def _():
                    keys = pl.ds(first, count * step)
                    q = q_ref[r, :] * jnp.asarray(0.125, BF16)
                    qz = jnp.zeros_like(q)
                    kk = k_ref[keys, :]
                    outs, tops, sums = [], [], []
                    for qh, vh in ((jnp.where(half, q, qz), va), (jnp.where(half, qz, q), vb)):
                        s = nt(qh, kk) + mask[r, keys]
                        top = jnp.max(s, 1, keepdims=True)
                        p = jnp.exp(s - top)
                        sums.append(jnp.sum(p, 1, keepdims=True))
                        tops.append(top)
                        outs.append(nn(p.astype(BF16), vh[keys, :]))
                    (la, lb), (ma, mb) = sums, tops
                    o_ref[r, :] = ((outs[0] + outs[1]) * jnp.where(half, 1.0 / la, 1.0 / lb)).astype(BF16)
                    lse = jnp.where(half, ma + jnp.log(la), mb + jnp.log(lb)).T
                    lse_ref[0:1, r] = lse[0:1, :]
                    lse_ref[1:2, r] = lse[64:65, :]

    def block(first):
        return (qkv, (n, 128), lambda p, *_: (0, first * pairs + p), False)

    return call(
        kernel, (pairs,),
        [block(0), block(1), block(2), whole(seg_col), whole(key_row)],
        [((n, d), BF16, (n, 128), lambda p, *_: (0, p)),
         ((8 * pairs, n), F32, (8, n), lambda p, *_: (p, 0))],
        [pltpu.VMEM((n, n), F32), pltpu.VMEM((n, 128), BF16), pltpu.VMEM((n, 128), BF16)],
        name="attend", prefetch=(wins,))


def attend_back(qkv, mixed, grad_mixed, lse, seg_row, key_col, wins, tk=256, step=256):
    n = qkv.shape[0]
    d = qkv.shape[1] // 3
    pairs = d // 128

    def kernel(win, q_ref, k_ref, v_ref, o_ref, g_ref, lse_ref, sr_ref, kc_ref,
               dq_ref, dk_ref, dv_ref, bq_ref, bv_ref, mask, qa, qb, ga, gb, kt, dots, dqt):
        fill_mask(mask, kc_ref, sr_ref, n)
        half = pair_masks((n, 128))
        q = q_ref[...] * jnp.asarray(0.125, BF16)
        zero = jnp.zeros_like(q)
        qa[...] = jnp.where(half, q, zero)
        qb[...] = jnp.where(half, zero, q)
        g = g_ref[...]
        ga[...] = jnp.where(half, g, zero)
        gb[...] = jnp.where(half, zero, g)
        kt[...] = k_ref[...].astype(F32).T.astype(BF16)
        prod = (g.astype(F32) * o_ref[...].astype(F32)).T
        dots[0:1, :] = col_sum(prod[:64])
        dots[1:2, :] = col_sum(prod[64:])
        dqt[...] = jnp.zeros_like(dqt)

        @pl.loop(0, n // tk)
        def _(t):
            keys = pl.ds(pl.multiple_of(t * tk, tk), tk)
            first = pl.multiple_of(win[0, t], 128)

            for count in range(1, n // step + 1):
                @pl.when(win[1, t] == count)
                def _():
                    kk = k_ref[keys, :]
                    vv = v_ref[keys, :]
                    dk = dv = None
                    for e in range(count):
                        cols = pl.ds(pl.multiple_of(first + e * step, 128), step)
                        m = mask[keys, cols]
                        for h, (qh, gh) in enumerate(((qa, ga), (qb, gb))):
                            qq = qh[cols, :]
                            gg = gh[cols, :]
                            p = jnp.exp(nt(kk, qq) + m - lse_ref[h:h + 1, cols])
                            ds = (p * (nt(vv, gg) - dots[h:h + 1, cols])).astype(BF16)
                            pv = nn(p.astype(BF16), gg)
                            pk = nn(ds, qq)
                            dv = pv if dv is None else dv + pv
                            dk = pk if dk is None else dk + pk
                            part = pl.ds(64 * h, 64)
                            dqt[part, cols] += nn(kt[part, keys], ds)
                    dk_ref[keys, :] = dk.astype(BF16)
                    dv_ref[keys, :] = dv.astype(BF16)

        dq = (dqt[...].T * 0.125).astype(BF16)
        dq_ref[...] = dq
        bq_ref[...] = jnp.broadcast_to(col_sum(dq.astype(F32)), (8, 128))
        bv_ref[...] = jnp.broadcast_to(col_sum(dv_ref[...].astype(F32)), (8, 128))

    def block(a, first=0):
        return (a, (n, 128), lambda p, *_: (0, first * pairs + p), False)

    cols = ((n, d), BF16, (n, 128), lambda p, *_: (0, p))
    sums = ((8, d), F32, (8, 128), lambda p, *_: (0, p))
    return call(
        kernel, (pairs,),
        [block(qkv, 0), block(qkv, 1), block(qkv, 2), block(mixed), block(grad_mixed),
         (lse, (8, n), lambda p, *_: (p, 0), False), whole(seg_row), whole(key_col)],
        [cols, cols, cols, sums, sums],
        [pltpu.VMEM((n, n), F32)] + [pltpu.VMEM((n, 128), BF16)] * 4
        + [pltpu.VMEM((128, n), BF16), pltpu.VMEM((8, n), F32), pltpu.VMEM((128, n), F32)],
        name="attend_back", prefetch=(wins,))


def middle(tokens, mixed, grad_output, grad_aligned, valid_col, vecs, up_b, align_b,
           out_w, up_t, down_w, align_t, tile=256, chunk=768):
    n, d = tokens.shape
    ff, al = up_t.shape[0], align_t.shape[0]

    def kernel(x_ref, m_ref, go_ref, ga_ref, v_ref, vec_ref, ub_ref, ab_ref, wo_ref, wu_ref, wd_ref, wa_ref,
               n_ref, act_ref, du_ref, gb_ref, out_ref, al_ref, r_ref, rb_ref, dm_ref,
               s768_ref, sff_ref, sal_ref, branch, dn):
        @pl.when(pl.program_id(0) == 0)
        def _():
            s768_ref[...] = jnp.zeros_like(s768_ref)
            sff_ref[...] = jnp.zeros_like(sff_ref)
            sal_ref[...] = jnp.zeros_like(sal_ref)

        resid = x_ref[...].astype(F32) + nn(m_ref[...], wo_ref[...]) + vec_ref[2:3, :]
        hat, rstd = row_stats(resid)
        low = (hat * vec_ref[6:7, :] + vec_ref[7:8, :]).astype(BF16)
        n_ref[...] = low
        valid = v_ref[...]
        ga = ga_ref[...]
        sal_ref[0:1, :] += col_sum(ga.astype(F32))
        grad = valid * (go_ref[...].astype(F32) + nn(ga, wa_ref[...]))
        gb = grad.astype(BF16)
        gb_ref[...] = gb
        branch[...] = jnp.zeros_like(branch)
        dn[...] = jnp.zeros_like(dn)

        @pl.loop(0, ff // chunk)
        def _(t):
            part = pl.ds(pl.multiple_of(t * chunk, chunk), chunk)
            wu = wu_ref[part, :]
            wd = wd_ref[part, :]
            act, slope = gelu_parts(nt(n_ref[...], wu) + ub_ref[0:1, part])
            act = act.astype(BF16)
            act_ref[:, part] = act
            branch[...] += nn(act, wd)
            du = slope * nt(gb_ref[...], wd)
            du = du.astype(BF16)
            du_ref[:, part] = du
            sff_ref[0:1, part] += col_sum(du.astype(F32))
            dn[...] += nn(du, wu)

        out = (valid * (resid + branch[...] + vec_ref[3:4, :])).astype(BF16)
        out_ref[...] = out
        al_ref[...] = (nt(out, wa_ref[...]) + ab_ref[...]).astype(BF16)
        dn2 = dn[...]
        res = grad + norm_back(dn2 * vec_ref[6:7, :], hat, rstd)
        r_ref[...] = res
        rb = res.astype(BF16)
        rb_ref[...] = rb
        dm_ref[...] = nt(rb, wo_ref[...]).astype(BF16)
        s768_ref[0:1, :] += col_sum(gb.astype(F32))
        s768_ref[1:2, :] += col_sum(rb.astype(F32))
        s768_ref[2:3, :] += col_sum(dn2 * hat)
        s768_ref[3:4, :] += col_sum(dn2)

    r = functools.partial(rows_out, n, tile=tile)
    return call(
        kernel, (n // tile,),
        [rows(tokens, tile), rows(mixed, tile), rows(grad_output, tile), rows(grad_aligned, tile),
         rows(valid_col, tile), whole(vecs), whole(up_b), whole(align_b), whole(out_w), whole(up_t),
         whole(down_w), whole(align_t)],
        [r(d, BF16), r(ff, BF16), r(ff, BF16), r(d, BF16), r(d, BF16), r(al, BF16), r(d, F32), r(d, BF16),
         r(d, BF16), fixed_out((8, d), F32), fixed_out((8, ff), F32), fixed_out((8, al), F32)],
        [pltpu.VMEM((tile, d), F32), pltpu.VMEM((tile, d), F32)],
        name="middle")


def finish(tokens, resid_grad, dq, dk, dv, vecs, qkv_t, tile=256):
    n, d = tokens.shape

    def kernel(x_ref, r_ref, dq_ref, dk_ref, dv_ref, vec_ref, w_ref, o_ref, s_ref):
        @pl.when(pl.program_id(0) == 0)
        def _():
            s_ref[...] = jnp.zeros_like(s_ref)

        dn = nn(dq_ref[...], w_ref[0:d, :]) + nn(dk_ref[...], w_ref[d:2 * d, :]) + nn(dv_ref[...], w_ref[2 * d:, :])
        hat, rstd = row_stats(x_ref[...].astype(F32))
        o_ref[...] = (r_ref[...] + norm_back(dn * vec_ref[4:5, :], hat, rstd)).astype(BF16)
        s_ref[0:1, :] += col_sum(dn * hat)
        s_ref[1:2, :] += col_sum(dn)

    return call(
        kernel, (n // tile,),
        [rows(tokens, tile), rows(resid_grad, tile), rows(dq, tile), rows(dk, tile), rows(dv, tile),
         whole(vecs), whole(qkv_t)],
        [rows_out(n, d, BF16, tile), fixed_out((8, d), F32)],
        name="finish")
MESHID = pl.DeviceIdType.MESH


def coords():
    y = lax.axis_index("dp")
    f = lax.axis_index("fsdp")
    return y, f // 4, lax.rem(f // 2, 2), lax.rem(f, 2)


def at_rows(first, count):
    return pl.ds(pl.multiple_of(first, 16), count)


class Gather:
    def __init__(self, items, nz, ssem, rsem, lsem):
        self.items, self.nz, self.ssem, self.rsem, self.lsem = items, nz, ssem, rsem, lsem
        self.y, self.z, self.x, self.c = coords()

    def device(self, y=None, z=None, x=None, c=None):
        pick = [own if new is None else new for own, new in zip((self.y, self.z, self.x, self.c), (y, z, x, c))]
        return (pick[0], pick[1] * 4 + pick[2] * 2 + pick[3])

    def ahead(self, d):
        return lax.rem(self.z + d, self.nz)

    def enter(self):
        barrier = pltpu.get_barrier_semaphore()
        peers = [self.device(c=1 - self.c), self.device(x=1 - self.x), self.device(y=1 - self.y)]
        peers += [self.device(z=self.ahead(d)) for d in range(1, self.nz)]
        for peer in peers:
            pl.semaphore_signal(barrier, inc=1, device_id=peer, device_id_type=MESHID)
        pl.semaphore_wait(barrier, len(peers))

    def span(self, i, which):
        _, _, lo, n, third = self.items[i]
        return {"all": (lo, n), "plane": (lo + self.y * third, n - third),
                "mine": (lo + self.y * (n - third), third)}[which]

    def local(self, i):
        own, full = self.items[i][:2]
        r = at_rows(*self.span(i, "plane"))
        return pltpu.make_async_copy(own.at[r], full.at[self.z, self.x, self.c, r], self.lsem.at[i])

    def copy(self, i, k):
        own, full = self.items[i][:2]
        every = pl.ds(0, self.nz)
        if k == 0:
            ref = full.at[every, self.x, self.c, at_rows(*self.span(i, "plane"))]
            src, to = ref, self.device(x=1 - self.x)
        elif k == 1:
            ref = full.at[every, :, self.c, at_rows(*self.span(i, "mine"))]
            src, to = ref, self.device(y=1 - self.y)
        elif k == 2:
            ref = full.at[every, :, self.c, at_rows(*self.span(i, "all"))]
            src, to = ref, self.device(c=1 - self.c)
        else:
            r = at_rows(*self.span(i, "plane"))
            src, ref, to = own.at[r], full.at[self.z, self.x, self.c, r], self.device(z=self.ahead(k - 2))
        return pltpu.make_async_remote_copy(
            src_ref=src, dst_ref=ref, send_sem=self.ssem.at[i, k], recv_sem=self.rsem.at[i, k],
            device_id=to, device_id_type=MESHID)

    def start(self, i):
        self.local(i).start()
        for d in range(1, self.nz):
            self.copy(i, 2 + d).start()

    def pass_z(self, i):
        for d in range(1, self.nz):
            self.copy(i, 2 + d).wait_recv()
        self.local(i).wait()
        self.copy(i, 0).start()

    def pass_x(self, i):
        self.copy(i, 0).wait_recv()
        self.copy(i, 1).start()

    def pass_y(self, i):
        self.copy(i, 1).wait_recv()
        self.copy(i, 2).start()

    def ready(self, i):
        self.copy(i, 2).wait_recv()

    def leave(self):
        for i in range(len(self.items)):
            for k in range(2 + self.nz):
                self.copy(i, k).wait_send()

    def events(self, link, hop):
        sizes = [full.shape[-1] * n for _, full, _, n, _ in self.items]
        out = []
        z = x = y = 0.0
        for i, size in enumerate(sizes):
            t = link * size / sum(sizes)
            z += t
            x = max(x, z + hop) + t
            y = max(y, x + hop) + t
            out += [(z + hop, self.pass_z, i), (x + hop, self.pass_x, i), (y + hop, self.pass_y, i),
                    (y + 2 * hop + t / 4, self.ready, i)]
        return sorted(out, key=lambda e: (e[0], e[2]))


def gather_attend(tokens, pack, shards, seg_col, key_row, own, nz, tile=512, tq=256, link=62.0, hop=2.0,
                  start=5.0, slots=(4.8, 1.45)):
    n, d = tokens.shape
    members = 4 * nz
    pairs = d // 128
    heights = [s.shape[0] for s in shards]
    cuts = [(1 + w, lo, min(48, h - lo) if h != 64 else 64) for w, h in enumerate(heights)
            for lo in range(0, h if h != 64 else 1, 48)]
    cuts = [(0, 0, pack.shape[0])] + cuts
    first_use = 1 + len([c for c in cuts if c[0] == 1])
    ni = len(cuts)

    def kernel(x_ref, sc_ref, kr_ref, p_ref, *refs):
        owns = (p_ref,) + refs[:5]
        n_ref, qkv_ref, vec_ref, o_ref, lse_ref = refs[5:10]
        fulls = refs[10:16]
        mask, va, vb, ssem, rsem, lsem = refs[16:]
        packs_ref, w_ref = fulls[:2]
        g = Gather([(owns[w], fulls[w], lo, k, max(16, k // 3 // 16 * 16)) for w, lo, k in cuts], nz, ssem, rsem, lsem)
        g.enter()
        for i in range(ni):
            g.start(i)

        @pl.loop(0, n // tq)
        def _(t):
            r = pl.ds(pl.multiple_of(t * tq, tq), tq)
            row_id = t * tq + lax.broadcasted_iota(jnp.int32, (tq, n), 0)
            col_id = lax.broadcasted_iota(jnp.int32, (tq, n), 1)
            keep = (sc_ref[r, :] == kr_ref[...]) | (row_id == col_id)
            mask[r, :] = jnp.where(keep, 0.0, NEG).astype(F32)

        events = g.events(link, hop)
        now = start + max(t for t, f, i in events if i < first_use and f == g.ready)

        def pump(until):
            while events and start + events[0][0] <= until:
                _, f, i = events.pop(0)
                f(i)

        pump(now)
        plan = []
        for k in range(n // tile + pairs * (n // tq)):
            now += slots[0] if k < n // tile else slots[1]
            mark = len([e for e in events if start + e[0] <= now])
            plan.append(events[:mark])
            del events[:mark]
        total = jnp.zeros((16, d), F32)
        row = lax.broadcasted_iota(jnp.int32, (128, d), 0)
        col = lax.broadcasted_iota(jnp.int32, (128, d), 1)
        for s in range(members):
            place = jnp.where((col == row + s * own) & (row < own), 1.0, 0.0).astype(BF16)
            total = total + nn(packs_ref[s // 4, s // 2 % 2, s % 2, 0:16, :], place)
        vec_ref[...] = total[:8]
        part = 3 * d // 2
        gap = jnp.zeros((1, d // 2), F32)
        biases = [jnp.concatenate([vec_ref[0:1, :], gap], 1), jnp.concatenate([gap, vec_ref[1:2, :]], 1)]

        @pl.loop(0, n // tile)
        def _(t):
            r = pl.ds(pl.multiple_of(t * tile, tile), tile)
            hat, _ = row_stats(x_ref[r, :].astype(F32))
            n_ref[r, :] = (hat * vec_ref[4:5, :] + vec_ref[5:6, :]).astype(BF16)
            for k in range(2):
                w = w_ref[k * (nz // 2):(k + 1) * (nz // 2)].reshape(part, d)
                qkv_ref[r, k * part:(k + 1) * part] = (nt(n_ref[r, :], w) + biases[k]).astype(BF16)
            for k in range(n // tile):
                if plan[k]:
                    @pl.when(t == k)
                    def _():
                        for _, f, i in plan[k]:
                            f(i)

        pumped = plan[n // tile:]
        low_half = pair_masks((n, 128))
        half = pair_masks((tq, 128))
        tiles = n // tq

        @pl.loop(0, pairs)
        def _(p):
            def cols(k):
                return pl.ds(pl.multiple_of(k * d + p * 128, 128), 128)

            v = qkv_ref[:, cols(2)]
            zero = jnp.zeros_like(v)
            va[...] = jnp.where(low_half, v, zero)
            vb[...] = jnp.where(low_half, zero, v)

            @pl.loop(0, tiles)
            def _(t):
                r = pl.ds(pl.multiple_of(t * tq, tq), tq)
                q = qkv_ref[r, cols(0)] * jnp.asarray(0.125, BF16)
                qz = jnp.zeros_like(q)
                kk = qkv_ref[:, cols(1)]
                outs, tops, sums = [], [], []
                for qh, vh in ((jnp.where(half, q, qz), va), (jnp.where(half, qz, q), vb)):
                    s = nt(qh, kk) + mask[r, :]
                    top = jnp.max(s, 1, keepdims=True)
                    e = jnp.exp(s - top)
                    sums.append(jnp.sum(e, 1, keepdims=True))
                    tops.append(top)
                    outs.append(nn(e.astype(BF16), vh[...]))
                (la, lb), (ma, mb) = sums, tops
                o_ref[r, cols(0)] = ((outs[0] + outs[1]) * jnp.where(half, 1.0 / la, 1.0 / lb)).astype(BF16)
                lse = jnp.where(half, ma + jnp.log(la), mb + jnp.log(lb)).T
                lse_ref[p, 0:1, r] = lse[0:1, :]
                lse_ref[p, 1:2, r] = lse[64:65, :]
                for k, step in enumerate(pumped):
                    if step:
                        @pl.when(p * tiles + t == k)
                        def _():
                            for _, f, i in step:
                                f(i)

        for _, f, i in events:
            f(i)
        g.leave()

    vm = pl.BlockSpec(memory_space=pltpu.VMEM)
    hbm = pl.BlockSpec(memory_space=pl.ANY)
    sds = jax.ShapeDtypeStruct

    def full(h, width):
        return sds((nz, 2, 2, h, width), BF16)

    outs = pl.pallas_call(
        kernel,
        out_shape=[sds((n, d), BF16), sds((n, 3 * d), BF16), sds((8, d), F32), sds((n, d), BF16),
                   sds((pairs, 8, n), F32), full(pack.shape[0], 128)] + [full(h, d) for h in heights],
        in_specs=[vm] * 9, out_specs=[vm] * 7 + [hbm] * 4,
        scratch_shapes=[pltpu.VMEM((n, n), F32), pltpu.VMEM((n, 128), BF16), pltpu.VMEM((n, 128), BF16),
                        pltpu.SemaphoreType.DMA((ni, 2 + nz)), pltpu.SemaphoreType.DMA((ni, 2 + nz)),
                        pltpu.SemaphoreType.DMA((ni,))],
        compiler_params=pltpu.CompilerParams(collective_id=0, has_side_effects=True, vmem_limit_bytes=60 << 20),
        name="gather_attend",
    )(tokens, seg_col, key_row, pack, *shards)
    normed, qkv, vecs, mixed, lse, packs = outs[:6]
    return (normed, qkv, vecs, mixed, lse.reshape(8 * pairs, n), packs.reshape(members, -1, 128),
            [w.reshape(-1, d) for w in outs[6:]])


def plan_steps(count, tiles, first_tile, hops, lags):
    steps = []
    for t in range(max(count + max(lags), first_tile + tiles + hops + 1)):
        stages = [(t - lag, kind) for kind, lag in zip(("compute", "sib", "y", "x", "z", "out"), (0,) + lags)]
        steps += [(kind, i) for i, kind in stages if 0 <= i < count]
        k = t - first_tile
        if 0 <= k < tiles:
            steps.append(("finish", k))
        elif 0 <= k - tiles <= hops:
            steps.append(("pack", k - tiles))
    return steps


def finish_and_reduce(pairs, tokens, resid_grad, vecs, qkv_t, sums, shard_rows, cuts, blocks, nz, collective, tile=256,
                      qkv=2, first_tile=7, lags=(1, 2, 4, 6, 7)):
    nw = len(pairs)
    lefts = [a for ls, _ in pairs for a in ls]
    rights = [r for _, r in pairs]
    n = rights[0].shape[0]
    width = rights[0].shape[1]
    max_left = max(sum(a.shape[1] for a in ls) for ls, _ in pairs)
    items = [(w, j) for w in range(nw) for j in range(width // blocks[w])]
    ni = len(items)
    first_tile = max(max(i for i, (w, _) in enumerate(items) if w == qkv), first_tile)
    steps = plan_steps(ni, n // tile, first_tile, 5, lags)

    def kernel(*refs):
        left_refs = refs[:len(lefts)]
        right_refs = refs[len(lefts):len(lefts) + nw]
        pos = len(lefts) + nw
        x_hbm, r_hbm, w_hbm, vec_ref = refs[pos:pos + 4]
        sum_refs = refs[pos + 4:pos + 9]
        pos += 9
        out_refs = refs[pos:pos + nw]
        pack_out, g_hbm = refs[pos + nw:pos + nw + 2]
        pos += 2 + nw
        x_ref, r_ref, w_ref, s1_ref, fsem = refs[pos:pos + 5]
        pos += 5
        lbuf, rbuf = refs[pos:pos + 2]
        part, sibb, yb, xb, zb, fin, finb = [refs[pos + 2 + k * nw:pos + 2 + (k + 1) * nw] for k in range(7)]
        pos += 2 + 7 * nw
        pbuf, ssem, rsem, psem, prsem, lsem = refs[pos:]

        y, z, x, c = coords()

        def dev(yy, zz, xx, cc):
            return (yy, zz * 4 + xx * 2 + cc)

        sib, xn, yn = dev(y, z, x, 1 - c), dev(y, z, 1 - x, c), dev(1 - y, z, x, c)
        zp = [lax.rem(z + d, nz) for d in range(nz)]
        zd = [dev(y, zp[d], x, c) for d in range(nz)]

        barrier = pltpu.get_barrier_semaphore()
        peers = [sib, xn, yn] + zd[1:]
        for p in peers:
            pl.semaphore_signal(barrier, inc=1, device_id=p, device_id_type=MESHID)

        loads = {}

        def load(w):
            at = 0
            got = []
            first = sum(len(ls) for ls, _ in pairs[:w])
            for k in range(len(pairs[w][0])):
                ref = left_refs[first + k]
                cols = ref.shape[1]
                cp = pltpu.make_async_copy(ref, lbuf.at[w % 2, :, pl.ds(at, cols)], lsem.at[w, k])
                cp.start()
                got.append(cp)
                at += cols
            cp = pltpu.make_async_copy(right_refs[w], rbuf.at[w % 2], lsem.at[w, 3])
            cp.start()
            got.append(cp)
            loads[w] = got

        started = []

        def send(i, k, src, dst, to):
            cp = pltpu.make_async_remote_copy(
                src_ref=src, dst_ref=dst, send_sem=ssem.at[i, k], recv_sem=rsem.at[i, k],
                device_id=to, device_id_type=MESHID)
            cp.start()
            started.append(cp)
            return cp

        flight = {}

        def spans(w):
            rw, a = shard_rows[w], cuts[w]
            return dict(plane=(y * a, rw - a), mine=(y * (rw - a), a), theirs=((1 - y) * (rw - a), a))

        def rows_of(w, kind):
            r0, k = spans(w)[kind]
            return pl.ds(pl.multiple_of(r0, 16), k)

        def compute(i):
            w, j = items[i]
            rw, lb = shard_rows[w], blocks[w]
            if j == 0:
                for cp in loads[w]:
                    cp.wait()
            cols = pl.ds(j * lb, lb)
            right = rbuf[w % 2, :, cols]

            @pl.loop(0, nz // 2)
            def _(half):
                left = lbuf[w % 2, :, pl.ds(pl.multiple_of(half * 8 * rw, 128), 8 * rw)]
                g = tn(left, right).astype(BF16)
                for k in range(8):
                    part[w][j, k % 2, (k // 2) % 2, 2 * half + k // 4] = g[k * rw:(k + 1) * rw]

            if w != qkv and j == width // lb - 1 and w + 2 < nw:
                load(w + 2)
            flight[i, 0] = send(i, 0, part[w].at[j, 1 - c], sibb[w].at[j], sib)

        def stage_sib(i):
            w, j = items[i]
            flight[i, 0].wait_recv()
            mine = part[w].at[j, c]

            @pl.loop(0, nz)
            def _(zz):
                for xx in range(2):
                    mine[xx, zz] = (mine[xx, zz].astype(F32) + sibb[w][j, xx, zz].astype(F32)).astype(BF16)

            flight[i, 1] = send(i, 1, mine.at[:, :, rows_of(w, "theirs")], yb[w].at[j], yn)

        def stage_y(i):
            w, j = items[i]
            flight[i, 1].wait_recv()
            mine = part[w].at[j, c]
            r = rows_of(w, "mine")

            @pl.loop(0, nz)
            def _(zz):
                for xx in range(2):
                    mine[xx, zz, r] = (mine[xx, zz, r].astype(F32) + yb[w][j, xx, zz].astype(F32)).astype(BF16)

            flight[i, 2] = send(i, 2, mine.at[1 - x, :, rows_of(w, "plane")], xb[w].at[j], xn)

        def stage_x(i):
            w, j = items[i]
            flight[i, 2].wait_recv()
            mine = part[w].at[j, c, x]
            r = rows_of(w, "plane")

            @pl.loop(0, nz)
            def _(zz):
                mine[zz, r] = (mine[zz, r].astype(F32) + xb[w][j, zz].astype(F32)).astype(BF16)

            for d in range(1, nz):
                flight[i, 2 + d] = send(i, 2 + d, mine.at[zp[d], r], zb[w].at[j, d - 1], zd[d])

        def stage_z(i):
            w, j = items[i]
            total = part[w][j, c, x, z, rows_of(w, "plane")].astype(F32)
            for d in range(1, nz):
                flight[i, 2 + d].wait_recv()
                total = total + zb[w][j, d - 1].astype(F32)
            fin[w][j] = total.astype(BF16)
            flight[i, 2 + nz] = send(i, 2 + nz, fin[w].at[j], finb[w].at[j], yn)

        def stage_out(i):
            w, j = items[i]
            rw, a, lb = shard_rows[w], cuts[w], blocks[w]
            cols = pl.ds(j * lb, lb)
            flight[i, 2 + nz].wait_recv()
            here, there = fin[w].at[j], finb[w].at[j]

            def at(r0, k):
                return pl.ds(pl.multiple_of(r0, 16), k)

            out_refs[w][at(y * (rw - a), a), cols] = here[at(y * (rw - 2 * a), a)].astype(F32)
            out_refs[w][at((1 - y) * (rw - a), a), cols] = there[at((1 - y) * (rw - 2 * a), a)].astype(F32)
            if rw > 2 * a:
                out_refs[w][pl.ds(a, rw - 2 * a), cols] = (
                    here[at((1 - y) * a, rw - 2 * a)].astype(F32) + there[at(y * a, rw - 2 * a)].astype(F32))

        pack_to = [sib, yn, xn, dev(y, z + 1 - 2 * lax.rem(z, 2), x, c), dev(y, lax.rem(z + 2, 4), x, c)]
        pack_cp = {}

        def pack_step(k):
            if k > 0:
                pack_cp[k - 1].wait()
                pbuf[0, k] = pbuf[0, k - 1] + pbuf[1, k - 1]
            else:
                pbuf[0, 0] = jnp.zeros_like(pbuf[0, 0])
                for row, col, value in sum_rows(s1_ref[...], *[ref[...] for ref in sum_refs]):
                    pbuf[0, 0, row:row + 1, 0:col] = value
            if k < len(pack_to):
                cp = pltpu.make_async_remote_copy(
                    src_ref=pbuf.at[0, k], dst_ref=pbuf.at[1, k], send_sem=psem.at[k], recv_sem=prsem.at[k],
                    device_id=pack_to[k], device_id_type=MESHID)
                cp.start()
                pack_cp[k] = cp
            else:
                pack_out[...] = pbuf[0, k]

        tiles = n // tile
        held = [pltpu.make_async_copy(w_hbm, w_ref, fsem.at[0]), pltpu.make_async_copy(x_hbm, x_ref, fsem.at[1])]
        written = []

        def resid(k):
            return pltpu.make_async_copy(r_hbm.at[pl.ds(k * tile, tile)], r_ref.at[k % 2], fsem.at[2 + tiles + k])

        def finish_tile(k):
            if k == 0:
                s1_ref[...] = jnp.zeros_like(s1_ref)
                for cp in held:
                    cp.wait()
            r = pl.ds(k * tile, tile)
            resid(k).wait()
            dn = nn(lbuf[qkv % 2, r, 0:width], w_ref[0:width, :])
            for part in range(1, 3):
                span = slice(part * width, (part + 1) * width)
                dn = dn + nn(lbuf[qkv % 2, r, span], w_ref[span, :])
            hat, rstd = row_stats(x_ref[r, :].astype(F32))
            x_ref[r, :] = (r_ref[k % 2] + norm_back(dn * vec_ref[4:5, :], hat, rstd)).astype(BF16)
            if k + 2 < tiles:
                resid(k + 2).start()
            s1_ref[0:1, :] += col_sum(dn * hat)
            s1_ref[1:2, :] += col_sum(dn)
            cp = pltpu.make_async_copy(x_ref.at[r], g_hbm.at[r], fsem.at[2 + k])
            cp.start()
            written.append(cp)
            if k == tiles - 1:
                load(qkv + 2)

        load(0)
        load(1)
        for cp in held + [resid(0), resid(1)]:
            cp.start()
        pl.semaphore_wait(barrier, len(peers))
        does = {"compute": compute, "sib": stage_sib, "y": stage_y, "x": stage_x, "z": stage_z, "out": stage_out,
                "finish": finish_tile, "pack": pack_step}
        for kind, i in steps:
            does[kind](i)
        for cp in started:
            cp.wait_send()
        for cp in written:
            cp.wait()

    any_spec = pl.BlockSpec(memory_space=pl.ANY)
    vm = pl.BlockSpec(memory_space=pltpu.VMEM)

    def per_weight(make):
        return [pltpu.VMEM(make(width // b, shard_rows[w], cuts[w], b), BF16) for w, b in enumerate(blocks)]

    tiles = n // tile
    scratch = [pltpu.VMEM((n, width), BF16), pltpu.VMEM((2, tile, width), F32), pltpu.VMEM(qkv_t.shape, BF16),
               pltpu.VMEM((8, width), F32), pltpu.SemaphoreType.DMA((2 + 2 * tiles,)),
               pltpu.VMEM((2, n, max_left), BF16), pltpu.VMEM((2, n, width), BF16)]
    scratch += per_weight(lambda j, rw, a, b: (j, 2, 2, nz, rw, b))
    scratch += per_weight(lambda j, rw, a, b: (j, 2, nz, rw, b))
    scratch += per_weight(lambda j, rw, a, b: (j, 2, nz, a, b))
    scratch += per_weight(lambda j, rw, a, b: (j, nz, rw - a, b))
    scratch += per_weight(lambda j, rw, a, b: (j, nz - 1, rw - a, b))
    scratch += per_weight(lambda j, rw, a, b: (j, rw - a, b))
    scratch += per_weight(lambda j, rw, a, b: (j, rw - a, b))
    scratch += [
        pltpu.VMEM((2, 6, 16, 1024), F32),
        pltpu.SemaphoreType.DMA((ni, 3 + nz)), pltpu.SemaphoreType.DMA((ni, 3 + nz)),
        pltpu.SemaphoreType.DMA((6,)), pltpu.SemaphoreType.DMA((6,)), pltpu.SemaphoreType.DMA((nw, 4)),
    ]
    outs = pl.pallas_call(
        kernel,
        out_shape=[jax.ShapeDtypeStruct((rw, width), F32) for rw in shard_rows]
        + [jax.ShapeDtypeStruct((16, 1024), F32), jax.ShapeDtypeStruct((n, width), BF16)],
        in_specs=[any_spec] * (len(lefts) + nw + 3) + [vm] * 6,
        out_specs=[vm] * (nw + 1) + [any_spec],
        scratch_shapes=scratch,
        compiler_params=pltpu.CompilerParams(
            collective_id=collective, has_side_effects=True, vmem_limit_bytes=63 << 20),
        name="finish_reduce",
    )(*lefts, *rights, tokens, resid_grad, qkv_t, vecs, *sums)
    return outs[:nw], outs[nw], outs[nw + 1]


def sum_rows(s1, bq, bv, s768, sff, sal):
    lines = [bq[0:1], bv[0:1], s768[1:2], s768[0:1], s1[0:1], s1[1:2], s768[2:3], s768[3:4], sal[0:1]]
    lines += [sff[0:1, k:k + 1024] for k in range(0, sff.shape[1], 1024)]
    return [(row, v.shape[1], v) for row, v in enumerate(lines)]


def reduce_all(pairs, tokens, resid_grad, vecs, qkv_t, sums, fast):
    if fast:
        left_rows = [sum(a.shape[1] for a in ls) for ls, _ in pairs]
        shard_rows = [r // 16 for r in left_rows]
        cuts = [max(16, (r * 5 // 16) // 16 * 16) for r in shard_rows]
        blocks = [384, 256, 256, 256, 384]
        return finish_and_reduce(pairs, tokens, resid_grad, vecs, qkv_t, sums, shard_rows, cuts, blocks, 4, 1)
    grad_tokens, s1 = finish(tokens, resid_grad, *pairs[2][0], vecs, qkv_t)
    terms = [jnp.concatenate([tn(a, r).astype(BF16) for a in ls], 0) for ls, r in pairs]
    got = [lax.psum(lax.psum_scatter(t, "fsdp", scatter_dimension=0, tiled=True), "dp").astype(F32) for t in terms]
    lines = [jnp.pad(v, ((0, 0), (0, 1024 - k))) for _, k, v in sum_rows(s1, *sums)]
    pack = jnp.pad(jnp.concatenate(lines, 0), ((0, 16 - len(lines)), (0, 0)))
    return got, lax.psum(pack, ("dp", "fsdp")), grad_tokens


def per_device(mesh_shape, *args):
    (tokens, segment_ids, padding, qkv_weight, query_bias, value_bias, out_weight, out_bias,
     first_gain, first_shift, second_gain, second_shift, up_weight, up_bias, down_weight, down_bias,
     align_weight, align_bias, grad_output, grad_aligned) = args
    n, d = tokens.shape
    small = [query_bias, value_bias, out_bias, down_bias, first_gain, first_shift, second_gain, second_shift]
    members = mesh_shape["fsdp"]
    own, ub, ab = query_bias.shape[0], up_bias.shape[0], align_bias.shape[0]
    ff, al = ub * members, ab * members
    fast = mesh_shape["dp"] == 2 and members == 16

    seg = segment_ids[0]
    pad_row = padding[0]
    keys = jnp.where(pad_row == 0, seg, -1)
    valid_col = (1.0 - pad_row.astype(F32))[:, None]
    wins = windows(seg, 256)

    if fast:
        nz = members // 4
        lines = [v[None] for v in small] + [up_bias[None, :128], up_bias[None, 128:], align_bias[None]]
        pack = sum(jnp.pad(v, ((k, 47 - k), (0, 128 - v.shape[1]))) for k, v in enumerate(lines))
        normed, qkv, vecs, mixed, lse, packs, full = gather_attend(
            tokens, pack, [qkv_weight.T, out_weight, align_weight.T, up_weight.T, down_weight],
            seg[:, None], keys[None, :], own, nz)
        qkv_t, out_w, align_t, up_t, down_w = full
        up_b = packs[:, 8:10].reshape(members, 256)[:, :ub].reshape(1, ff).astype(F32)
        align_b = packs[:, 10, :ab].reshape(1, al).astype(F32)
    else:
        def gathered(a):
            return lax.all_gather(a, "fsdp", axis=0, tiled=True)

        qkv_t, out_w, up_t, down_w, align_t = [
            gathered(a) for a in (qkv_weight.T, out_weight, up_weight.T, down_weight, align_weight.T)]
        vecs = jnp.stack([gathered(v) for v in small]).astype(F32)
        up_b = gathered(up_bias).astype(F32)[None]
        align_b = gathered(align_bias).astype(F32)[None]
        qkv_b = jnp.concatenate([vecs[0:1], jnp.zeros((1, d), F32), vecs[1:2]], 1)
        normed, qkv = project(tokens, vecs, qkv_b, qkv_t)
        mixed, lse = attend(qkv, seg[:, None], keys[None, :], wins)
    (n2, act, du, gb, block_out, aligned, res, rb, dm, s768, sff, sal) = middle(
        tokens, mixed, grad_output, grad_aligned, valid_col, vecs, up_b, align_b, out_w, up_t, down_w, align_t)
    dq, dk, dv, bq, bv = attend_back(qkv, mixed, dm, lse, seg[None, :], keys[:, None], wins)
    pairs = [([grad_aligned], block_out), ([act], gb), ([dq, dk, dv], normed), ([du], n2), ([mixed], rb)]
    (g_align, g_down, g_qkv, g_up, g_out), pack, grad_tokens = reduce_all(
        pairs, tokens, res, vecs, qkv_t, (bq, bv, s768, sff, sal), fast)
    me = lax.axis_index("fsdp")
    vec = lax.dynamic_slice(pack, (0, me * own), (8, own))
    g_ub = lax.dynamic_slice(pack[9:9 + ff // 1024].reshape(ff), (me * ub,), (ub,))
    g_ab = lax.dynamic_slice(pack[8], (me * ab,), (ab,))
    return (block_out, aligned, grad_tokens, g_qkv.T, vec[0], vec[1], g_out, vec[2], vec[4], vec[5], vec[6],
            vec[7], g_up.T, g_ub, g_down, vec[3], g_align.T, g_ab)


def solution(mesh):
    rows_spec = P(("dp", "fsdp"), None)
    vec, by_col, by_row = P("fsdp"), P(None, "fsdp"), P("fsdp", None)
    in_specs = (rows_spec, rows_spec, rows_spec, by_col, vec, vec, by_row, vec, vec, vec, vec, vec,
                by_col, vec, by_row, vec, by_col, vec, rows_spec, rows_spec)
    out_specs = (rows_spec, rows_spec, rows_spec, by_col, vec, vec, by_row, vec, vec, vec, vec, vec,
                 by_col, vec, by_row, vec, by_col, vec)
    return jax.shard_map(functools.partial(per_device, dict(mesh.shape)), mesh=mesh, in_specs=in_specs,
                         out_specs=out_specs, check_vma=False)
```

```python
import functools

import jax
import jax.numpy as jnp
from jax import lax
from jax.experimental import pallas as pl
from jax.experimental.pallas import tpu as pltpu
from jax.sharding import PartitionSpec as P

HEADS = 12
F32 = jnp.float32
BF16 = jnp.bfloat16
NEG = -1e30


def nn(a, b):
    return lax.dot_general(a, b, (((1,), (0,)), ((), ())), preferred_element_type=F32)


def nt(a, b):
    return lax.dot_general(a, b, (((1,), (1,)), ((), ())), preferred_element_type=F32)


def tn(a, b):
    return lax.dot_general(a, b, (((0,), (0,)), ((), ())), preferred_element_type=F32)


def col_sum(v):
    return jnp.sum(v, 0, keepdims=True)


def gelu_parts(u):
    z = jnp.abs(u) * (0.5 ** 0.5)
    ez = jnp.exp(-(z * z))
    t = 1.0 / (1.0 + 0.33 * z)
    poly = -0.13593485572044933
    for coef in (0.46271278142719047, -0.3554798541586114, 0.412577688277986, 0.044992638979585504,
                 0.2019288303128453, 0.18283654298343202, 0.18636614548593147):
        poly = poly * t + coef
    half_erfc = (0.5 * t) * poly * ez
    cdf = jnp.where(u > 0, 1.0 - half_erfc, half_erfc)
    return u * cdf, cdf + u * ez * 0.3989422804014327


def row_stats(x):
    mean = jnp.mean(x, -1, keepdims=True)
    centered = x - mean
    rstd = lax.rsqrt(jnp.mean(centered * centered, -1, keepdims=True) + 1e-05)
    return centered * rstd, rstd


def norm_back(grad_hat, hat, rstd):
    return rstd * (grad_hat - jnp.mean(grad_hat, -1, keepdims=True)
                   - hat * jnp.mean(grad_hat * hat, -1, keepdims=True))


def call(kernel, grid, ins, outs, scratch=(), name=None, prefetch=(), limit=60):
    return pl.pallas_call(
        kernel,
        grid_spec=pltpu.PrefetchScalarGridSpec(
            num_scalar_prefetch=len(prefetch), grid=grid,
            in_specs=[pl.BlockSpec(b, m, **({"pipeline_mode": pl.Buffered(1)} if once else {}))
                      for _, b, m, once in ins],
            out_specs=[pl.BlockSpec(b, m) for _, _, b, m in outs],
            scratch_shapes=list(scratch)),
        out_shape=[jax.ShapeDtypeStruct(s, d) for s, d, _, _ in outs],
        compiler_params=pltpu.CompilerParams(
            dimension_semantics=("arbitrary",) * len(grid), vmem_limit_bytes=limit << 20),
        name=name,
    )(*prefetch, *[a for a, _, _, _ in ins])


def whole(a):
    n = a.ndim
    return (a, a.shape, lambda *_: (0,) * n, True)


def rows(a, tile):
    return (a, (tile, a.shape[1]), lambda i, *_: (i, 0), False)


def rows_out(n, width, dtype, tile):
    return ((n, width), dtype, (tile, width), lambda i, *_: (i, 0))


def fixed_out(shape, dtype):
    n = len(shape)
    return (shape, dtype, shape, lambda *_: (0,) * n)


def project(tokens, vecs, qkv_bias, qkv_t, tile=256):
    n, d = tokens.shape

    def kernel(x_ref, v_ref, b_ref, w_ref, n_ref, o_ref):
        hat, _ = row_stats(x_ref[...].astype(F32))
        low = (hat * v_ref[4:5, :] + v_ref[5:6, :]).astype(BF16)
        n_ref[...] = low
        for part in range(3):
            cols = pl.ds(part * d, d)
            o_ref[:, cols] = (nt(low, w_ref[cols, :]) + b_ref[:, cols]).astype(BF16)

    return call(
        kernel, (n // tile,),
        [rows(tokens, tile), whole(vecs), whole(qkv_bias), whole(qkv_t)],
        [rows_out(n, d, BF16, tile), rows_out(n, 3 * d, BF16, tile)],
        name="project")


def pair_masks(shape):
    lane = lax.broadcasted_iota(jnp.int32, shape, 1)
    return lane < 64


def windows(seg, tile, step=256):
    n = seg.shape[0]
    first = seg[::tile]
    last = seg[tile - 1::tile]
    lo = jnp.sum(seg[None, :] < first[:, None], 1, dtype=jnp.int32) // 128 * 128
    hi = jnp.sum(seg[None, :] <= last[:, None], 1, dtype=jnp.int32)
    count = (hi - lo + step - 1) // step
    return jnp.stack([jnp.minimum(lo, n - count * step), count])


def fill_mask(mask, rows_ref, cols_ref, n, tile=256):
    @pl.when(pl.program_id(0) == 0)
    def _():
        @pl.loop(0, n // tile)
        def _(t):
            r = pl.ds(pl.multiple_of(t * tile, tile), tile)
            row_id = t * tile + lax.broadcasted_iota(jnp.int32, (tile, n), 0)
            col_id = lax.broadcasted_iota(jnp.int32, (tile, n), 1)
            keep = (rows_ref[r, :] == cols_ref[...]) | (row_id == col_id)
            mask[r, :] = jnp.where(keep, 0.0, NEG).astype(F32)


def attend(qkv, seg_col, key_row, wins, tq=256, step=256):
    n = qkv.shape[0]
    d = qkv.shape[1] // 3
    pairs = d // 128

    def kernel(win, q_ref, k_ref, v_ref, sc_ref, kr_ref, o_ref, lse_ref, mask, va, vb):
        fill_mask(mask, sc_ref, kr_ref, n)
        v = v_ref[...]
        low_half = pair_masks((n, 128))
        zero = jnp.zeros_like(v)
        va[...] = jnp.where(low_half, v, zero)
        vb[...] = jnp.where(low_half, zero, v)
        half = pair_masks((tq, 128))

        @pl.loop(0, n // tq)
        def _(t):
            r = pl.ds(pl.multiple_of(t * tq, tq), tq)
            first = pl.multiple_of(win[0, t], 128)

            for count in range(1, n // step + 1):
                @pl.when(win[1, t] == count)
                def _():
                    keys = pl.ds(first, count * step)
                    q = q_ref[r, :] * jnp.asarray(0.125, BF16)
                    qz = jnp.zeros_like(q)
                    kk = k_ref[keys, :]
                    outs, tops, sums = [], [], []
                    for qh, vh in ((jnp.where(half, q, qz), va), (jnp.where(half, qz, q), vb)):
                        s = nt(qh, kk) + mask[r, keys]
                        top = jnp.max(s, 1, keepdims=True)
                        p = jnp.exp(s - top)
                        sums.append(jnp.sum(p, 1, keepdims=True))
                        tops.append(top)
                        outs.append(nn(p.astype(BF16), vh[keys, :]))
                    (la, lb), (ma, mb) = sums, tops
                    o_ref[r, :] = ((outs[0] + outs[1]) * jnp.where(half, 1.0 / la, 1.0 / lb)).astype(BF16)
                    lse = jnp.where(half, ma + jnp.log(la), mb + jnp.log(lb)).T
                    lse_ref[0:1, r] = lse[0:1, :]
                    lse_ref[1:2, r] = lse[64:65, :]

    def block(first):
        return (qkv, (n, 128), lambda p, *_: (0, first * pairs + p), False)

    return call(
        kernel, (pairs,),
        [block(0), block(1), block(2), whole(seg_col), whole(key_row)],
        [((n, d), BF16, (n, 128), lambda p, *_: (0, p)),
         ((8 * pairs, n), F32, (8, n), lambda p, *_: (p, 0))],
        [pltpu.VMEM((n, n), F32), pltpu.VMEM((n, 128), BF16), pltpu.VMEM((n, 128), BF16)],
        name="attend", prefetch=(wins,))


def attend_back(qkv, mixed, grad_mixed, lse, seg_row, key_col, wins, tk=256, step=256):
    n = qkv.shape[0]
    d = qkv.shape[1] // 3
    pairs = d // 128

    def kernel(win, q_ref, k_ref, v_ref, o_ref, g_ref, lse_ref, sr_ref, kc_ref,
               dq_ref, dk_ref, dv_ref, bq_ref, bv_ref, mask, qa, qb, ga, gb, kt, dots, dqt):
        fill_mask(mask, kc_ref, sr_ref, n)
        half = pair_masks((n, 128))
        q = q_ref[...] * jnp.asarray(0.125, BF16)
        zero = jnp.zeros_like(q)
        qa[...] = jnp.where(half, q, zero)
        qb[...] = jnp.where(half, zero, q)
        g = g_ref[...]
        ga[...] = jnp.where(half, g, zero)
        gb[...] = jnp.where(half, zero, g)
        kt[...] = k_ref[...].astype(F32).T.astype(BF16)
        prod = (g.astype(F32) * o_ref[...].astype(F32)).T
        dots[0:1, :] = col_sum(prod[:64])
        dots[1:2, :] = col_sum(prod[64:])
        dqt[...] = jnp.zeros_like(dqt)

        @pl.loop(0, n // tk)
        def _(t):
            keys = pl.ds(pl.multiple_of(t * tk, tk), tk)
            first = pl.multiple_of(win[0, t], 128)

            for count in range(1, n // step + 1):
                @pl.when(win[1, t] == count)
                def _():
                    kk = k_ref[keys, :]
                    vv = v_ref[keys, :]
                    dk = dv = None
                    for e in range(count):
                        cols = pl.ds(pl.multiple_of(first + e * step, 128), step)
                        m = mask[keys, cols]
                        for h, (qh, gh) in enumerate(((qa, ga), (qb, gb))):
                            qq = qh[cols, :]
                            gg = gh[cols, :]
                            p = jnp.exp(nt(kk, qq) + m - lse_ref[h:h + 1, cols])
                            ds = (p * (nt(vv, gg) - dots[h:h + 1, cols])).astype(BF16)
                            pv = nn(p.astype(BF16), gg)
                            pk = nn(ds, qq)
                            dv = pv if dv is None else dv + pv
                            dk = pk if dk is None else dk + pk
                            part = pl.ds(64 * h, 64)
                            dqt[part, cols] += nn(kt[part, keys], ds)
                    dk_ref[keys, :] = dk.astype(BF16)
                    dv_ref[keys, :] = dv.astype(BF16)

        dq = (dqt[...].T * 0.125).astype(BF16)
        dq_ref[...] = dq
        bq_ref[...] = jnp.broadcast_to(col_sum(dq.astype(F32)), (8, 128))
        bv_ref[...] = jnp.broadcast_to(col_sum(dv_ref[...].astype(F32)), (8, 128))

    def block(a, first=0):
        return (a, (n, 128), lambda p, *_: (0, first * pairs + p), False)

    cols = ((n, d), BF16, (n, 128), lambda p, *_: (0, p))
    sums = ((8, d), F32, (8, 128), lambda p, *_: (0, p))
    return call(
        kernel, (pairs,),
        [block(qkv, 0), block(qkv, 1), block(qkv, 2), block(mixed), block(grad_mixed),
         (lse, (8, n), lambda p, *_: (p, 0), False), whole(seg_row), whole(key_col)],
        [cols, cols, cols, sums, sums],
        [pltpu.VMEM((n, n), F32)] + [pltpu.VMEM((n, 128), BF16)] * 4
        + [pltpu.VMEM((128, n), BF16), pltpu.VMEM((8, n), F32), pltpu.VMEM((128, n), F32)],
        name="attend_back", prefetch=(wins,))


def middle(tokens, mixed, grad_output, grad_aligned, valid_col, vecs, up_b, align_b,
           out_w, up_t, down_w, align_t, tile=256, chunk=768):
    n, d = tokens.shape
    ff, al = up_t.shape[0], align_t.shape[0]

    def kernel(x_ref, m_ref, go_ref, ga_ref, v_ref, vec_ref, ub_ref, ab_ref, wo_ref, wu_ref, wd_ref, wa_ref,
               n_ref, act_ref, du_ref, gb_ref, out_ref, al_ref, r_ref, rb_ref, dm_ref,
               s768_ref, sff_ref, sal_ref, branch, dn):
        @pl.when(pl.program_id(0) == 0)
        def _():
            s768_ref[...] = jnp.zeros_like(s768_ref)
            sff_ref[...] = jnp.zeros_like(sff_ref)
            sal_ref[...] = jnp.zeros_like(sal_ref)

        resid = x_ref[...].astype(F32) + nn(m_ref[...], wo_ref[...]) + vec_ref[2:3, :]
        hat, rstd = row_stats(resid)
        low = (hat * vec_ref[6:7, :] + vec_ref[7:8, :]).astype(BF16)
        n_ref[...] = low
        valid = v_ref[...]
        ga = ga_ref[...]
        sal_ref[0:1, :] += col_sum(ga.astype(F32))
        grad = valid * (go_ref[...].astype(F32) + nn(ga, wa_ref[...]))
        gb = grad.astype(BF16)
        gb_ref[...] = gb
        branch[...] = jnp.zeros_like(branch)
        dn[...] = jnp.zeros_like(dn)

        @pl.loop(0, ff // chunk)
        def _(t):
            part = pl.ds(pl.multiple_of(t * chunk, chunk), chunk)
            wu = wu_ref[part, :]
            wd = wd_ref[part, :]
            act, slope = gelu_parts(nt(n_ref[...], wu) + ub_ref[0:1, part])
            act = act.astype(BF16)
            act_ref[:, part] = act
            branch[...] += nn(act, wd)
            du = slope * nt(gb_ref[...], wd)
            du = du.astype(BF16)
            du_ref[:, part] = du
            sff_ref[0:1, part] += col_sum(du.astype(F32))
            dn[...] += nn(du, wu)

        out = (valid * (resid + branch[...] + vec_ref[3:4, :])).astype(BF16)
        out_ref[...] = out
        al_ref[...] = (nt(out, wa_ref[...]) + ab_ref[...]).astype(BF16)
        dn2 = dn[...]
        res = grad + norm_back(dn2 * vec_ref[6:7, :], hat, rstd)
        r_ref[...] = res
        rb = res.astype(BF16)
        rb_ref[...] = rb
        dm_ref[...] = nt(rb, wo_ref[...]).astype(BF16)
        s768_ref[0:1, :] += col_sum(gb.astype(F32))
        s768_ref[1:2, :] += col_sum(rb.astype(F32))
        s768_ref[2:3, :] += col_sum(dn2 * hat)
        s768_ref[3:4, :] += col_sum(dn2)

    r = functools.partial(rows_out, n, tile=tile)
    return call(
        kernel, (n // tile,),
        [rows(tokens, tile), rows(mixed, tile), rows(grad_output, tile), rows(grad_aligned, tile),
         rows(valid_col, tile), whole(vecs), whole(up_b), whole(align_b), whole(out_w), whole(up_t),
         whole(down_w), whole(align_t)],
        [r(d, BF16), r(ff, BF16), r(ff, BF16), r(d, BF16), r(d, BF16), r(al, BF16), r(d, F32), r(d, BF16),
         r(d, BF16), fixed_out((8, d), F32), fixed_out((8, ff), F32), fixed_out((8, al), F32)],
        [pltpu.VMEM((tile, d), F32), pltpu.VMEM((tile, d), F32)],
        name="middle")


def finish(tokens, resid_grad, dq, dk, dv, vecs, qkv_t, tile=256):
    n, d = tokens.shape

    def kernel(x_ref, r_ref, dq_ref, dk_ref, dv_ref, vec_ref, w_ref, o_ref, s_ref):
        @pl.when(pl.program_id(0) == 0)
        def _():
            s_ref[...] = jnp.zeros_like(s_ref)

        dn = nn(dq_ref[...], w_ref[0:d, :]) + nn(dk_ref[...], w_ref[d:2 * d, :]) + nn(dv_ref[...], w_ref[2 * d:, :])
        hat, rstd = row_stats(x_ref[...].astype(F32))
        o_ref[...] = (r_ref[...] + norm_back(dn * vec_ref[4:5, :], hat, rstd)).astype(BF16)
        s_ref[0:1, :] += col_sum(dn * hat)
        s_ref[1:2, :] += col_sum(dn)

    return call(
        kernel, (n // tile,),
        [rows(tokens, tile), rows(resid_grad, tile), rows(dq, tile), rows(dk, tile), rows(dv, tile),
         whole(vecs), whole(qkv_t)],
        [rows_out(n, d, BF16, tile), fixed_out((8, d), F32)],
        name="finish")
MESHID = pl.DeviceIdType.MESH


def coords():
    y = lax.axis_index("dp")
    f = lax.axis_index("fsdp")
    return y, f // 4, lax.rem(f // 2, 2), lax.rem(f, 2)


def at_rows(first, count):
    return pl.ds(pl.multiple_of(first, 16), count)


class Gather:
    def __init__(self, items, nz, ssem, rsem, lsem):
        self.items, self.nz, self.ssem, self.rsem, self.lsem = items, nz, ssem, rsem, lsem
        self.y, self.z, self.x, self.c = coords()

    def device(self, y=None, z=None, x=None, c=None):
        pick = [own if new is None else new for own, new in zip((self.y, self.z, self.x, self.c), (y, z, x, c))]
        return (pick[0], pick[1] * 4 + pick[2] * 2 + pick[3])

    def ahead(self, d):
        return lax.rem(self.z + d, self.nz)

    def enter(self):
        barrier = pltpu.get_barrier_semaphore()
        peers = [self.device(c=1 - self.c), self.device(x=1 - self.x), self.device(y=1 - self.y)]
        peers += [self.device(z=self.ahead(d)) for d in range(1, self.nz)]
        for peer in peers:
            pl.semaphore_signal(barrier, inc=1, device_id=peer, device_id_type=MESHID)
        pl.semaphore_wait(barrier, len(peers))

    def span(self, i, which):
        _, _, lo, n, third = self.items[i]
        return {"all": (lo, n), "plane": (lo + self.y * third, n - third),
                "mine": (lo + self.y * (n - third), third)}[which]

    def local(self, i):
        own, full = self.items[i][:2]
        r = at_rows(*self.span(i, "plane"))
        return pltpu.make_async_copy(own.at[r], full.at[self.z, self.x, self.c, r], self.lsem.at[i])

    def copy(self, i, k):
        own, full = self.items[i][:2]
        every = pl.ds(0, self.nz)
        if k == 0:
            ref = full.at[every, self.x, self.c, at_rows(*self.span(i, "plane"))]
            src, to = ref, self.device(x=1 - self.x)
        elif k == 1:
            ref = full.at[every, :, self.c, at_rows(*self.span(i, "mine"))]
            src, to = ref, self.device(y=1 - self.y)
        elif k == 2:
            ref = full.at[every, :, self.c, at_rows(*self.span(i, "all"))]
            src, to = ref, self.device(c=1 - self.c)
        else:
            r = at_rows(*self.span(i, "plane"))
            src, ref, to = own.at[r], full.at[self.z, self.x, self.c, r], self.device(z=self.ahead(k - 2))
        return pltpu.make_async_remote_copy(
            src_ref=src, dst_ref=ref, send_sem=self.ssem.at[i, k], recv_sem=self.rsem.at[i, k],
            device_id=to, device_id_type=MESHID)

    def start(self, i):
        self.local(i).start()
        for d in range(1, self.nz):
            self.copy(i, 2 + d).start()

    def pass_z(self, i):
        for d in range(1, self.nz):
            self.copy(i, 2 + d).wait_recv()
        self.local(i).wait()
        self.copy(i, 0).start()

    def pass_x(self, i):
        self.copy(i, 0).wait_recv()
        self.copy(i, 1).start()

    def pass_y(self, i):
        self.copy(i, 1).wait_recv()
        self.copy(i, 2).start()

    def ready(self, i):
        self.copy(i, 2).wait_recv()

    def leave(self):
        for i in range(len(self.items)):
            for k in range(2 + self.nz):
                self.copy(i, k).wait_send()

    def events(self, link, hop):
        sizes = [full.shape[-1] * n for _, full, _, n, _ in self.items]
        out = []
        z = x = y = 0.0
        for i, size in enumerate(sizes):
            t = link * size / sum(sizes)
            z += t
            x = max(x, z + hop) + t
            y = max(y, x + hop) + t
            out += [(z + hop, self.pass_z, i), (x + hop, self.pass_x, i), (y + hop, self.pass_y, i),
                    (y + 2 * hop + t / 4, self.ready, i)]
        return sorted(out, key=lambda e: (e[0], e[2]))


def gather_attend(tokens, pack, shards, seg_col, key_row, own, nz, tile=512, tq=256, link=62.0, hop=2.0,
                  start=5.0, slots=(4.8, 1.45)):
    n, d = tokens.shape
    members = 4 * nz
    pairs = d // 128
    heights = [s.shape[0] for s in shards]
    cuts = [(1 + w, lo, min(48, h - lo) if h != 64 else 64) for w, h in enumerate(heights)
            for lo in range(0, h if h != 64 else 1, 48)]
    cuts = [(0, 0, pack.shape[0])] + cuts
    first_use = 1 + len([c for c in cuts if c[0] == 1])
    ni = len(cuts)

    def kernel(x_ref, sc_ref, kr_ref, p_ref, *refs):
        owns = (p_ref,) + refs[:5]
        n_ref, qkv_ref, vec_ref, o_ref, lse_ref = refs[5:10]
        fulls = refs[10:16]
        mask, va, vb, ssem, rsem, lsem = refs[16:]
        packs_ref, w_ref = fulls[:2]
        g = Gather([(owns[w], fulls[w], lo, k, max(16, k // 3 // 16 * 16)) for w, lo, k in cuts], nz, ssem, rsem, lsem)
        g.enter()
        for i in range(ni):
            g.start(i)

        @pl.loop(0, n // tq)
        def _(t):
            r = pl.ds(pl.multiple_of(t * tq, tq), tq)
            row_id = t * tq + lax.broadcasted_iota(jnp.int32, (tq, n), 0)
            col_id = lax.broadcasted_iota(jnp.int32, (tq, n), 1)
            keep = (sc_ref[r, :] == kr_ref[...]) | (row_id == col_id)
            mask[r, :] = jnp.where(keep, 0.0, NEG).astype(F32)

        events = g.events(link, hop)
        now = start + max(t for t, f, i in events if i < first_use and f == g.ready)

        def pump(until):
            while events and start + events[0][0] <= until:
                _, f, i = events.pop(0)
                f(i)

        pump(now)
        plan = []
        for k in range(n // tile + pairs * (n // tq)):
            now += slots[0] if k < n // tile else slots[1]
            mark = len([e for e in events if start + e[0] <= now])
            plan.append(events[:mark])
            del events[:mark]
        total = jnp.zeros((16, d), F32)
        row = lax.broadcasted_iota(jnp.int32, (128, d), 0)
        col = lax.broadcasted_iota(jnp.int32, (128, d), 1)
        for s in range(members):
            place = jnp.where((col == row + s * own) & (row < own), 1.0, 0.0).astype(BF16)
            total = total + nn(packs_ref[s // 4, s // 2 % 2, s % 2, 0:16, :], place)
        vec_ref[...] = total[:8]
        part = 3 * d // 2
        gap = jnp.zeros((1, d // 2), F32)
        biases = [jnp.concatenate([vec_ref[0:1, :], gap], 1), jnp.concatenate([gap, vec_ref[1:2, :]], 1)]

        @pl.loop(0, n // tile)
        def _(t):
            r = pl.ds(pl.multiple_of(t * tile, tile), tile)
            hat, _ = row_stats(x_ref[r, :].astype(F32))
            n_ref[r, :] = (hat * vec_ref[4:5, :] + vec_ref[5:6, :]).astype(BF16)
            for k in range(2):
                w = w_ref[k * (nz // 2):(k + 1) * (nz // 2)].reshape(part, d)
                qkv_ref[r, k * part:(k + 1) * part] = (nt(n_ref[r, :], w) + biases[k]).astype(BF16)
            for k in range(n // tile):
                if plan[k]:
                    @pl.when(t == k)
                    def _():
                        for _, f, i in plan[k]:
                            f(i)

        pumped = plan[n // tile:]
        low_half = pair_masks((n, 128))
        half = pair_masks((tq, 128))
        tiles = n // tq

        @pl.loop(0, pairs)
        def _(p):
            def cols(k):
                return pl.ds(pl.multiple_of(k * d + p * 128, 128), 128)

            v = qkv_ref[:, cols(2)]
            zero = jnp.zeros_like(v)
            va[...] = jnp.where(low_half, v, zero)
            vb[...] = jnp.where(low_half, zero, v)

            @pl.loop(0, tiles)
            def _(t):
                r = pl.ds(pl.multiple_of(t * tq, tq), tq)
                q = qkv_ref[r, cols(0)] * jnp.asarray(0.125, BF16)
                qz = jnp.zeros_like(q)
                kk = qkv_ref[:, cols(1)]
                outs, tops, sums = [], [], []
                for qh, vh in ((jnp.where(half, q, qz), va), (jnp.where(half, qz, q), vb)):
                    s = nt(qh, kk) + mask[r, :]
                    top = jnp.max(s, 1, keepdims=True)
                    e = jnp.exp(s - top)
                    sums.append(jnp.sum(e, 1, keepdims=True))
                    tops.append(top)
                    outs.append(nn(e.astype(BF16), vh[...]))
                (la, lb), (ma, mb) = sums, tops
                o_ref[r, cols(0)] = ((outs[0] + outs[1]) * jnp.where(half, 1.0 / la, 1.0 / lb)).astype(BF16)
                lse = jnp.where(half, ma + jnp.log(la), mb + jnp.log(lb)).T
                lse_ref[p, 0:1, r] = lse[0:1, :]
                lse_ref[p, 1:2, r] = lse[64:65, :]
                for k, step in enumerate(pumped):
                    if step:
                        @pl.when(p * tiles + t == k)
                        def _():
                            for _, f, i in step:
                                f(i)

        for _, f, i in events:
            f(i)
        g.leave()

    vm = pl.BlockSpec(memory_space=pltpu.VMEM)
    hbm = pl.BlockSpec(memory_space=pl.ANY)
    sds = jax.ShapeDtypeStruct

    def full(h, width):
        return sds((nz, 2, 2, h, width), BF16)

    outs = pl.pallas_call(
        kernel,
        out_shape=[sds((n, d), BF16), sds((n, 3 * d), BF16), sds((8, d), F32), sds((n, d), BF16),
                   sds((pairs, 8, n), F32), full(pack.shape[0], 128)] + [full(h, d) for h in heights],
        in_specs=[vm] * 9, out_specs=[vm] * 7 + [hbm] * 4,
        scratch_shapes=[pltpu.VMEM((n, n), F32), pltpu.VMEM((n, 128), BF16), pltpu.VMEM((n, 128), BF16),
                        pltpu.SemaphoreType.DMA((ni, 2 + nz)), pltpu.SemaphoreType.DMA((ni, 2 + nz)),
                        pltpu.SemaphoreType.DMA((ni,))],
        compiler_params=pltpu.CompilerParams(collective_id=0, has_side_effects=True, vmem_limit_bytes=60 << 20),
        name="gather_attend",
    )(tokens, seg_col, key_row, pack, *shards)
    normed, qkv, vecs, mixed, lse, packs = outs[:6]
    return (normed, qkv, vecs, mixed, lse.reshape(8 * pairs, n), packs.reshape(members, -1, 128),
            [w.reshape(-1, d) for w in outs[6:]])


def plan_steps(count, tiles, first_tile, hops, lags):
    steps = []
    for t in range(max(count + max(lags), first_tile + tiles + hops + 1)):
        stages = [(t - lag, kind) for kind, lag in zip(("compute", "sib", "y", "x", "z", "out"), (0,) + lags)]
        steps += [(kind, i) for i, kind in stages if 0 <= i < count]
        k = t - first_tile
        if 0 <= k < tiles:
            steps.append(("finish", k))
        elif 0 <= k - tiles <= hops:
            steps.append(("pack", k - tiles))
    return steps


def finish_and_reduce(pairs, tokens, resid_grad, vecs, qkv_t, sums, shard_rows, cuts, blocks, nz, collective, tile=256,
                      qkv=2, first_tile=7, lags=(1, 3, 5, 7, 8)):
    nw = len(pairs)
    lefts = [a for ls, _ in pairs for a in ls]
    rights = [r for _, r in pairs]
    n = rights[0].shape[0]
    width = rights[0].shape[1]
    max_left = max(sum(a.shape[1] for a in ls) for ls, _ in pairs)
    items = [(w, j) for w in range(nw) for j in range(width // blocks[w])]
    ni = len(items)
    first_tile = max(max(i for i, (w, _) in enumerate(items) if w == qkv), first_tile)
    steps = plan_steps(ni, n // tile, first_tile, 5, lags)

    def kernel(*refs):
        left_refs = refs[:len(lefts)]
        right_refs = refs[len(lefts):len(lefts) + nw]
        pos = len(lefts) + nw
        x_hbm, r_hbm, w_hbm, vec_ref = refs[pos:pos + 4]
        sum_refs = refs[pos + 4:pos + 9]
        pos += 9
        out_refs = refs[pos:pos + nw]
        pack_out, g_hbm = refs[pos + nw:pos + nw + 2]
        pos += 2 + nw
        x_ref, r_ref, w_ref, s1_ref, fsem = refs[pos:pos + 5]
        pos += 5
        lbuf, rbuf = refs[pos:pos + 2]
        part, sibb, yb, xb, zb, fin, finb = [refs[pos + 2 + k * nw:pos + 2 + (k + 1) * nw] for k in range(7)]
        pos += 2 + 7 * nw
        pbuf, ssem, rsem, psem, prsem, lsem = refs[pos:]

        y, z, x, c = coords()

        def dev(yy, zz, xx, cc):
            return (yy, zz * 4 + xx * 2 + cc)

        sib, xn, yn = dev(y, z, x, 1 - c), dev(y, z, 1 - x, c), dev(1 - y, z, x, c)
        zp = [lax.rem(z + d, nz) for d in range(nz)]
        zd = [dev(y, zp[d], x, c) for d in range(nz)]

        barrier = pltpu.get_barrier_semaphore()
        peers = [sib, xn, yn] + zd[1:]
        for p in peers:
            pl.semaphore_signal(barrier, inc=1, device_id=p, device_id_type=MESHID)

        loads = {}

        def load(w):
            at = 0
            got = []
            first = sum(len(ls) for ls, _ in pairs[:w])
            for k in range(len(pairs[w][0])):
                ref = left_refs[first + k]
                cols = ref.shape[1]
                cp = pltpu.make_async_copy(ref, lbuf.at[w % 2, :, pl.ds(at, cols)], lsem.at[w, k])
                cp.start()
                got.append(cp)
                at += cols
            cp = pltpu.make_async_copy(right_refs[w], rbuf.at[w % 2], lsem.at[w, 3])
            cp.start()
            got.append(cp)
            loads[w] = got

        started = []

        def send(i, k, src, dst, to):
            cp = pltpu.make_async_remote_copy(
                src_ref=src, dst_ref=dst, send_sem=ssem.at[i, k], recv_sem=rsem.at[i, k],
                device_id=to, device_id_type=MESHID)
            cp.start()
            started.append(cp)
            return cp

        flight = {}

        def spans(w):
            rw, a = shard_rows[w], cuts[w]
            return dict(plane=(y * a, rw - a), mine=(y * (rw - a), a), theirs=((1 - y) * (rw - a), a))

        def rows_of(w, kind):
            r0, k = spans(w)[kind]
            return pl.ds(pl.multiple_of(r0, 16), k)

        def compute(i):
            w, j = items[i]
            rw, lb = shard_rows[w], blocks[w]
            if j == 0:
                for cp in loads[w]:
                    cp.wait()
            cols = pl.ds(j * lb, lb)
            right = rbuf[w % 2, :, cols]

            @pl.loop(0, nz // 2)
            def _(half):
                left = lbuf[w % 2, :, pl.ds(pl.multiple_of(half * 8 * rw, 128), 8 * rw)]
                g = tn(left, right).astype(BF16)
                for k in range(8):
                    part[w][j, k % 2, (k // 2) % 2, 2 * half + k // 4] = g[k * rw:(k + 1) * rw]

            if w != qkv and j == width // lb - 1 and w + 2 < nw:
                load(w + 2)
            flight[i, 0] = send(i, 0, part[w].at[j, 1 - c], sibb[w].at[j], sib)

        def stage_sib(i):
            w, j = items[i]
            flight[i, 0].wait_recv()
            mine = part[w].at[j, c]

            @pl.loop(0, nz)
            def _(zz):
                for xx in range(2):
                    mine[xx, zz] = (mine[xx, zz].astype(F32) + sibb[w][j, xx, zz].astype(F32)).astype(BF16)

            flight[i, 1] = send(i, 1, mine.at[:, :, rows_of(w, "theirs")], yb[w].at[j], yn)

        def stage_y(i):
            w, j = items[i]
            flight[i, 1].wait_recv()
            mine = part[w].at[j, c]
            r = rows_of(w, "mine")

            @pl.loop(0, nz)
            def _(zz):
                for xx in range(2):
                    mine[xx, zz, r] = (mine[xx, zz, r].astype(F32) + yb[w][j, xx, zz].astype(F32)).astype(BF16)

            flight[i, 2] = send(i, 2, mine.at[1 - x, :, rows_of(w, "plane")], xb[w].at[j], xn)

        def stage_x(i):
            w, j = items[i]
            flight[i, 2].wait_recv()
            mine = part[w].at[j, c, x]
            r = rows_of(w, "plane")

            @pl.loop(0, nz)
            def _(zz):
                mine[zz, r] = (mine[zz, r].astype(F32) + xb[w][j, zz].astype(F32)).astype(BF16)

            for d in range(1, nz):
                flight[i, 2 + d] = send(i, 2 + d, mine.at[zp[d], r], zb[w].at[j, d - 1], zd[d])

        def stage_z(i):
            w, j = items[i]
            total = part[w][j, c, x, z, rows_of(w, "plane")].astype(F32)
            for d in range(1, nz):
                flight[i, 2 + d].wait_recv()
                total = total + zb[w][j, d - 1].astype(F32)
            fin[w][j] = total.astype(BF16)
            flight[i, 2 + nz] = send(i, 2 + nz, fin[w].at[j], finb[w].at[j], yn)

        def stage_out(i):
            w, j = items[i]
            rw, a, lb = shard_rows[w], cuts[w], blocks[w]
            cols = pl.ds(j * lb, lb)
            flight[i, 2 + nz].wait_recv()
            here, there = fin[w].at[j], finb[w].at[j]

            def at(r0, k):
                return pl.ds(pl.multiple_of(r0, 16), k)

            out_refs[w][at(y * (rw - a), a), cols] = here[at(y * (rw - 2 * a), a)].astype(F32)
            out_refs[w][at((1 - y) * (rw - a), a), cols] = there[at((1 - y) * (rw - 2 * a), a)].astype(F32)
            if rw > 2 * a:
                out_refs[w][pl.ds(a, rw - 2 * a), cols] = (
                    here[at((1 - y) * a, rw - 2 * a)].astype(F32) + there[at(y * a, rw - 2 * a)].astype(F32))

        pack_to = [sib, yn, xn, dev(y, z + 1 - 2 * lax.rem(z, 2), x, c), dev(y, lax.rem(z + 2, 4), x, c)]
        pack_cp = {}

        def pack_step(k):
            if k > 0:
                pack_cp[k - 1].wait()
                pbuf[0, k] = pbuf[0, k - 1] + pbuf[1, k - 1]
            else:
                pbuf[0, 0] = jnp.zeros_like(pbuf[0, 0])
                for row, col, value in sum_rows(s1_ref[...], *[ref[...] for ref in sum_refs]):
                    pbuf[0, 0, row:row + 1, 0:col] = value
            if k < len(pack_to):
                cp = pltpu.make_async_remote_copy(
                    src_ref=pbuf.at[0, k], dst_ref=pbuf.at[1, k], send_sem=psem.at[k], recv_sem=prsem.at[k],
                    device_id=pack_to[k], device_id_type=MESHID)
                cp.start()
                pack_cp[k] = cp
            else:
                pack_out[...] = pbuf[0, k]

        tiles = n // tile
        held = [pltpu.make_async_copy(w_hbm, w_ref, fsem.at[0]), pltpu.make_async_copy(x_hbm, x_ref, fsem.at[1])]
        written = []

        def resid(k):
            return pltpu.make_async_copy(r_hbm.at[pl.ds(k * tile, tile)], r_ref.at[k % 2], fsem.at[2 + tiles + k])

        def finish_tile(k):
            if k == 0:
                s1_ref[...] = jnp.zeros_like(s1_ref)
                for cp in held:
                    cp.wait()
            r = pl.ds(k * tile, tile)
            resid(k).wait()
            dn = nn(lbuf[qkv % 2, r, 0:width], w_ref[0:width, :])
            for part in range(1, 3):
                span = slice(part * width, (part + 1) * width)
                dn = dn + nn(lbuf[qkv % 2, r, span], w_ref[span, :])
            hat, rstd = row_stats(x_ref[r, :].astype(F32))
            x_ref[r, :] = (r_ref[k % 2] + norm_back(dn * vec_ref[4:5, :], hat, rstd)).astype(BF16)
            if k + 2 < tiles:
                resid(k + 2).start()
            s1_ref[0:1, :] += col_sum(dn * hat)
            s1_ref[1:2, :] += col_sum(dn)
            cp = pltpu.make_async_copy(x_ref.at[r], g_hbm.at[r], fsem.at[2 + k])
            cp.start()
            written.append(cp)
            if k == tiles - 1:
                load(qkv + 2)

        load(0)
        load(1)
        for cp in held + [resid(0), resid(1)]:
            cp.start()
        pl.semaphore_wait(barrier, len(peers))
        does = {"compute": compute, "sib": stage_sib, "y": stage_y, "x": stage_x, "z": stage_z, "out": stage_out,
                "finish": finish_tile, "pack": pack_step}
        for kind, i in steps:
            does[kind](i)
        for cp in started:
            cp.wait_send()
        for cp in written:
            cp.wait()

    any_spec = pl.BlockSpec(memory_space=pl.ANY)
    vm = pl.BlockSpec(memory_space=pltpu.VMEM)

    def per_weight(make):
        return [pltpu.VMEM(make(width // b, shard_rows[w], cuts[w], b), BF16) for w, b in enumerate(blocks)]

    tiles = n // tile
    scratch = [pltpu.VMEM((n, width), BF16), pltpu.VMEM((2, tile, width), F32), pltpu.VMEM(qkv_t.shape, BF16),
               pltpu.VMEM((8, width), F32), pltpu.SemaphoreType.DMA((2 + 2 * tiles,)),
               pltpu.VMEM((2, n, max_left), BF16), pltpu.VMEM((2, n, width), BF16)]
    scratch += per_weight(lambda j, rw, a, b: (j, 2, 2, nz, rw, b))
    scratch += per_weight(lambda j, rw, a, b: (j, 2, nz, rw, b))
    scratch += per_weight(lambda j, rw, a, b: (j, 2, nz, a, b))
    scratch += per_weight(lambda j, rw, a, b: (j, nz, rw - a, b))
    scratch += per_weight(lambda j, rw, a, b: (j, nz - 1, rw - a, b))
    scratch += per_weight(lambda j, rw, a, b: (j, rw - a, b))
    scratch += per_weight(lambda j, rw, a, b: (j, rw - a, b))
    scratch += [
        pltpu.VMEM((2, 6, 16, 1024), F32),
        pltpu.SemaphoreType.DMA((ni, 3 + nz)), pltpu.SemaphoreType.DMA((ni, 3 + nz)),
        pltpu.SemaphoreType.DMA((6,)), pltpu.SemaphoreType.DMA((6,)), pltpu.SemaphoreType.DMA((nw, 4)),
    ]
    outs = pl.pallas_call(
        kernel,
        out_shape=[jax.ShapeDtypeStruct((rw, width), F32) for rw in shard_rows]
        + [jax.ShapeDtypeStruct((16, 1024), F32), jax.ShapeDtypeStruct((n, width), BF16)],
        in_specs=[any_spec] * (len(lefts) + nw + 3) + [vm] * 6,
        out_specs=[vm] * (nw + 1) + [any_spec],
        scratch_shapes=scratch,
        compiler_params=pltpu.CompilerParams(
            collective_id=collective, has_side_effects=True, vmem_limit_bytes=63 << 20),
        name="finish_reduce",
    )(*lefts, *rights, tokens, resid_grad, qkv_t, vecs, *sums)
    return outs[:nw], outs[nw], outs[nw + 1]


def sum_rows(s1, bq, bv, s768, sff, sal):
    lines = [bq[0:1], bv[0:1], s768[1:2], s768[0:1], s1[0:1], s1[1:2], s768[2:3], s768[3:4], sal[0:1]]
    lines += [sff[0:1, k:k + 1024] for k in range(0, sff.shape[1], 1024)]
    return [(row, v.shape[1], v) for row, v in enumerate(lines)]


def reduce_all(pairs, tokens, resid_grad, vecs, qkv_t, sums, fast):
    if fast:
        left_rows = [sum(a.shape[1] for a in ls) for ls, _ in pairs]
        shard_rows = [r // 16 for r in left_rows]
        cuts = [max(16, (r * 5 // 16) // 16 * 16) for r in shard_rows]
        blocks = [384, 256, 256, 256, 384]
        return finish_and_reduce(pairs, tokens, resid_grad, vecs, qkv_t, sums, shard_rows, cuts, blocks, 4, 1)
    grad_tokens, s1 = finish(tokens, resid_grad, *pairs[2][0], vecs, qkv_t)
    terms = [jnp.concatenate([tn(a, r).astype(BF16) for a in ls], 0) for ls, r in pairs]
    got = [lax.psum(lax.psum_scatter(t, "fsdp", scatter_dimension=0, tiled=True), "dp").astype(F32) for t in terms]
    lines = [jnp.pad(v, ((0, 0), (0, 1024 - k))) for _, k, v in sum_rows(s1, *sums)]
    pack = jnp.pad(jnp.concatenate(lines, 0), ((0, 16 - len(lines)), (0, 0)))
    return got, lax.psum(pack, ("dp", "fsdp")), grad_tokens


def per_device(mesh_shape, *args):
    (tokens, segment_ids, padding, qkv_weight, query_bias, value_bias, out_weight, out_bias,
     first_gain, first_shift, second_gain, second_shift, up_weight, up_bias, down_weight, down_bias,
     align_weight, align_bias, grad_output, grad_aligned) = args
    n, d = tokens.shape
    small = [query_bias, value_bias, out_bias, down_bias, first_gain, first_shift, second_gain, second_shift]
    members = mesh_shape["fsdp"]
    own, ub, ab = query_bias.shape[0], up_bias.shape[0], align_bias.shape[0]
    ff, al = ub * members, ab * members
    fast = mesh_shape["dp"] == 2 and members == 16

    seg = segment_ids[0]
    pad_row = padding[0]
    keys = jnp.where(pad_row == 0, seg, -1)
    valid_col = (1.0 - pad_row.astype(F32))[:, None]
    wins = windows(seg, 256)

    if fast:
        nz = members // 4
        lines = [v[None] for v in small] + [up_bias[None, :128], up_bias[None, 128:], align_bias[None]]
        pack = sum(jnp.pad(v, ((k, 47 - k), (0, 128 - v.shape[1]))) for k, v in enumerate(lines))
        normed, qkv, vecs, mixed, lse, packs, full = gather_attend(
            tokens, pack, [qkv_weight.T, out_weight, align_weight.T, up_weight.T, down_weight],
            seg[:, None], keys[None, :], own, nz)
        qkv_t, out_w, align_t, up_t, down_w = full
        up_b = packs[:, 8:10].reshape(members, 256)[:, :ub].reshape(1, ff).astype(F32)
        align_b = packs[:, 10, :ab].reshape(1, al).astype(F32)
    else:
        def gathered(a):
            return lax.all_gather(a, "fsdp", axis=0, tiled=True)

        qkv_t, out_w, up_t, down_w, align_t = [
            gathered(a) for a in (qkv_weight.T, out_weight, up_weight.T, down_weight, align_weight.T)]
        vecs = jnp.stack([gathered(v) for v in small]).astype(F32)
        up_b = gathered(up_bias).astype(F32)[None]
        align_b = gathered(align_bias).astype(F32)[None]
        qkv_b = jnp.concatenate([vecs[0:1], jnp.zeros((1, d), F32), vecs[1:2]], 1)
        normed, qkv = project(tokens, vecs, qkv_b, qkv_t)
        mixed, lse = attend(qkv, seg[:, None], keys[None, :], wins)
    (n2, act, du, gb, block_out, aligned, res, rb, dm, s768, sff, sal) = middle(
        tokens, mixed, grad_output, grad_aligned, valid_col, vecs, up_b, align_b, out_w, up_t, down_w, align_t)
    dq, dk, dv, bq, bv = attend_back(qkv, mixed, dm, lse, seg[None, :], keys[:, None], wins)
    pairs = [([grad_aligned], block_out), ([act], gb), ([dq, dk, dv], normed), ([du], n2), ([mixed], rb)]
    (g_align, g_down, g_qkv, g_up, g_out), pack, grad_tokens = reduce_all(
        pairs, tokens, res, vecs, qkv_t, (bq, bv, s768, sff, sal), fast)
    me = lax.axis_index("fsdp")
    vec = lax.dynamic_slice(pack, (0, me * own), (8, own))
    g_ub = lax.dynamic_slice(pack[9:9 + ff // 1024].reshape(ff), (me * ub,), (ub,))
    g_ab = lax.dynamic_slice(pack[8], (me * ab,), (ab,))
    return (block_out, aligned, grad_tokens, g_qkv.T, vec[0], vec[1], g_out, vec[2], vec[4], vec[5], vec[6],
            vec[7], g_up.T, g_ub, g_down, vec[3], g_align.T, g_ab)


def solution(mesh):
    rows_spec = P(("dp", "fsdp"), None)
    vec, by_col, by_row = P("fsdp"), P(None, "fsdp"), P("fsdp", None)
    in_specs = (rows_spec, rows_spec, rows_spec, by_col, vec, vec, by_row, vec, vec, vec, vec, vec,
                by_col, vec, by_row, vec, by_col, vec, rows_spec, rows_spec)
    out_specs = (rows_spec, rows_spec, rows_spec, by_col, vec, vec, by_row, vec, vec, vec, vec, vec,
                 by_col, vec, by_row, vec, by_col, vec)
    return jax.shard_map(functools.partial(per_device, dict(mesh.shape)), mesh=mesh, in_specs=in_specs,
                         out_specs=out_specs, check_vma=False)
```
